32 devices in a mesh: expert: 8 (over z, y), tensor: 4 (over x, core).
Axes of the slice: x: 2, y: 2, z: 4, core: 2. Of those that a mesh axis runs over, the one named last changes fastest.
Arguments:
- tokens: bfloat16 [1024, 7168], P('expert', 'tensor'), may hold values from -6 to 6
- out_grad: bfloat16 [1024, 7168], P('expert', 'tensor'), may hold values from -1.5 to 1.5
- expert_ids: int32 [1024, 2], P('expert'), may hold values from 0 to 7, all different within a row; in each aligned block of 128 rows (0 to 127, 128 to 255, ...) at most 48 rows name the same one
- gate_values: bfloat16 [1024, 2], P('expert'), may hold values from 0.099609375 to 1
- w_gate: bfloat16 [8, 7168, 1024], P('expert', None, 'tensor'), may hold values from -0.0625 to 0.0625
- w_up: bfloat16 [8, 7168, 1024], P('expert', None, 'tensor'), may hold values from -0.0625 to 0.0625
- w_down: bfloat16 [8, 1024, 7168], P('expert', 'tensor'), may hold values from -0.1875 to 0.1875
Outputs:
- d_tokens: bfloat16 [1024, 7168], P('expert', 'tensor')
- d_gates: float32 [1024, 2], P('expert')
The draws below stay inside these ranges and needn't reach their ends.
Inputs may be any that keep to these rules, and one draw needn't show every extreme that they name: `expert_ids`: each row names 2 different experts. Among the 128 rows held at one index along `expert` (one aligned block) no expert is named by more than 48 rows, and in some such block one expert is named by exactly 48.
All inputs are finite; a program needn't handle non-finite values.
Results may differ from the reference program's by a relative error of at most 0.0049.
Values may be sent and summed in bfloat16 or wider, within the bound.
A program may use at most 128 MiB of HBM per device.

```python
import math
import jax
import jax.numpy as jnp
import numpy as np
from jax import lax

D = 7168
FF = 1024
TOP = 2
TOK_GRP = 128
EXPERTS = 8
MOST = 48
TOKENS = 1024
N_EXPERT = 8


def steps_of(rng, shape, pieces, least, top_value):
    factor_of = 1.0
    for axis_at, shards_of in pieces:
        steps = jax.random.uniform(jax.random.fold_in(jax.random.fold_in(rng, 6), axis_at), (shards_of,), jnp.float32, least / len(pieces), top_value / len(pieces))
        factor_of = factor_of * jnp.repeat(jnp.exp(steps), shape[axis_at] // shards_of).reshape((-1,) + (1,) * (len(shape) - 1 - axis_at))
    return factor_of


def routed_block(own_key, own, number, rows, count, top, limit, lean):
    order = jax.random.permutation(own_key, count)
    packed, common = shares(count, rows * top, limit, lean, True), shares(count, rows * top, limit, lean, False)
    places = jnp.arange(count)

    def named(tallies, rotation):
        used = int((tallies > 0).sum())
        fixed = max(1, used // 4)
        shifted = fixed + (places - fixed + rotation * (used - fixed)) % max(1, count - fixed)
        return jnp.zeros((count,), jnp.int32).at[order[jnp.where(places < fixed, places, shifted)]].set(jnp.asarray(tallies, jnp.int32))

    tallies = jnp.where(number % 4 == 0, named(packed, number // 4), named(common, number - number // 4 - 1))
    mixed = jax.random.permutation(jax.random.fold_in(own, 3), count)
    donor, receiver = mixed[0:count // 2 * 2:2], mixed[1:count // 2 * 2:2]
    slack = jnp.minimum(tallies[donor] - 1, limit - tallies[receiver]) // 2
    slack = jnp.where((donor == order[0]) | (receiver == order[0]) | (tallies[receiver] == 0), 0, jnp.maximum(slack, 0))
    shifted = jax.random.randint(jax.random.fold_in(own, 4), (count // 2,), 0, 1 << 20) % (slack + 1)
    tallies = tallies.at[donor].add(-shifted).at[receiver].add(shifted)
    members = jnp.searchsorted(jnp.cumsum(tallies), jnp.arange(rows * top), side="right").astype(jnp.int32)
    listing = members.reshape(top, rows).T
    listing = listing[jax.random.permutation(jax.random.fold_in(own, 1), rows)]
    rotation = jax.random.randint(jax.random.fold_in(own, 2), (rows, 1), 0, top)
    return jnp.take_along_axis(listing, (jnp.arange(top)[None, :] + rotation) % top, axis=1)


def shares(count, total, limit, lean, full):
    weights = [(1 << 20) // math.isqrt(grade ** lean) + 1 for grade in range(1, count + 1)]
    largest = limit if full else min(limit, max(-(-total // count), total * weights[0] // sum(weights)))
    least = 1 if total - largest >= count - 1 else 0
    given, rest = [largest] + [least] * (count - 1), total - largest - least * (count - 1)
    while rest > 0:
        free = [i for i in range(1, count) if given[i] < largest] or [i for i in range(1, count) if given[i] < limit]
        whole, remaining = sum([weights[i] for i in free]), rest
        for i in free:
            more = min(limit - given[i], max(1, remaining * weights[i] // whole), rest)
            given[i] = given[i] + more
            rest = rest - more
    return np.array(given)


def scatter_about(key, extent, spread, reach, cuts=(), kind=jnp.bfloat16):
    result = spread * jax.random.normal(key, extent, jnp.float32)
    if cuts:
        result = result * steps_of(key, extent, cuts, -0.22, 0.18)
    return jnp.clip(result, -reach, reach).astype(kind)


def setup_inputs(seed: int = 0) -> dict:
    keys = jax.random.split(jax.random.key(seed), 8)
    tokens = scatter_about(keys[0], (TOKENS, D), 1.0, 6.0, ((0, 8), (1, 4)))
    out_grad = scatter_about(keys[1], (TOKENS, D), 0.25, 1.5, ((0, 8), (1, 4)))
    expert_ids_keys = jax.random.split(jax.random.fold_in(keys[2], 1), TOKENS // TOK_GRP)
    expert_ids_turns = jax.random.permutation(jax.random.fold_in(keys[2], 3), TOKENS // TOK_GRP)
    expert_ids = jax.vmap(lambda own, number: routed_block(jax.random.fold_in(keys[2], 2), own, number, TOK_GRP, EXPERTS, TOP, MOST, 2))(expert_ids_keys, expert_ids_turns).reshape((TOKENS, TOP))
    gate_values = jnp.clip(0.099609375 + 0.9003906 * jax.random.uniform(keys[3], (TOKENS, TOP), jnp.float32) ** steps_of(keys[3], (TOKENS, TOP), ((0, 8),), -0.2, 0.2), 0.099609375, 1.0).astype(jnp.bfloat16)
    w_gate = scatter_about(keys[4], (EXPERTS, D, FF), D ** -0.5, 0.0625, ((0, 8), (2, 4)))
    w_up = scatter_about(keys[5], (EXPERTS, D, FF), D ** -0.5, 0.0625, ((0, 8), (2, 4)))
    w_down = scatter_about(keys[6], (EXPERTS, FF, D), FF ** -0.5, 0.1875, ((0, 8), (1, 4)))
    return dict(tokens=tokens, out_grad=out_grad, expert_ids=expert_ids, gate_values=gate_values, w_gate=w_gate, w_up=w_up, w_down=w_down)


def reference(tokens, out_grad, expert_ids, gate_values, w_gate, w_up, w_down):
    assign = TOK_GRP * TOP
    grouped = expert_ids.reshape(N_EXPERT, assign)
    onehot = (grouped[:, :, None] == jnp.arange(EXPERTS, dtype=jnp.int32)[None, None, :]).astype(jnp.int32)
    before = jnp.cumsum(onehot, axis=1) - onehot
    rank = jnp.sum(before * onehot, axis=2).astype(jnp.int32)
    source = jnp.broadcast_to(jnp.arange(N_EXPERT, dtype=jnp.int32)[:, None], (N_EXPERT, assign))
    position = (source * assign + jnp.arange(assign, dtype=jnp.int32)[None, :]).astype(jnp.int32)
    table = jnp.full((EXPERTS, N_EXPERT, MOST), -1, jnp.int32).at[grouped, source, rank].set(position)
    table = table.reshape(EXPERTS, N_EXPERT * MOST)
    gate_flat = gate_values.reshape(-1).astype(jnp.float32)

    def one_expert(totals, inputs):
        grad_acc, slot_acc = totals
        slots, gate_mat, up_mat, down_mat = inputs
        is_live = slots >= 0
        safe_pos = jnp.where(is_live, slots, 0).astype(jnp.int32)
        tok_index = (safe_pos // TOP).astype(jnp.int32)
        zero_bf = jnp.zeros((), jnp.bfloat16)
        rows_x = jnp.where(is_live[:, None], tokens[tok_index], zero_bf)
        rows_dy = jnp.where(is_live[:, None], out_grad[tok_index], zero_bf)
        weight_g = jnp.where(is_live, gate_flat[safe_pos], jnp.float32(0.0))
        pre_act = jnp.dot(rows_x, gate_mat, preferred_element_type=jnp.float32)
        up_proj = jnp.dot(rows_x, up_mat, preferred_element_type=jnp.float32)
        grad_hid = jnp.dot(rows_dy, down_mat.T, preferred_element_type=jnp.float32)
        sigma = jax.nn.sigmoid(pre_act)
        active = pre_act * sigma
        slot_grad = jnp.sum(active * up_proj * grad_hid, axis=1)
        scaled = weight_g[:, None] * grad_hid
        grad_up = (scaled * active).astype(jnp.bfloat16)
        grad_pre = (scaled * up_proj * sigma * (1.0 + pre_act * (1.0 - sigma))).astype(jnp.bfloat16)
        contrib = jnp.dot(grad_pre, gate_mat.T, preferred_element_type=jnp.float32)
        contrib = contrib + jnp.dot(grad_up, up_mat.T, preferred_element_type=jnp.float32)
        grad_acc = grad_acc.at[tok_index].add(jnp.where(is_live[:, None], contrib, jnp.float32(0.0)))
        slot_acc = slot_acc.at[safe_pos].add(jnp.where(is_live, slot_grad, jnp.float32(0.0)))
        return (grad_acc, slot_acc), None

    start_acc = (jnp.zeros((TOKENS, D), jnp.float32), jnp.zeros((TOKENS * TOP,), jnp.float32))
    (grad_acc, slot_acc), _ = lax.scan(one_expert, start_acc, (table, w_gate, w_up, w_down))
    return grad_acc.astype(jnp.bfloat16), slot_acc.reshape(TOKENS, TOP)
```

```python
import functools

import jax
import jax.numpy as jnp
from jax import lax
from jax.experimental import pallas as pl
from jax.experimental.pallas import tpu as pltpu
from jax.sharding import PartitionSpec as P


MESH = pl.DeviceIdType.MESH
VMEM = pl.BlockSpec(memory_space=pltpu.VMEM)
VMEM_BYTES = 56 * 1024 * 1024


def positions(n):
    me = lax.axis_index("expert")
    share = lax.axis_index("tensor")
    pair, side = share // 2, share % 2
    return me, share, pair * 2 + 1 - side, (1 - pair) * 2 + side


def greet(n, me, share, near, far):
    barrier = pltpu.get_barrier_semaphore()

    @pl.loop(1, n)
    def _(step):
        pl.semaphore_signal(
            barrier, inc=1, device_id=(lax.rem(me + step, n), share), device_id_type=MESH
        )

    for peer in (near, far):
        pl.semaphore_signal(barrier, inc=1, device_id=(me, peer), device_id_type=MESH)
    pl.semaphore_wait(barrier, n + 1)


def remote(src, dst, sems, index, device):
    return pltpu.make_async_remote_copy(
        src_ref=src,
        dst_ref=dst,
        send_sem=sems[0].at[index],
        recv_sem=sems[1].at[index],
        device_id=device,
        device_id_type=MESH,
    )


def spread_kernel(n, x_ref, dy_ref, g_ref, x_out, dy_out, g_out, *sems):
    me, share, near, far = positions(n)
    quarter = x_ref.shape[2]
    by_group, to_near, to_far, passed, gates = (sems[2 * i : 2 * i + 2] for i in range(5))
    own = sems[10]
    pairs = ((x_ref, x_out), (dy_ref, dy_out))

    def cols(which):
        return pl.ds(pl.multiple_of(which * quarter, 128), quarter)

    def block(which, group, owner):
        return pairs[which][1].at[group, :, cols(owner)]

    def dispatch(which, source, target):
        return remote(
            pairs[which][0].at[target],
            block(which, source, share),
            by_group,
            which * n + source,
            (target, share),
        )

    def gate_copy(source, target):
        return remote(
            g_ref.at[target], g_out.at[source], gates, source, (target, share)
        )

    def along(which, group, sent, sems_of, peer):
        return remote(
            block(which, group, sent),
            block(which, group, sent),
            sems_of,
            which * n + group,
            (me, peer),
        )

    greet(n, me, share, near, far)
    own_copies = [
        pltpu.make_async_copy(src.at[me], block(which, me, share), own.at[which])
        for which, (src, _) in enumerate(pairs)
    ]
    own_copies.append(pltpu.make_async_copy(g_ref.at[me], g_out.at[me], own.at[2]))
    for copy in own_copies:
        copy.start()
    for which in range(2):

        @pl.loop(1, n)
        def _(step):
            target = lax.rem(me + step, n)
            dispatch(which, me, target).start()

    @pl.loop(1, n)
    def _(step):
        gate_copy(me, lax.rem(me + step, n)).start()

    for copy in own_copies:
        copy.wait()

    def share_out(which, group):
        along(which, group, share, to_far, far).start()
        along(which, group, share, to_near, near).start()

    def pass_on(which, group):
        along(which, group, far, to_far, far).wait_recv()
        along(which, group, far, passed, near).start()

    for which in range(2):
        share_out(which, me)

        @pl.loop(1, n)
        def _(step):
            group = lax.rem(me - step + n, n)
            dispatch(which, group, me).wait_recv()
            share_out(which, group)
            pass_on(which, lax.rem(me - step + 1 + n, n))

        pass_on(which, lax.rem(me + 1, n))
    for which in range(2):

        @pl.loop(0, n)
        def _(group):
            along(which, group, near, to_near, near).wait_recv()
            along(which, group, 3 - share, passed, near).wait_recv()
            along(which, group, share, to_far, far).wait_send()
            along(which, group, share, to_near, near).wait_send()
            along(which, group, far, passed, near).wait_send()

        @pl.loop(1, n)
        def _(step):
            dispatch(which, me, lax.rem(me + step, n)).wait_send()

    @pl.loop(1, n)
    def _(step):
        gate_copy(me, lax.rem(me + step, n)).wait_send()
        gate_copy(lax.rem(me - step + n, n), me).wait_recv()


def spread(send_x, send_dy, send_g):
    n, most, quarter = send_x.shape
    wide = jax.ShapeDtypeStruct((n, most, 4 * quarter), send_x.dtype)
    dma = pltpu.SemaphoreType.DMA
    return pl.pallas_call(
        functools.partial(spread_kernel, n),
        out_shape=(wide, wide, jax.ShapeDtypeStruct(send_g.shape, send_g.dtype)),
        in_specs=[VMEM] * 3,
        out_specs=[VMEM] * 3,
        scratch_shapes=[dma((2 * n,))] * 8 + [dma((n,)), dma((n,)), dma((3,))],
        compiler_params=pltpu.CompilerParams(
            collective_id=0, has_side_effects=True, vmem_limit_bytes=VMEM_BYTES
        ),
    )(send_x, send_dy, send_g)


def collect_kernel(n, c_ref, p_ref, out, grad_out, near_got, far_put, far_got, put, total,
                   part_got, part_sum, *sems):
    me, share, near, far = positions(n)
    quarter = out.shape[2]
    to_near, to_far, back, grads, parts = (sems[2 * i : 2 * i + 2] for i in range(5))
    own = sems[10]

    def cols(which):
        return pl.ds(pl.multiple_of(which * quarter, 128), quarter)

    def half(group, slot):
        wanted = near if slot == 1 else 3 - share
        return remote(
            c_ref.at[group, :, cols(wanted)],
            near_got.at[group, slot],
            to_near,
            group * 2 + slot,
            (me, near),
        )

    def across(group):
        return remote(far_put.at[group], far_got.at[group], to_far, group, (me, far))

    def home(source, target):
        return remote(put.at[target], out.at[source], back, source, (target, share))

    def grad_home(source, target):
        return remote(
            part_sum.at[target], grad_out.at[source], grads, source, (target, share)
        )

    greet(n, me, share, near, far)
    part_near = remote(p_ref, part_got.at[0], parts, 0, (me, near))
    part_near.start()

    @pl.loop(0, n)
    def _(step):
        group = lax.rem(me + 1 + step, n)
        half(group, 0).start()
        half(group, 1).start()

    part_near.wait()
    part_sum[...] = p_ref[...] + part_got[0]
    part_far = remote(part_sum, part_got.at[1], parts, 1, (me, far))
    part_far.start()
    part_far.wait()
    part_sum[...] = part_sum[...] + part_got[1]

    @pl.loop(1, n)
    def _(step):
        grad_home(me, lax.rem(me + step, n)).start()

    def pair_sum(group):
        half(group, 0).wait_recv()
        mine = c_ref[group, :, cols(far)].astype(jnp.float32)
        far_put[group] = (mine + near_got[group, 0].astype(jnp.float32)).astype(far_put.dtype)
        across(group).start()
        half(group, 1).wait_recv()
        mine = c_ref[group, :, cols(share)].astype(jnp.float32)
        total[group] = mine + near_got[group, 1].astype(jnp.float32)

    def full_sum(group):
        across(group).wait_recv()
        put[group] = (total[group] + far_got[group].astype(jnp.float32)).astype(put.dtype)

    def send_home(group):
        full_sum(group)
        home(me, group).start()

    pair_sum(lax.rem(me + 1, n))

    @pl.loop(2, n + 1)
    def _(step):
        pair_sum(lax.rem(me + step, n))
        send_home(lax.rem(me + step - 1, n))

    full_sum(me)
    own_copies = [
        pltpu.make_async_copy(put.at[me], out.at[me], own.at[0]),
        pltpu.make_async_copy(part_sum.at[me], grad_out.at[me], own.at[1]),
    ]
    for copy in own_copies:
        copy.start()
    for copy in own_copies:
        copy.wait()

    @pl.loop(0, n)
    def _(group):
        half(group, 0).wait_send()
        half(group, 1).wait_send()
        across(group).wait_send()

    @pl.loop(1, n)
    def _(step):
        target = lax.rem(me + step, n)
        source = lax.rem(me - step + n, n)
        home(me, target).wait_send()
        grad_home(me, target).wait_send()
        home(source, me).wait_recv()
        grad_home(source, me).wait_recv()


def collect(contrib, partial_grad):
    n, most, width = contrib.shape
    quarter = width // 4
    kind = contrib.dtype
    dma = pltpu.SemaphoreType.DMA
    stage = pltpu.VMEM((n, most, quarter), kind)
    return pl.pallas_call(
        functools.partial(collect_kernel, n),
        out_shape=(
            jax.ShapeDtypeStruct((n, most, quarter), kind),
            jax.ShapeDtypeStruct(partial_grad.shape, partial_grad.dtype),
        ),
        in_specs=[VMEM] * 2,
        out_specs=[VMEM] * 2,
        scratch_shapes=[
            pltpu.VMEM((n, 2, most, quarter), kind),
            stage,
            stage,
            stage,
            pltpu.VMEM((n, most, quarter), jnp.float32),
            pltpu.VMEM((2,) + partial_grad.shape, jnp.float32),
            pltpu.VMEM(partial_grad.shape, jnp.float32),
            dma((2 * n,)),
            dma((2 * n,)),
        ]
        + [dma((n,))] * 6
        + [dma((2,)), dma((2,)), dma((2,))],
        compiler_params=pltpu.CompilerParams(
            collective_id=1, has_side_effects=True, vmem_limit_bytes=VMEM_BYTES
        ),
    )(contrib, partial_grad)


BATCHES = ((0, 4), (4, 6), (6, 7), (7, 8))


def fused_kernel(n, most, tok_ref, grad_ref, ids_ref, gv_ref, gate_hbm, up_hbm, down_hbm,
                 out, gate_out, send, gath, g_put, g_got, gu_w, down_w, chooser, code, pre_up,
                 dz, dpdu, near_put, mine, near_got, far_put, far_got, put, back, total,
                 part, part_got, part_sum, part_back, load, *sems):
    me, share, near, far = positions(n)
    diag = 3 - share
    quarter = tok_ref.shape[1]
    tok_rows = tok_ref.shape[0]
    hidden = down_w.shape[0]
    chunk = quarter // 7
    (by_group, gates, to_far, to_near, passed, halves, over, back_sems, grads, parts) = (
        sems[2 * i : 2 * i + 2] for i in range(10)
    )

    def partner(step):
        at = me
        for bit in (1, 2, 4):
            if step & bit:
                at = at + bit * (1 - 2 * lax.rem(me // bit, 2))
        return at

    def nt(left, right):
        return lax.dot_general(
            left, right, (((1,), (1,)), ((), ())), preferred_element_type=jnp.float32
        )

    def dispatch(step):
        return remote(
            send.at[step], gath.at[step, share], by_group, step, (partner(step), share)
        )

    def gate_copy(step):
        return remote(g_put.at[step], g_got.at[step], gates, step, (partner(step), share))

    def along_far(step):
        block = gath.at[step, share]
        return remote(block, block, to_far, step, (me, far))

    def along_near(step):
        block = gath.at[step, share]
        return remote(block, block, to_near, step, (me, near))

    def pass_near(step):
        block = gath.at[step, far]
        return remote(block, block, passed, step, (me, near))

    def half(batch, slot):
        first, last = BATCHES[batch]
        span = pl.ds(first, last - first)
        return remote(
            near_put.at[slot, span], near_got.at[slot, span], halves, batch * 2 + slot, (me, near)
        )

    def across(step):
        return remote(far_put.at[step], far_got.at[step], over, step, (me, far))

    def home(step):
        return remote(put.at[step], back.at[step], back_sems, step, (partner(step), share))

    def grad_home(step):
        return remote(
            part_sum.at[step], part_back.at[step], grads, step, (partner(step), share)
        )

    def part_copy(batch, which):
        first, last = BATCHES[batch]
        span = pl.ds(first, last - first)
        peer = (near, far, diag)[which]
        return remote(
            part.at[span], part_got.at[which, span], parts, batch * 3 + which, (me, peer)
        )

    loads = [
        pltpu.make_async_copy(gate_hbm, gu_w.at[:, pl.ds(0, hidden)], load.at[0]),
        pltpu.make_async_copy(up_hbm, gu_w.at[:, pl.ds(hidden, hidden)], load.at[1]),
        pltpu.make_async_copy(down_hbm, down_w, load.at[2]),
    ]
    barrier = pltpu.get_barrier_semaphore()
    for step in range(1, n):
        pl.semaphore_signal(
            barrier, inc=1, device_id=(partner(step), share), device_id_type=MESH
        )
    for peer in (near, far, diag):
        pl.semaphore_signal(barrier, inc=1, device_id=(me, peer), device_id_type=MESH)

    lane = lax.broadcasted_iota(jnp.int32, (tok_rows, 128), 1)
    row = lax.broadcasted_iota(jnp.int32, (tok_rows, 128), 0)
    ids = ids_ref[...]
    gv = gv_ref[...].astype(jnp.float32)
    first_named, second_named = lane == ids[:, 0:1], lane == ids[:, 1:2]
    named = jnp.where(first_named | second_named, 1.0, 0.0)
    earlier = jnp.where(lane < row, 1.0, 0.0).astype(jnp.bfloat16)
    rank = jnp.dot(earlier, named.astype(jnp.bfloat16), preferred_element_type=jnp.float32)
    codes = jnp.where(named > 0.5, rank, -1.0)
    code[...] = codes
    codes_t = codes.T
    weight_t = (
        jnp.where(first_named, gv[:, 0:1], 0.0) + jnp.where(second_named, gv[:, 1:2], 0.0)
    ).T
    slot_row = lax.broadcasted_iota(jnp.int32, (most, tok_rows), 0).astype(jnp.float32)

    def choose(step):
        at = row == partner(step)
        its_code = jnp.sum(jnp.where(at, codes_t, 0.0), axis=0, keepdims=True)
        its_weight = jnp.sum(jnp.where(at, weight_t, 0.0), axis=0, keepdims=True)
        hit = jnp.where(slot_row == its_code, 1.0, 0.0)
        chooser[step] = hit.astype(chooser.dtype)
        slot_weight = jnp.sum(hit * its_weight, axis=1, keepdims=True)
        g_put[step] = jnp.broadcast_to(slot_weight, (most, 128)).astype(g_put.dtype)

    def pick(step, which):
        rows_of = (tok_ref, grad_ref)[which]
        return jnp.dot(
            chooser[step], rows_of[...], preferred_element_type=jnp.float32
        ).astype(send.dtype)

    def give(step):
        choose(step)
        for which in range(2):
            send[step, which] = pick(step, which)
        dispatch(step).start()
        gate_copy(step).start()

    choose(0)
    for which in range(2):
        gath[0, share, which] = pick(0, which)
    g_got[0] = g_put[0]
    pl.semaphore_wait(barrier, n + 2)
    along_far(0).start()
    along_near(0).start()
    for step in (4, 1, 2, 5, 3, 6, 7):
        give(step)
    for copy in loads:
        copy.start()

    def project(batch):
        first, last = BATCHES[batch]
        rows = (last - first) * most

        @pl.loop(0, 4)
        def _(q):
            at = pl.ds(pl.multiple_of(q * quarter, 128), quarter)
            x = gath[first:last, q, 0].reshape(rows, quarter)
            dy = gath[first:last, q, 1].reshape(rows, quarter)
            got = jnp.dot(x, gu_w[at, :], preferred_element_type=jnp.float32)
            got_dz = nt(dy, down_w[:, at])

            @pl.when(q == 0)
            def _():
                pre_up[0:rows, :] = got
                dz[0:rows, :] = got_dz

            @pl.when(q > 0)
            def _():
                pre_up[0:rows, :] += got
                dz[0:rows, :] += got_dz

    diagonal = lax.broadcasted_iota(jnp.int32, (most, 128), 0) == lax.broadcasted_iota(
        jnp.int32, (most, 128), 1
    )

    def activate(batch):
        first, last = BATCHES[batch]
        for step in range(first, last):
            if step:
                gate_copy(step).wait_recv()
            at = slice((step - first) * most, (step - first + 1) * most)
            pre_b, up_b, dz_b = pre_up[at, 0:hidden], pre_up[at, hidden:], dz[at, :]
            sigma = jax.nn.sigmoid(pre_b)
            active = pre_b * sigma
            slot_sum = jnp.sum(active * up_b * dz_b, axis=1, keepdims=True)
            flat = jnp.sum(jnp.where(diagonal, slot_sum, 0.0), axis=0, keepdims=True)
            part[step] = jnp.broadcast_to(flat, (8, 128))
            scaled = g_got[step][:, :1].astype(jnp.float32) * dz_b
            dpdu[at, hidden:] = (scaled * active).astype(dpdu.dtype)
            dpdu[at, 0:hidden] = (
                scaled * up_b * sigma * (1.0 + pre_b * (1.0 - sigma))
            ).astype(dpdu.dtype)
        for which in range(3):
            part_copy(batch, which).start()

    def expand(batch, wanted, store):
        first, last = BATCHES[batch]
        rows = (last - first) * most

        @pl.loop(0, 7)
        def _(step):
            start = wanted * quarter + step * chunk
            at = pl.ds(pl.multiple_of(start, 128), chunk)
            value = nt(dpdu[0:rows, :], gu_w[at, :])
            store(
                pl.ds(pl.multiple_of(step * chunk, 128), chunk),
                value.reshape(last - first, most, chunk),
            )

    def give_back(batch):
        first, last = BATCHES[batch]
        for slot, wanted in ((0, diag), (1, near)):

            def keep(at, value):
                near_put[slot, first:last, :, at] = value.astype(near_put.dtype)

            expand(batch, wanted, keep)
            half(batch, slot).start()
        for slot, wanted in ((0, far), (1, share)):

            def keep_wide(at, value):
                mine[slot, first:last, :, at] = value

            expand(batch, wanted, keep_wide)

    def cross(batch, steps):
        for step in steps:
            far_put[step] = (mine[0, step] + near_got[0, step].astype(jnp.float32)).astype(
                far_put.dtype
            )
            across(step).start()

    def go_home(step):
        across(step).wait_recv()
        value = mine[1, step] + near_got[1, step].astype(jnp.float32)
        value = (value + far_got[step].astype(jnp.float32)).astype(put.dtype)
        if step:
            put[step] = value
            home(step).start()
        else:
            back[0] = value

    def share_parts(batch):
        first, last = BATCHES[batch]
        for which in range(3):
            part_copy(batch, which).wait_recv()
        for step in range(first, last):
            part_sum[step] = (
                part[step] + part_got[0, step] + part_got[1, step] + part_got[2, step]
            )
            if step:
                grad_home(step).start()
            else:
                part_back[0] = part_sum[0]

    def arrive(step):
        dispatch(step).wait_recv()
        along_far(step).start()
        along_near(step).start()

    def pass_on(step):
        along_far_from(step).wait_recv()
        pass_near(step).start()

    def along_far_from(step):
        block = gath.at[step, far]
        return remote(block, block, to_far, step, (me, far))

    def settle(step):
        block = gath.at[step, near]
        remote(block, block, to_near, step, (me, near)).wait_recv()
        block = gath.at[step, diag]
        remote(block, block, passed, step, (me, near)).wait_recv()

    arrive(1)
    pass_on(0)
    arrive(2)
    pass_on(1)
    arrive(4)
    pass_on(2)
    arrive(3)
    pass_on(4)
    arrive(5)
    pass_on(3)
    for copy in loads:
        copy.wait()
    for step in range(4):
        settle(step)
    project(0)
    activate(0)
    arrive(6)
    pass_on(5)
    give_back(0)
    half(0, 0).wait_recv()
    half(0, 1).wait_recv()
    settle(4)
    settle(5)
    project(1)
    activate(1)
    give_back(1)
    half(1, 0).wait_recv()
    half(1, 1).wait_recv()
    cross(1, (4, 5))
    pass_on(6)
    share_parts(0)
    settle(6)
    project(2)
    activate(2)
    arrive(7)
    give_back(2)
    half(2, 0).wait_recv()
    half(2, 1).wait_recv()
    cross(2, (6,))
    cross(0, (2,))
    share_parts(1)
    go_home(4)
    go_home(5)
    pass_on(7)
    settle(7)
    project(3)
    activate(3)
    give_back(3)
    half(3, 0).wait_recv()
    half(3, 1).wait_recv()
    cross(3, (7,))
    cross(0, (3, 1, 0))
    share_parts(2)
    go_home(6)
    share_parts(3)
    go_home(2)
    go_home(7)

    def take(steps, fresh):
        for step in steps:
            if step:
                home(step).wait_recv()
        first, last = min(steps), max(steps) + 1
        rows = (last - first) * most
        picks = chooser[first:last].reshape(rows, tok_rows)

        @pl.loop(0, 7)
        def _(step):
            at = pl.ds(pl.multiple_of(step * chunk, 128), chunk)
            got = lax.dot_general(
                picks,
                back[first:last, :, at].reshape(rows, chunk),
                (((0,), (0,)), ((), ())),
                preferred_element_type=jnp.float32,
            )
            if fresh:
                total[:, at] = got
            else:
                out[:, at] = (total[:, at] + got).astype(out.dtype)

    go_home(3)
    go_home(1)
    take((4, 5, 6, 7), True)
    grad_total = jnp.zeros((tok_rows, 2), jnp.float32)
    ids = ids_ref[...]
    lane = lax.broadcasted_iota(jnp.int32, (tok_rows, 128), 1)
    for step in range(n):
        if step:
            grad_home(step).wait_recv()
        its_code = jnp.sum(
            jnp.where(lane == partner(step), code[...], 0.0), axis=1, keepdims=True
        )
        held = part_back[step][0:1, :]
        value = jnp.sum(
            jnp.where(lane.astype(jnp.float32) == its_code, held, 0.0), axis=1, keepdims=True
        )
        grad_total = grad_total + jnp.where(ids == partner(step), value, 0.0)
    gate_out[...] = grad_total
    go_home(0)
    take((0, 1, 2, 3), False)

    for step in range(n):
        along_far(step).wait_send()
        along_near(step).wait_send()
        pass_near(step).wait_send()
        across(step).wait_send()
        if step:
            dispatch(step).wait_send()
            gate_copy(step).wait_send()
            home(step).wait_send()
            grad_home(step).wait_send()
    for batch in range(len(BATCHES)):
        for slot in range(2):
            half(batch, slot).wait_send()
        for which in range(3):
            part_copy(batch, which).wait_send()


def fused(tokens, out_grad, expert_ids, gate_values, gate_mat, up_mat, down_mat):
    n = lax.axis_size("expert")
    tok_rows, quarter = tokens.shape
    most = 3 * tok_rows * expert_ids.shape[1] // (2 * n)
    kind = tokens.dtype
    hidden = gate_mat.shape[1]
    rows = max(last - first for first, last in BATCHES) * most
    dma = pltpu.SemaphoreType.DMA
    anywhere = pl.BlockSpec(memory_space=pl.ANY)
    stage = pltpu.VMEM((n, most, quarter), kind)
    pair = pltpu.VMEM((2, n, most, quarter), kind)
    flat = pltpu.VMEM((n, 8, 128), jnp.float32)
    narrow = pltpu.VMEM((n, most, 128), kind)
    return pl.pallas_call(
        functools.partial(fused_kernel, n, most),
        out_shape=(
            jax.ShapeDtypeStruct(tokens.shape, kind),
            jax.ShapeDtypeStruct(expert_ids.shape, jnp.float32),
        ),
        in_specs=[VMEM] * 4 + [anywhere] * 3,
        out_specs=[VMEM] * 2,
        scratch_shapes=[
            pltpu.VMEM((n, 2, most, quarter), kind),
            pltpu.VMEM((n, 4, 2, most, quarter), kind),
            narrow,
            narrow,
            pltpu.VMEM((4 * quarter, 2 * hidden), kind),
            pltpu.VMEM(down_mat.shape, kind),
            pltpu.VMEM((n, most, tok_rows), kind),
            pltpu.VMEM((tok_rows, 128), jnp.float32),
            pltpu.VMEM((rows, 2 * hidden), jnp.float32),
            pltpu.VMEM((rows, hidden), jnp.float32),
            pltpu.VMEM((rows, 2 * hidden), kind),
            pair,
            pltpu.VMEM((2, n, most, quarter), jnp.float32),
            pair,
            stage,
            stage,
            stage,
            stage,
            pltpu.VMEM(tokens.shape, jnp.float32),
            flat,
            pltpu.VMEM((3, n, 8, 128), jnp.float32),
            flat,
            flat,
            dma((3,)),
        ]
        + [dma((n,))] * 10
        + [dma((2 * len(BATCHES),))] * 2
        + [dma((n,))] * 6
        + [dma((3 * len(BATCHES),))] * 2,
        compiler_params=pltpu.CompilerParams(
            collective_id=2, has_side_effects=True, vmem_limit_bytes=VMEM_BYTES
        ),
    )(tokens, out_grad, expert_ids, gate_values, gate_mat, up_mat, down_mat)


def in_steps(send_x, send_dy, send_g, gate_mat, up_mat, down_mat):
    n_experts, most_slots, quarter = send_x.shape
    slot_count = n_experts * most_slots
    piece_x, piece_dy, recv_g = spread(
        send_x,
        send_dy,
        send_g.reshape(n_experts, 1, most_slots),
    )
    piece_x = piece_x.reshape(slot_count, 4 * quarter)
    piece_dy = piece_dy.reshape(slot_count, 4 * quarter)
    pre_sum = jnp.dot(piece_x, gate_mat, preferred_element_type=jnp.float32)
    up_sum = jnp.dot(piece_x, up_mat, preferred_element_type=jnp.float32)
    grad_sum = lax.dot_general(
        piece_dy, down_mat, (((1,), (1,)), ((), ())), preferred_element_type=jnp.float32
    )
    sigma = jax.nn.sigmoid(pre_sum)
    active = pre_sum * sigma
    partial_grad = jnp.sum(active * up_sum * grad_sum, axis=1)
    weight_g = recv_g.reshape(slot_count)
    scaled = weight_g[:, None] * grad_sum
    grad_up = (scaled * active).astype(jnp.bfloat16)
    grad_pre = (scaled * up_sum * sigma * (1.0 + pre_sum * (1.0 - sigma))).astype(jnp.bfloat16)
    contrib = lax.dot_general(
        grad_pre, gate_mat, (((1,), (1,)), ((), ())), preferred_element_type=jnp.float32
    )
    contrib = contrib + lax.dot_general(
        grad_up, up_mat, (((1,), (1,)), ((), ())), preferred_element_type=jnp.float32
    )
    returned, returned_grad = collect(
        contrib.astype(jnp.bfloat16).reshape(n_experts, most_slots, 4 * quarter),
        partial_grad.reshape(n_experts, 1, most_slots),
    )
    return returned, returned_grad


def local(tokens, out_grad, expert_ids, gate_values, w_gate, w_up, w_down):
    n_experts = lax.axis_size("expert")
    shares = lax.axis_size("tensor")
    tok_rows, quarter = tokens.shape
    top_count = expert_ids.shape[1]
    most_slots = 3 * tok_rows * top_count // (2 * n_experts)
    slot_count = n_experts * most_slots
    weights = (w_gate[0], w_up[0], w_down[0])
    fits = most_slots == 48 and tok_rows == 128 and top_count == 2 and quarter == 1792
    if fits and n_experts == 8 and shares == 4 and w_gate.shape[2] == 256:
        return fused(tokens, out_grad, expert_ids, gate_values, *weights)
    flat_ids = expert_ids.reshape(-1)
    onehot = flat_ids[:, None] == jnp.arange(n_experts, dtype=jnp.int32)[None, :]
    earlier = jnp.tri(flat_ids.shape[0], k=-1, dtype=jnp.bfloat16)
    before = jnp.dot(earlier, onehot.astype(jnp.bfloat16), preferred_element_type=jnp.float32)
    rank = jnp.sum(jnp.where(onehot, before, 0.0), axis=1).astype(jnp.int32)
    slot_of = (flat_ids * most_slots + rank).reshape(tok_rows, top_count)
    matches = slot_of[None, :, :] == jnp.arange(slot_count, dtype=jnp.int32)[:, None, None]
    chooser = jnp.any(matches, axis=2).astype(jnp.bfloat16)
    send_x = jnp.dot(chooser, tokens, preferred_element_type=jnp.float32).astype(jnp.bfloat16)
    send_dy = jnp.dot(chooser, out_grad, preferred_element_type=jnp.float32).astype(jnp.bfloat16)
    gate_wide = gate_values.astype(jnp.float32)[None, :, :]
    send_g = jnp.sum(jnp.where(matches, gate_wide, 0.0), axis=(1, 2))
    send_x = send_x.reshape(n_experts, most_slots, quarter)
    send_dy = send_dy.reshape(n_experts, most_slots, quarter)
    returned, returned_grad = in_steps(send_x, send_dy, send_g, *weights)
    d_tokens = lax.dot_general(
        chooser,
        returned.reshape(slot_count, quarter),
        (((0,), (0,)), ((), ())),
        preferred_element_type=jnp.float32,
    ).astype(jnp.bfloat16)
    grad_wide = returned_grad.reshape(slot_count)[:, None, None]
    d_gates = jnp.sum(jnp.where(matches, grad_wide, 0.0), axis=0)
    return (d_tokens, d_gates)


def solution(mesh):
    placed = (
        P("expert", "tensor"),
        P("expert", "tensor"),
        P("expert", None),
        P("expert", None),
        P("expert", None, "tensor"),
        P("expert", None, "tensor"),
        P("expert", "tensor", None),
    )
    return jax.shard_map(
        local,
        mesh=mesh,
        in_specs=placed,
        out_specs=(P("expert", "tensor"), P("expert", None)),
        check_vma=False,
    )
```

```python
import functools

import jax
import jax.numpy as jnp
from jax import lax
from jax.experimental import pallas as pl
from jax.experimental.pallas import tpu as pltpu
from jax.sharding import PartitionSpec as P


MESH = pl.DeviceIdType.MESH
VMEM = pl.BlockSpec(memory_space=pltpu.VMEM)
VMEM_BYTES = 56 * 1024 * 1024


def positions(n):
    me = lax.axis_index("expert")
    share = lax.axis_index("tensor")
    pair, side = share // 2, share % 2
    return me, share, pair * 2 + 1 - side, (1 - pair) * 2 + side


def greet(n, me, share, near, far):
    barrier = pltpu.get_barrier_semaphore()

    @pl.loop(1, n)
    def _(step):
        pl.semaphore_signal(
            barrier, inc=1, device_id=(lax.rem(me + step, n), share), device_id_type=MESH
        )

    for peer in (near, far):
        pl.semaphore_signal(barrier, inc=1, device_id=(me, peer), device_id_type=MESH)
    pl.semaphore_wait(barrier, n + 1)


def remote(src, dst, sems, index, device):
    return pltpu.make_async_remote_copy(
        src_ref=src,
        dst_ref=dst,
        send_sem=sems[0].at[index],
        recv_sem=sems[1].at[index],
        device_id=device,
        device_id_type=MESH,
    )


def spread_kernel(n, x_ref, dy_ref, g_ref, x_out, dy_out, g_out, *sems):
    me, share, near, far = positions(n)
    quarter = x_ref.shape[2]
    by_group, to_near, to_far, passed, gates = (sems[2 * i : 2 * i + 2] for i in range(5))
    own = sems[10]
    pairs = ((x_ref, x_out), (dy_ref, dy_out))

    def cols(which):
        return pl.ds(pl.multiple_of(which * quarter, 128), quarter)

    def block(which, group, owner):
        return pairs[which][1].at[group, :, cols(owner)]

    def dispatch(which, source, target):
        return remote(
            pairs[which][0].at[target],
            block(which, source, share),
            by_group,
            which * n + source,
            (target, share),
        )

    def gate_copy(source, target):
        return remote(
            g_ref.at[target], g_out.at[source], gates, source, (target, share)
        )

    def along(which, group, sent, sems_of, peer):
        return remote(
            block(which, group, sent),
            block(which, group, sent),
            sems_of,
            which * n + group,
            (me, peer),
        )

    greet(n, me, share, near, far)
    own_copies = [
        pltpu.make_async_copy(src.at[me], block(which, me, share), own.at[which])
        for which, (src, _) in enumerate(pairs)
    ]
    own_copies.append(pltpu.make_async_copy(g_ref.at[me], g_out.at[me], own.at[2]))
    for copy in own_copies:
        copy.start()
    for which in range(2):

        @pl.loop(1, n)
        def _(step):
            target = lax.rem(me + step, n)
            dispatch(which, me, target).start()

    @pl.loop(1, n)
    def _(step):
        gate_copy(me, lax.rem(me + step, n)).start()

    for copy in own_copies:
        copy.wait()

    def share_out(which, group):
        along(which, group, share, to_far, far).start()
        along(which, group, share, to_near, near).start()

    def pass_on(which, group):
        along(which, group, far, to_far, far).wait_recv()
        along(which, group, far, passed, near).start()

    for which in range(2):
        share_out(which, me)

        @pl.loop(1, n)
        def _(step):
            group = lax.rem(me - step + n, n)
            dispatch(which, group, me).wait_recv()
            share_out(which, group)
            pass_on(which, lax.rem(me - step + 1 + n, n))

        pass_on(which, lax.rem(me + 1, n))
    for which in range(2):

        @pl.loop(0, n)
        def _(group):
            along(which, group, near, to_near, near).wait_recv()
            along(which, group, 3 - share, passed, near).wait_recv()
            along(which, group, share, to_far, far).wait_send()
            along(which, group, share, to_near, near).wait_send()
            along(which, group, far, passed, near).wait_send()

        @pl.loop(1, n)
        def _(step):
            dispatch(which, me, lax.rem(me + step, n)).wait_send()

    @pl.loop(1, n)
    def _(step):
        gate_copy(me, lax.rem(me + step, n)).wait_send()
        gate_copy(lax.rem(me - step + n, n), me).wait_recv()


def spread(send_x, send_dy, send_g):
    n, most, quarter = send_x.shape
    wide = jax.ShapeDtypeStruct((n, most, 4 * quarter), send_x.dtype)
    dma = pltpu.SemaphoreType.DMA
    return pl.pallas_call(
        functools.partial(spread_kernel, n),
        out_shape=(wide, wide, jax.ShapeDtypeStruct(send_g.shape, send_g.dtype)),
        in_specs=[VMEM] * 3,
        out_specs=[VMEM] * 3,
        scratch_shapes=[dma((2 * n,))] * 8 + [dma((n,)), dma((n,)), dma((3,))],
        compiler_params=pltpu.CompilerParams(
            collective_id=0, has_side_effects=True, vmem_limit_bytes=VMEM_BYTES
        ),
    )(send_x, send_dy, send_g)


def collect_kernel(n, c_ref, p_ref, out, grad_out, near_got, far_put, far_got, put, total,
                   part_got, part_sum, *sems):
    me, share, near, far = positions(n)
    quarter = out.shape[2]
    to_near, to_far, back, grads, parts = (sems[2 * i : 2 * i + 2] for i in range(5))
    own = sems[10]

    def cols(which):
        return pl.ds(pl.multiple_of(which * quarter, 128), quarter)

    def half(group, slot):
        wanted = near if slot == 1 else 3 - share
        return remote(
            c_ref.at[group, :, cols(wanted)],
            near_got.at[group, slot],
            to_near,
            group * 2 + slot,
            (me, near),
        )

    def across(group):
        return remote(far_put.at[group], far_got.at[group], to_far, group, (me, far))

    def home(source, target):
        return remote(put.at[target], out.at[source], back, source, (target, share))

    def grad_home(source, target):
        return remote(
            part_sum.at[target], grad_out.at[source], grads, source, (target, share)
        )

    greet(n, me, share, near, far)
    part_near = remote(p_ref, part_got.at[0], parts, 0, (me, near))
    part_near.start()

    @pl.loop(0, n)
    def _(step):
        group = lax.rem(me + 1 + step, n)
        half(group, 0).start()
        half(group, 1).start()

    part_near.wait()
    part_sum[...] = p_ref[...] + part_got[0]
    part_far = remote(part_sum, part_got.at[1], parts, 1, (me, far))
    part_far.start()
    part_far.wait()
    part_sum[...] = part_sum[...] + part_got[1]

    @pl.loop(1, n)
    def _(step):
        grad_home(me, lax.rem(me + step, n)).start()

    def pair_sum(group):
        half(group, 0).wait_recv()
        mine = c_ref[group, :, cols(far)].astype(jnp.float32)
        far_put[group] = (mine + near_got[group, 0].astype(jnp.float32)).astype(far_put.dtype)
        across(group).start()
        half(group, 1).wait_recv()
        mine = c_ref[group, :, cols(share)].astype(jnp.float32)
        total[group] = mine + near_got[group, 1].astype(jnp.float32)

    def full_sum(group):
        across(group).wait_recv()
        put[group] = (total[group] + far_got[group].astype(jnp.float32)).astype(put.dtype)

    def send_home(group):
        full_sum(group)
        home(me, group).start()

    pair_sum(lax.rem(me + 1, n))

    @pl.loop(2, n + 1)
    def _(step):
        pair_sum(lax.rem(me + step, n))
        send_home(lax.rem(me + step - 1, n))

    full_sum(me)
    own_copies = [
        pltpu.make_async_copy(put.at[me], out.at[me], own.at[0]),
        pltpu.make_async_copy(part_sum.at[me], grad_out.at[me], own.at[1]),
    ]
    for copy in own_copies:
        copy.start()
    for copy in own_copies:
        copy.wait()

    @pl.loop(0, n)
    def _(group):
        half(group, 0).wait_send()
        half(group, 1).wait_send()
        across(group).wait_send()

    @pl.loop(1, n)
    def _(step):
        target = lax.rem(me + step, n)
        source = lax.rem(me - step + n, n)
        home(me, target).wait_send()
        grad_home(me, target).wait_send()
        home(source, me).wait_recv()
        grad_home(source, me).wait_recv()


def collect(contrib, partial_grad):
    n, most, width = contrib.shape
    quarter = width // 4
    kind = contrib.dtype
    dma = pltpu.SemaphoreType.DMA
    stage = pltpu.VMEM((n, most, quarter), kind)
    return pl.pallas_call(
        functools.partial(collect_kernel, n),
        out_shape=(
            jax.ShapeDtypeStruct((n, most, quarter), kind),
            jax.ShapeDtypeStruct(partial_grad.shape, partial_grad.dtype),
        ),
        in_specs=[VMEM] * 2,
        out_specs=[VMEM] * 2,
        scratch_shapes=[
            pltpu.VMEM((n, 2, most, quarter), kind),
            stage,
            stage,
            stage,
            pltpu.VMEM((n, most, quarter), jnp.float32),
            pltpu.VMEM((2,) + partial_grad.shape, jnp.float32),
            pltpu.VMEM(partial_grad.shape, jnp.float32),
            dma((2 * n,)),
            dma((2 * n,)),
        ]
        + [dma((n,))] * 6
        + [dma((2,)), dma((2,)), dma((2,))],
        compiler_params=pltpu.CompilerParams(
            collective_id=1, has_side_effects=True, vmem_limit_bytes=VMEM_BYTES
        ),
    )(contrib, partial_grad)


BATCHES = ((0, 4), (4, 6), (6, 7), (7, 8))


def fused_kernel(n, most, tok_ref, grad_ref, ids_ref, gv_ref, gate_hbm, up_hbm, down_hbm,
                 out, gate_out, send, gath, g_put, g_got, gu_w, down_w, chooser, code, pre_up,
                 dz, dpdu, near_put, mine, near_got, far_put, far_got, put, back, gu_t, down_t,
                 eye, spread_t, part, part_got, part_sum, part_back, load, *sems):
    me, share, near, far = positions(n)
    diag = 3 - share
    quarter = tok_ref.shape[1]
    tok_rows = tok_ref.shape[0]
    hidden = down_w.shape[0]
    chunk = quarter // 7
    (by_group, gates, to_far, to_near, passed, halves, over, back_sems, grads, parts) = (
        sems[2 * i : 2 * i + 2] for i in range(10)
    )

    def dest(i):
        at = me
        for bit in (1, 2, 4):
            if i & bit:
                at = at + bit * (1 - 2 * lax.rem(me // bit, 2))
        return at

    def nt(left, right):
        return lax.dot_general(
            left, right, (((1,), (1,)), ((), ())), preferred_element_type=jnp.float32
        )

    def remote_to(src, dst, sems_of, sent, landed, device):
        return pltpu.make_async_remote_copy(
            src_ref=src,
            dst_ref=dst,
            send_sem=sems_of[0].at[sent],
            recv_sem=sems_of[1].at[landed],
            device_id=(device, share),
            device_id_type=MESH,
        )

    def dispatch(i):
        return remote_to(send.at[i], gath.at[i, share], by_group, i, i, dest(i))

    def dispatched(p):
        block = gath.at[p, share]
        return remote_to(block, block, by_group, p, p, dest(p))

    def gate_copy(i):
        return remote_to(g_put.at[i], g_got.at[i], gates, i, i, dest(i))

    def gate_copied(p):
        return remote_to(g_got.at[p], g_got.at[p], gates, p, p, dest(p))

    def along_far(step):
        block = gath.at[step, share]
        return remote(block, block, to_far, step, (me, far))

    def along_near(step):
        block = gath.at[step, share]
        return remote(block, block, to_near, step, (me, near))

    def pass_near(step):
        block = gath.at[step, far]
        return remote(block, block, passed, step, (me, near))

    def half(batch, slot):
        first, last = BATCHES[batch]
        span = pl.ds(first, last - first)
        return remote(
            near_put.at[slot, span], near_got.at[slot, span], halves, batch * 2 + slot, (me, near)
        )

    def across(step):
        return remote(far_put.at[step], far_got.at[step], over, step, (me, far))

    def home(p):
        return remote_to(put.at[p], back.at[p], back_sems, p, p, dest(p))

    def came_home(i):
        return remote_to(back.at[i], back.at[i], back_sems, i, i, dest(i))

    def grad_home(p):
        return remote_to(part_sum.at[p], part_back.at[p], grads, p, p, dest(p))

    def grad_came_home(i):
        return remote_to(part_back.at[i], part_back.at[i], grads, i, i, dest(i))

    def part_copy(batch, which):
        first, last = BATCHES[batch]
        span = pl.ds(first, last - first)
        peer = (near, far, diag)[which]
        return remote(
            part.at[span], part_got.at[which, span], parts, batch * 3 + which, (me, peer)
        )

    loads = [
        pltpu.make_async_copy(gate_hbm, gu_w.at[:, pl.ds(0, hidden)], load.at[0]),
        pltpu.make_async_copy(up_hbm, gu_w.at[:, pl.ds(hidden, hidden)], load.at[1]),
        pltpu.make_async_copy(down_hbm, down_w, load.at[2]),
    ]
    for copy in loads:
        copy.start()
    barrier = pltpu.get_barrier_semaphore()
    for step in range(1, n):
        pl.semaphore_signal(barrier, inc=1, device_id=(dest(step), share), device_id_type=MESH)
    for peer in (near, far, diag):
        pl.semaphore_signal(barrier, inc=1, device_id=(me, peer), device_id_type=MESH)

    lane = lax.broadcasted_iota(jnp.int32, (tok_rows, 128), 1)
    row = lax.broadcasted_iota(jnp.int32, (tok_rows, 128), 0)
    ids = ids_ref[...]
    gv = gv_ref[...].astype(jnp.float32)
    first_named, second_named = row == ids[0:1, :], row == ids[1:2, :]
    named = jnp.where(first_named | second_named, 1.0, 0.0)
    earlier = jnp.where(row < lane, 1.0, 0.0).astype(jnp.bfloat16)
    rank = jnp.dot(named.astype(jnp.bfloat16), earlier, preferred_element_type=jnp.float32)
    codes = jnp.where(named > 0.5, rank, -1.0)
    code[...] = codes
    weight_t = jnp.where(first_named, gv[0:1, :], 0.0) + jnp.where(second_named, gv[1:2, :], 0.0)
    slot_row = lax.broadcasted_iota(jnp.int32, (most, tok_rows), 0).astype(jnp.float32)

    def code_of(i):
        return jnp.sum(jnp.where(row == dest(i), code[...], 0.0), axis=0, keepdims=True)

    def choose(i):
        its_weight = jnp.sum(jnp.where(row == dest(i), weight_t, 0.0), axis=0, keepdims=True)
        hit = jnp.where(slot_row == code_of(i), 1.0, 0.0)
        chooser[i] = hit.astype(chooser.dtype)
        slot_weight = jnp.sum(hit * its_weight, axis=1, keepdims=True)
        g_put[i] = jnp.broadcast_to(slot_weight, (most, 128)).astype(g_put.dtype)

    def pick(step, which):
        rows_of = (tok_ref, grad_ref)[which]
        return jnp.dot(
            chooser[step], rows_of[...], preferred_element_type=jnp.float32
        ).astype(send.dtype)

    for i in range(n):
        choose(i)
        for which in range(2):
            if i:
                send[i, which] = pick(i, which)
            else:
                gath[0, share, which] = pick(0, which)
    g_got[0] = g_put[0]
    pl.semaphore_wait(barrier, n + 2)
    along_far(0).start()
    along_near(0).start()
    for i in (4, 1, 2, 5, 3, 6, 7):
        gate_copy(i).start()
        dispatch(i).start()

    def turn_inputs():
        wide_row = lax.broadcasted_iota(jnp.int32, (hidden, hidden), 0)
        wide_lane = lax.broadcasted_iota(jnp.int32, (hidden, hidden), 1)
        eye[...] = jnp.where(wide_row == wide_lane, 1.0, 0.0).astype(eye.dtype)

    def turn(q):
        for step in range(7):
            at = slice(q * quarter + step * chunk, q * quarter + (step + 1) * chunk)
            for part_at in (0, hidden):
                gu_t[part_at : part_at + hidden, at] = nt(
                    eye[...], gu_w[at, part_at : part_at + hidden]
                ).astype(gu_t.dtype)

    def turn_down(q):
        for step in range(7):
            at = slice(q * quarter + step * chunk, q * quarter + (step + 1) * chunk)
            down_t[at, :] = nt(eye[...], down_w[:, at]).astype(down_t.dtype)

    def project(batch):
        first, last = BATCHES[batch]
        rows = (last - first) * most

        @pl.loop(0, 4)
        def _(q):
            at = pl.ds(pl.multiple_of(q * quarter, 128), quarter)
            x = gath[first:last, q, 0].reshape(rows, quarter)
            dy = gath[first:last, q, 1].reshape(rows, quarter)
            got = jnp.dot(x, gu_w[at, :], preferred_element_type=jnp.float32)
            got_dz = jnp.dot(dy, down_t[at, :], preferred_element_type=jnp.float32)

            @pl.when(q == 0)
            def _():
                pre_up[0:rows, :] = got
                dz[0:rows, :] = got_dz

            @pl.when(q > 0)
            def _():
                pre_up[0:rows, :] += got
                dz[0:rows, :] += got_dz

    diagonal = lax.broadcasted_iota(jnp.int32, (most, 128), 0) == lax.broadcasted_iota(
        jnp.int32, (most, 128), 1
    )

    def activate(batch):
        first, last = BATCHES[batch]
        for step in range(first, last):
            if step:
                gate_copied(step).wait_recv()
            at = slice((step - first) * most, (step - first + 1) * most)
            pre_b, up_b, dz_b = pre_up[at, 0:hidden], pre_up[at, hidden:], dz[at, :]
            sigma = jax.nn.sigmoid(pre_b)
            active = pre_b * sigma
            slot_sum = jnp.sum(active * up_b * dz_b, axis=1, keepdims=True)
            flat = jnp.sum(jnp.where(diagonal, slot_sum, 0.0), axis=0, keepdims=True)
            part[step] = jnp.broadcast_to(flat, (8, 128))
            scaled = g_got[step][:, :1].astype(jnp.float32) * dz_b
            dpdu[at, hidden:] = (scaled * active).astype(dpdu.dtype)
            dpdu[at, 0:hidden] = (
                scaled * up_b * sigma * (1.0 + pre_b * (1.0 - sigma))
            ).astype(dpdu.dtype)
        for which in range(3):
            part_copy(batch, which).start()

    def expand(batch, wanted, store):
        first, last = BATCHES[batch]
        rows = (last - first) * most

        for step in range(7):
            start = wanted * quarter + step * chunk
            at = pl.ds(pl.multiple_of(start, 128), chunk)
            value = jnp.dot(
                dpdu[0:rows, :], gu_t[:, at], preferred_element_type=jnp.float32
            )
            store(
                slice(step * chunk, (step + 1) * chunk),
                value.reshape(last - first, most, chunk),
            )

    def give_back(batch):
        first, last = BATCHES[batch]
        for slot, wanted in ((0, diag), (1, near)):

            def keep(at, value):
                near_put[slot, first:last, :, at] = value.astype(near_put.dtype)

            expand(batch, wanted, keep)
            half(batch, slot).start()
        for slot, wanted in ((0, far), (1, share)):

            def keep_wide(at, value):
                mine[slot, first:last, :, at] = value

            expand(batch, wanted, keep_wide)

    def cross(batch, steps):
        for step in steps:
            far_put[step] = (mine[0, step] + near_got[0, step].astype(jnp.float32)).astype(
                far_put.dtype
            )
            across(step).start()

    def go_home(step):
        across(step).wait_recv()
        value = mine[1, step] + near_got[1, step].astype(jnp.float32)
        value = (value + far_got[step].astype(jnp.float32)).astype(put.dtype)
        if step:
            put[step] = value
            home(step).start()
        else:
            back[0] = value

    def share_parts(batch):
        first, last = BATCHES[batch]
        for which in range(3):
            part_copy(batch, which).wait_recv()
        for step in range(first, last):
            part_sum[step] = (
                part[step] + part_got[0, step] + part_got[1, step] + part_got[2, step]
            )
            if step:
                grad_home(step).start()
            else:
                part_back[0] = part_sum[0]

    def arrive(step):
        dispatched(step).wait_recv()
        along_far(step).start()
        along_near(step).start()

    def pass_on(step):
        along_far_from(step).wait_recv()
        pass_near(step).start()

    def along_far_from(step):
        block = gath.at[step, far]
        return remote(block, block, to_far, step, (me, far))

    def settle(step):
        block = gath.at[step, near]
        remote(block, block, to_near, step, (me, near)).wait_recv()
        block = gath.at[step, diag]
        remote(block, block, passed, step, (me, near)).wait_recv()

    turn_inputs()
    for copy in loads:
        copy.wait()
    for q in range(4):
        turn(q)
    arrive(1)
    pass_on(0)
    for q in range(4):
        turn_down(q)
    arrive(2)
    arrive(4)
    pass_on(1)
    arrive(3)
    pass_on(2)
    arrive(5)
    pass_on(4)
    pass_on(3)
    for step in range(4):
        settle(step)
    project(0)
    activate(0)
    arrive(6)
    give_back(0)
    half(0, 0).wait_recv()
    half(0, 1).wait_recv()
    share_parts(0)
    pass_on(5)
    settle(4)
    settle(5)
    project(1)
    activate(1)
    give_back(1)
    half(1, 0).wait_recv()
    half(1, 1).wait_recv()
    cross(1, (4, 5))
    pass_on(6)
    settle(6)
    project(2)
    activate(2)
    arrive(7)
    give_back(2)
    half(2, 0).wait_recv()
    half(2, 1).wait_recv()
    cross(2, (6,))
    go_home(4)
    go_home(5)
    share_parts(1)
    share_parts(2)
    cross(0, (2,))
    pass_on(7)
    settle(7)
    project(3)
    activate(3)
    give_back(3)
    half(3, 0).wait_recv()
    half(3, 1).wait_recv()
    cross(3, (7,))
    cross(0, (3, 1, 0))
    go_home(6)
    share_parts(3)
    go_home(2)
    go_home(7)
    go_home(3)

    ids = ids_ref[...]
    grad_total = jnp.zeros((2, tok_rows), jnp.float32)
    for i in range(n):
        if i:
            grad_came_home(i).wait_recv()
        held = part_back[i][0:1, 0:most]
        hit = chooser[i].astype(jnp.float32)
        value = lax.dot_general(
            held,
            hit,
            (((1,), (0,)), ((), ())),
            precision=lax.Precision.HIGHEST,
            preferred_element_type=jnp.float32,
        )
        grad_total = grad_total + jnp.where(ids == dest(i), value, 0.0)
    gate_out[...] = grad_total
    for i in range(n):
        spread_t[:, i * most : (i + 1) * most] = chooser[i].astype(jnp.float32).T.astype(
            spread_t.dtype
        )
    go_home(1)
    came_home(4).wait_recv()
    came_home(5).wait_recv()
    came_home(6).wait_recv()
    came_home(7).wait_recv()
    came_home(2).wait_recv()
    came_home(3).wait_recv()
    came_home(1).wait_recv()
    go_home(0)

    @pl.loop(0, 7)
    def _(step):
        at = pl.ds(pl.multiple_of(step * chunk, 128), chunk)
        out[:, at] = jnp.dot(
            spread_t[...],
            back[:, :, at].reshape(n * most, chunk),
            preferred_element_type=jnp.float32,
        ).astype(out.dtype)

    for step in range(n):
        along_far(step).wait_send()
        along_near(step).wait_send()
        pass_near(step).wait_send()
        across(step).wait_send()
        if step:
            dispatch(step).wait_send()
            gate_copy(step).wait_send()
            home(step).wait_send()
            grad_home(step).wait_send()
    for batch in range(len(BATCHES)):
        for slot in range(2):
            half(batch, slot).wait_send()
        for which in range(3):
            part_copy(batch, which).wait_send()


def fused(tokens, out_grad, expert_ids, gate_values, gate_mat, up_mat, down_mat):
    n = lax.axis_size("expert")
    tok_rows, quarter = tokens.shape
    flipped = expert_ids.T
    most = 3 * tok_rows * expert_ids.shape[1] // (2 * n)
    kind = tokens.dtype
    hidden = gate_mat.shape[1]
    rows = max(last - first for first, last in BATCHES) * most
    dma = pltpu.SemaphoreType.DMA
    anywhere = pl.BlockSpec(memory_space=pl.ANY)
    stage = pltpu.VMEM((n, most, quarter), kind)
    pair = pltpu.VMEM((2, n, most, quarter), kind)
    flat = pltpu.VMEM((n, 8, 128), jnp.float32)
    narrow = pltpu.VMEM((n, most, 128), kind)
    d_tokens, d_gates = pl.pallas_call(
        functools.partial(fused_kernel, n, most),
        out_shape=(
            jax.ShapeDtypeStruct(tokens.shape, kind),
            jax.ShapeDtypeStruct(flipped.shape, jnp.float32),
        ),
        in_specs=[VMEM] * 4 + [anywhere] * 3,
        out_specs=[VMEM] * 2,
        scratch_shapes=[
            pltpu.VMEM((n, 2, most, quarter), kind),
            pltpu.VMEM((n, 4, 2, most, quarter), kind),
            narrow,
            narrow,
            pltpu.VMEM((4 * quarter, 2 * hidden), kind),
            pltpu.VMEM(down_mat.shape, kind),
            pltpu.VMEM((n, most, tok_rows), kind),
            pltpu.VMEM((tok_rows, 128), jnp.float32),
            pltpu.VMEM((rows, 2 * hidden), jnp.float32),
            pltpu.VMEM((rows, hidden), jnp.float32),
            pltpu.VMEM((rows, 2 * hidden), kind),
            pair,
            pltpu.VMEM((2, n, most, quarter), jnp.float32),
            pair,
            stage,
            stage,
            stage,
            stage,
            pltpu.VMEM((2 * hidden, 4 * quarter), kind),
            pltpu.VMEM((4 * quarter, hidden), kind),
            pltpu.VMEM((hidden, hidden), kind),
            pltpu.VMEM((tok_rows, n * most), kind),
            flat,
            pltpu.VMEM((3, n, 8, 128), jnp.float32),
            flat,
            flat,
            dma((3,)),
        ]
        + [dma((n,))] * 10
        + [dma((2 * len(BATCHES),))] * 2
        + [dma((n,))] * 6
        + [dma((3 * len(BATCHES),))] * 2,
        compiler_params=pltpu.CompilerParams(
            collective_id=2, has_side_effects=True, vmem_limit_bytes=VMEM_BYTES
        ),
    )(tokens, out_grad, flipped, gate_values.T, gate_mat, up_mat, down_mat)
    return d_tokens, d_gates.T


def in_steps(send_x, send_dy, send_g, gate_mat, up_mat, down_mat):
    n_experts, most_slots, quarter = send_x.shape
    slot_count = n_experts * most_slots
    piece_x, piece_dy, recv_g = spread(
        send_x,
        send_dy,
        send_g.reshape(n_experts, 1, most_slots),
    )
    piece_x = piece_x.reshape(slot_count, 4 * quarter)
    piece_dy = piece_dy.reshape(slot_count, 4 * quarter)
    pre_sum = jnp.dot(piece_x, gate_mat, preferred_element_type=jnp.float32)
    up_sum = jnp.dot(piece_x, up_mat, preferred_element_type=jnp.float32)
    grad_sum = lax.dot_general(
        piece_dy, down_mat, (((1,), (1,)), ((), ())), preferred_element_type=jnp.float32
    )
    sigma = jax.nn.sigmoid(pre_sum)
    active = pre_sum * sigma
    partial_grad = jnp.sum(active * up_sum * grad_sum, axis=1)
    weight_g = recv_g.reshape(slot_count)
    scaled = weight_g[:, None] * grad_sum
    grad_up = (scaled * active).astype(jnp.bfloat16)
    grad_pre = (scaled * up_sum * sigma * (1.0 + pre_sum * (1.0 - sigma))).astype(jnp.bfloat16)
    contrib = lax.dot_general(
        grad_pre, gate_mat, (((1,), (1,)), ((), ())), preferred_element_type=jnp.float32
    )
    contrib = contrib + lax.dot_general(
        grad_up, up_mat, (((1,), (1,)), ((), ())), preferred_element_type=jnp.float32
    )
    returned, returned_grad = collect(
        contrib.astype(jnp.bfloat16).reshape(n_experts, most_slots, 4 * quarter),
        partial_grad.reshape(n_experts, 1, most_slots),
    )
    return returned, returned_grad


def local(tokens, out_grad, expert_ids, gate_values, w_gate, w_up, w_down):
    n_experts = lax.axis_size("expert")
    shares = lax.axis_size("tensor")
    tok_rows, quarter = tokens.shape
    top_count = expert_ids.shape[1]
    most_slots = 3 * tok_rows * top_count // (2 * n_experts)
    slot_count = n_experts * most_slots
    weights = (w_gate[0], w_up[0], w_down[0])
    fits = most_slots == 48 and tok_rows == 128 and top_count == 2 and quarter == 1792
    if fits and n_experts == 8 and shares == 4 and w_gate.shape[2] == 256:
        return fused(tokens, out_grad, expert_ids, gate_values, *weights)
    flat_ids = expert_ids.reshape(-1)
    onehot = flat_ids[:, None] == jnp.arange(n_experts, dtype=jnp.int32)[None, :]
    earlier = jnp.tri(flat_ids.shape[0], k=-1, dtype=jnp.bfloat16)
    before = jnp.dot(earlier, onehot.astype(jnp.bfloat16), preferred_element_type=jnp.float32)
    rank = jnp.sum(jnp.where(onehot, before, 0.0), axis=1).astype(jnp.int32)
    slot_of = (flat_ids * most_slots + rank).reshape(tok_rows, top_count)
    matches = slot_of[None, :, :] == jnp.arange(slot_count, dtype=jnp.int32)[:, None, None]
    chooser = jnp.any(matches, axis=2).astype(jnp.bfloat16)
    send_x = jnp.dot(chooser, tokens, preferred_element_type=jnp.float32).astype(jnp.bfloat16)
    send_dy = jnp.dot(chooser, out_grad, preferred_element_type=jnp.float32).astype(jnp.bfloat16)
    gate_wide = gate_values.astype(jnp.float32)[None, :, :]
    send_g = jnp.sum(jnp.where(matches, gate_wide, 0.0), axis=(1, 2))
    send_x = send_x.reshape(n_experts, most_slots, quarter)
    send_dy = send_dy.reshape(n_experts, most_slots, quarter)
    returned, returned_grad = in_steps(send_x, send_dy, send_g, *weights)
    d_tokens = lax.dot_general(
        chooser,
        returned.reshape(slot_count, quarter),
        (((0,), (0,)), ((), ())),
        preferred_element_type=jnp.float32,
    ).astype(jnp.bfloat16)
    grad_wide = returned_grad.reshape(slot_count)[:, None, None]
    d_gates = jnp.sum(jnp.where(matches, grad_wide, 0.0), axis=0)
    return (d_tokens, d_gates)


def solution(mesh):
    placed = (
        P("expert", "tensor"),
        P("expert", "tensor"),
        P("expert", None),
        P("expert", None),
        P("expert", None, "tensor"),
        P("expert", None, "tensor"),
        P("expert", "tensor", None),
    )
    return jax.shard_map(
        local,
        mesh=mesh,
        in_specs=placed,
        out_specs=(P("expert", "tensor"), P("expert", None)),
        check_vma=False,
    )
```

```python
import functools

import jax
import jax.numpy as jnp
from jax import lax
from jax.experimental import pallas as pl
from jax.experimental.pallas import tpu as pltpu
from jax.sharding import PartitionSpec as P


MESH = pl.DeviceIdType.MESH
VMEM = pl.BlockSpec(memory_space=pltpu.VMEM)
VMEM_BYTES = 56 * 1024 * 1024


def positions(n):
    me = lax.axis_index("expert")
    share = lax.axis_index("tensor")
    pair, side = share // 2, share % 2
    return me, share, pair * 2 + 1 - side, (1 - pair) * 2 + side


def greet(n, me, share, near, far):
    barrier = pltpu.get_barrier_semaphore()

    @pl.loop(1, n)
    def _(step):
        pl.semaphore_signal(
            barrier, inc=1, device_id=(lax.rem(me + step, n), share), device_id_type=MESH
        )

    for peer in (near, far):
        pl.semaphore_signal(barrier, inc=1, device_id=(me, peer), device_id_type=MESH)
    pl.semaphore_wait(barrier, n + 1)


def remote(src, dst, sems, index, device):
    return pltpu.make_async_remote_copy(
        src_ref=src,
        dst_ref=dst,
        send_sem=sems[0].at[index],
        recv_sem=sems[1].at[index],
        device_id=device,
        device_id_type=MESH,
    )


def spread_kernel(n, x_ref, dy_ref, g_ref, x_out, dy_out, g_out, *sems):
    me, share, near, far = positions(n)
    quarter = x_ref.shape[2]
    by_group, to_near, to_far, passed, gates = (sems[2 * i : 2 * i + 2] for i in range(5))
    own = sems[10]
    pairs = ((x_ref, x_out), (dy_ref, dy_out))

    def cols(which):
        return pl.ds(pl.multiple_of(which * quarter, 128), quarter)

    def block(which, group, owner):
        return pairs[which][1].at[group, :, cols(owner)]

    def dispatch(which, source, target):
        return remote(
            pairs[which][0].at[target],
            block(which, source, share),
            by_group,
            which * n + source,
            (target, share),
        )

    def gate_copy(source, target):
        return remote(
            g_ref.at[target], g_out.at[source], gates, source, (target, share)
        )

    def along(which, group, sent, sems_of, peer):
        return remote(
            block(which, group, sent),
            block(which, group, sent),
            sems_of,
            which * n + group,
            (me, peer),
        )

    greet(n, me, share, near, far)
    own_copies = [
        pltpu.make_async_copy(src.at[me], block(which, me, share), own.at[which])
        for which, (src, _) in enumerate(pairs)
    ]
    own_copies.append(pltpu.make_async_copy(g_ref.at[me], g_out.at[me], own.at[2]))
    for copy in own_copies:
        copy.start()
    for which in range(2):

        @pl.loop(1, n)
        def _(step):
            target = lax.rem(me + step, n)
            dispatch(which, me, target).start()

    @pl.loop(1, n)
    def _(step):
        gate_copy(me, lax.rem(me + step, n)).start()

    for copy in own_copies:
        copy.wait()

    def share_out(which, group):
        along(which, group, share, to_far, far).start()
        along(which, group, share, to_near, near).start()

    def pass_on(which, group):
        along(which, group, far, to_far, far).wait_recv()
        along(which, group, far, passed, near).start()

    for which in range(2):
        share_out(which, me)

        @pl.loop(1, n)
        def _(step):
            group = lax.rem(me - step + n, n)
            dispatch(which, group, me).wait_recv()
            share_out(which, group)
            pass_on(which, lax.rem(me - step + 1 + n, n))

        pass_on(which, lax.rem(me + 1, n))
    for which in range(2):

        @pl.loop(0, n)
        def _(group):
            along(which, group, near, to_near, near).wait_recv()
            along(which, group, 3 - share, passed, near).wait_recv()
            along(which, group, share, to_far, far).wait_send()
            along(which, group, share, to_near, near).wait_send()
            along(which, group, far, passed, near).wait_send()

        @pl.loop(1, n)
        def _(step):
            dispatch(which, me, lax.rem(me + step, n)).wait_send()

    @pl.loop(1, n)
    def _(step):
        gate_copy(me, lax.rem(me + step, n)).wait_send()
        gate_copy(lax.rem(me - step + n, n), me).wait_recv()


def spread(send_x, send_dy, send_g):
    n, most, quarter = send_x.shape
    wide = jax.ShapeDtypeStruct((n, most, 4 * quarter), send_x.dtype)
    dma = pltpu.SemaphoreType.DMA
    return pl.pallas_call(
        functools.partial(spread_kernel, n),
        out_shape=(wide, wide, jax.ShapeDtypeStruct(send_g.shape, send_g.dtype)),
        in_specs=[VMEM] * 3,
        out_specs=[VMEM] * 3,
        scratch_shapes=[dma((2 * n,))] * 8 + [dma((n,)), dma((n,)), dma((3,))],
        compiler_params=pltpu.CompilerParams(
            collective_id=0, has_side_effects=True, vmem_limit_bytes=VMEM_BYTES
        ),
    )(send_x, send_dy, send_g)


def collect_kernel(n, c_ref, p_ref, out, grad_out, near_got, far_put, far_got, put, total,
                   part_got, part_sum, *sems):
    me, share, near, far = positions(n)
    quarter = out.shape[2]
    to_near, to_far, back, grads, parts = (sems[2 * i : 2 * i + 2] for i in range(5))
    own = sems[10]

    def cols(which):
        return pl.ds(pl.multiple_of(which * quarter, 128), quarter)

    def half(group, slot):
        wanted = near if slot == 1 else 3 - share
        return remote(
            c_ref.at[group, :, cols(wanted)],
            near_got.at[group, slot],
            to_near,
            group * 2 + slot,
            (me, near),
        )

    def across(group):
        return remote(far_put.at[group], far_got.at[group], to_far, group, (me, far))

    def home(source, target):
        return remote(put.at[target], out.at[source], back, source, (target, share))

    def grad_home(source, target):
        return remote(
            part_sum.at[target], grad_out.at[source], grads, source, (target, share)
        )

    greet(n, me, share, near, far)
    part_near = remote(p_ref, part_got.at[0], parts, 0, (me, near))
    part_near.start()

    @pl.loop(0, n)
    def _(step):
        group = lax.rem(me + 1 + step, n)
        half(group, 0).start()
        half(group, 1).start()

    part_near.wait()
    part_sum[...] = p_ref[...] + part_got[0]
    part_far = remote(part_sum, part_got.at[1], parts, 1, (me, far))
    part_far.start()
    part_far.wait()
    part_sum[...] = part_sum[...] + part_got[1]

    @pl.loop(1, n)
    def _(step):
        grad_home(me, lax.rem(me + step, n)).start()

    def pair_sum(group):
        half(group, 0).wait_recv()
        mine = c_ref[group, :, cols(far)].astype(jnp.float32)
        far_put[group] = (mine + near_got[group, 0].astype(jnp.float32)).astype(far_put.dtype)
        across(group).start()
        half(group, 1).wait_recv()
        mine = c_ref[group, :, cols(share)].astype(jnp.float32)
        total[group] = mine + near_got[group, 1].astype(jnp.float32)

    def full_sum(group):
        across(group).wait_recv()
        put[group] = (total[group] + far_got[group].astype(jnp.float32)).astype(put.dtype)

    def send_home(group):
        full_sum(group)
        home(me, group).start()

    pair_sum(lax.rem(me + 1, n))

    @pl.loop(2, n + 1)
    def _(step):
        pair_sum(lax.rem(me + step, n))
        send_home(lax.rem(me + step - 1, n))

    full_sum(me)
    own_copies = [
        pltpu.make_async_copy(put.at[me], out.at[me], own.at[0]),
        pltpu.make_async_copy(part_sum.at[me], grad_out.at[me], own.at[1]),
    ]
    for copy in own_copies:
        copy.start()
    for copy in own_copies:
        copy.wait()

    @pl.loop(0, n)
    def _(group):
        half(group, 0).wait_send()
        half(group, 1).wait_send()
        across(group).wait_send()

    @pl.loop(1, n)
    def _(step):
        target = lax.rem(me + step, n)
        source = lax.rem(me - step + n, n)
        home(me, target).wait_send()
        grad_home(me, target).wait_send()
        home(source, me).wait_recv()
        grad_home(source, me).wait_recv()


def collect(contrib, partial_grad):
    n, most, width = contrib.shape
    quarter = width // 4
    kind = contrib.dtype
    dma = pltpu.SemaphoreType.DMA
    stage = pltpu.VMEM((n, most, quarter), kind)
    return pl.pallas_call(
        functools.partial(collect_kernel, n),
        out_shape=(
            jax.ShapeDtypeStruct((n, most, quarter), kind),
            jax.ShapeDtypeStruct(partial_grad.shape, partial_grad.dtype),
        ),
        in_specs=[VMEM] * 2,
        out_specs=[VMEM] * 2,
        scratch_shapes=[
            pltpu.VMEM((n, 2, most, quarter), kind),
            stage,
            stage,
            stage,
            pltpu.VMEM((n, most, quarter), jnp.float32),
            pltpu.VMEM((2,) + partial_grad.shape, jnp.float32),
            pltpu.VMEM(partial_grad.shape, jnp.float32),
            dma((2 * n,)),
            dma((2 * n,)),
        ]
        + [dma((n,))] * 6
        + [dma((2,)), dma((2,)), dma((2,))],
        compiler_params=pltpu.CompilerParams(
            collective_id=1, has_side_effects=True, vmem_limit_bytes=VMEM_BYTES
        ),
    )(contrib, partial_grad)


BATCHES = ((0, 4), (4, 6), (6, 7), (7, 8))


def fused_kernel(n, most, tok_ref, grad_ref, ids_ref, gv_ref, gate_hbm, up_hbm, down_hbm,
                 out, gate_out, send, gath, g_put, g_got, gu_w, down_w, chooser, code, pre_up,
                 dz, dpdu, near_put, mine, near_got, far_put, far_got, put, back, gu_t, down_t,
                 eye, spread_t, part, part_got, part_sum, part_back, load, *sems):
    me, share, near, far = positions(n)
    diag = 3 - share
    quarter = tok_ref.shape[1]
    tok_rows = tok_ref.shape[0]
    hidden = down_w.shape[0]
    chunk = quarter // 7
    (by_group, gates, to_far, to_near, passed, halves, over, back_sems, grads, parts) = (
        sems[2 * i : 2 * i + 2] for i in range(10)
    )

    inner = lax.rem((me // 2 + 1) // 2, 2)

    def dest(i):
        at = me
        for bit in (1, 2, 4):
            if i & bit:
                at = at + bit * (1 - 2 * lax.rem(me // bit, 2))
        return at

    def place(i):
        return {2: 4 - 2 * inner, 3: 5 - 2 * inner, 4: 2 + 2 * inner, 5: 3 + 2 * inner}.get(i, i)

    def origin(p):
        return {2: 2 + 2 * inner, 3: 3 + 2 * inner, 4: 4 - 2 * inner, 5: 5 - 2 * inner}.get(p, p)

    def source(p):
        if p in (2, 3, 4, 5):
            other = p + 2 if p < 4 else p - 2
            return dest(p) * (1 - inner) + dest(other) * inner
        return dest(p)

    def nt(left, right):
        return lax.dot_general(
            left, right, (((1,), (1,)), ((), ())), preferred_element_type=jnp.float32
        )

    def remote_to(src, dst, sems_of, sent, landed, device):
        return pltpu.make_async_remote_copy(
            src_ref=src,
            dst_ref=dst,
            send_sem=sems_of[0].at[sent],
            recv_sem=sems_of[1].at[landed],
            device_id=(device, share),
            device_id_type=MESH,
        )

    def dispatch(i):
        p = place(i)
        return remote_to(send.at[i], gath.at[p, share], by_group, i, p, dest(i))

    def dispatched(p):
        block = gath.at[p, share]
        return remote_to(block, block, by_group, p, p, source(p))

    def gate_copy(i):
        p = place(i)
        return remote_to(g_put.at[i], g_got.at[p], gates, i, p, dest(i))

    def gate_copied(p):
        return remote_to(g_got.at[p], g_got.at[p], gates, p, p, source(p))

    def along_far(step):
        block = gath.at[step, share]
        return remote(block, block, to_far, step, (me, far))

    def along_near(step):
        block = gath.at[step, share]
        return remote(block, block, to_near, step, (me, near))

    def pass_near(step):
        block = gath.at[step, far]
        return remote(block, block, passed, step, (me, near))

    def half(batch, slot):
        first, last = BATCHES[batch]
        span = pl.ds(first, last - first)
        return remote(
            near_put.at[slot, span], near_got.at[slot, span], halves, batch * 2 + slot, (me, near)
        )

    def across(step):
        return remote(far_put.at[step], far_got.at[step], over, step, (me, far))

    def home(p):
        i = origin(p)
        return remote_to(put.at[p], back.at[i], back_sems, p, i, source(p))

    def came_home(i):
        return remote_to(back.at[i], back.at[i], back_sems, i, i, dest(i))

    def grad_home(p):
        i = origin(p)
        return remote_to(part_sum.at[p], part_back.at[i], grads, p, i, source(p))

    def grad_came_home(i):
        return remote_to(part_back.at[i], part_back.at[i], grads, i, i, dest(i))

    def part_copy(batch, which):
        first, last = BATCHES[batch]
        span = pl.ds(first, last - first)
        peer = (near, far, diag)[which]
        return remote(
            part.at[span], part_got.at[which, span], parts, batch * 3 + which, (me, peer)
        )

    loads = [
        pltpu.make_async_copy(gate_hbm, gu_w.at[:, pl.ds(0, hidden)], load.at[0]),
        pltpu.make_async_copy(up_hbm, gu_w.at[:, pl.ds(hidden, hidden)], load.at[1]),
        pltpu.make_async_copy(down_hbm, down_w, load.at[2]),
    ]
    for copy in loads:
        copy.start()
    barrier = pltpu.get_barrier_semaphore()
    for step in range(1, n):
        pl.semaphore_signal(barrier, inc=1, device_id=(dest(step), share), device_id_type=MESH)
    for peer in (near, far, diag):
        pl.semaphore_signal(barrier, inc=1, device_id=(me, peer), device_id_type=MESH)

    lane = lax.broadcasted_iota(jnp.int32, (tok_rows, 128), 1)
    row = lax.broadcasted_iota(jnp.int32, (tok_rows, 128), 0)
    ids = ids_ref[...]
    gv = gv_ref[...].astype(jnp.float32)
    first_named, second_named = row == ids[0:1, :], row == ids[1:2, :]
    named = jnp.where(first_named | second_named, 1.0, 0.0)
    earlier = jnp.where(row < lane, 1.0, 0.0).astype(jnp.bfloat16)
    rank = jnp.dot(named.astype(jnp.bfloat16), earlier, preferred_element_type=jnp.float32)
    codes = jnp.where(named > 0.5, rank, -1.0)
    code[...] = codes
    weight_t = jnp.where(first_named, gv[0:1, :], 0.0) + jnp.where(second_named, gv[1:2, :], 0.0)
    slot_row = lax.broadcasted_iota(jnp.int32, (most, tok_rows), 0).astype(jnp.float32)

    def code_of(i):
        return jnp.sum(jnp.where(row == dest(i), code[...], 0.0), axis=0, keepdims=True)

    def choose(i):
        its_weight = jnp.sum(jnp.where(row == dest(i), weight_t, 0.0), axis=0, keepdims=True)
        hit = jnp.where(slot_row == code_of(i), 1.0, 0.0)
        chooser[i] = hit.astype(chooser.dtype)
        slot_weight = jnp.sum(hit * its_weight, axis=1, keepdims=True)
        g_put[i] = jnp.broadcast_to(slot_weight, (most, 128)).astype(g_put.dtype)

    def pick(step, which):
        rows_of = (tok_ref, grad_ref)[which]
        return jnp.dot(
            chooser[step], rows_of[...], preferred_element_type=jnp.float32
        ).astype(send.dtype)

    for i in range(n):
        choose(i)
        for which in range(2):
            if i:
                send[i, which] = pick(i, which)
            else:
                gath[0, share, which] = pick(0, which)
    g_got[0] = g_put[0]
    pl.semaphore_wait(barrier, n + 2)
    along_far(0).start()
    along_near(0).start()
    for i in (4, 1, 5, 2, 3, 6, 7):
        gate_copy(i).start()
        dispatch(i).start()

    def turn_inputs():
        wide_row = lax.broadcasted_iota(jnp.int32, (hidden, hidden), 0)
        wide_lane = lax.broadcasted_iota(jnp.int32, (hidden, hidden), 1)
        eye[...] = jnp.where(wide_row == wide_lane, 1.0, 0.0).astype(eye.dtype)

    def turn(q):
        for step in range(7):
            at = slice(q * quarter + step * chunk, q * quarter + (step + 1) * chunk)
            for part_at in (0, hidden):
                gu_t[part_at : part_at + hidden, at] = nt(
                    eye[...], gu_w[at, part_at : part_at + hidden]
                ).astype(gu_t.dtype)

    def turn_down(q):
        for step in range(7):
            at = slice(q * quarter + step * chunk, q * quarter + (step + 1) * chunk)
            down_t[at, :] = nt(eye[...], down_w[:, at]).astype(down_t.dtype)

    def span_of(batch):
        first, last = BATCHES[batch]
        return slice(first * most, last * most)

    def project(batch, others):
        first, last = BATCHES[batch]
        rows = (last - first) * most
        span = span_of(batch)
        for q in (far, diag) if others else (share, near):
            at = pl.ds(pl.multiple_of(q * quarter, 128), quarter)
            x = gath[first:last, q, 0].reshape(rows, quarter)
            dy = gath[first:last, q, 1].reshape(rows, quarter)
            got = jnp.dot(x, gu_w[at, :], preferred_element_type=jnp.float32)
            got_dz = jnp.dot(dy, down_t[at, :], preferred_element_type=jnp.float32)
            if q is share:
                pre_up[span, :] = got
                dz[span, :] = got_dz
            else:
                pre_up[span, :] += got
                dz[span, :] += got_dz

    diagonal = lax.broadcasted_iota(jnp.int32, (most, 128), 0) == lax.broadcasted_iota(
        jnp.int32, (most, 128), 1
    )

    def activate(batch):
        first, last = BATCHES[batch]
        for step in range(first, last):
            if step:
                gate_copied(step).wait_recv()
            at = slice(step * most, (step + 1) * most)
            pre_b, up_b, dz_b = pre_up[at, 0:hidden], pre_up[at, hidden:], dz[at, :]
            sigma = jax.nn.sigmoid(pre_b)
            active = pre_b * sigma
            slot_sum = jnp.sum(active * up_b * dz_b, axis=1, keepdims=True)
            flat = jnp.sum(jnp.where(diagonal, slot_sum, 0.0), axis=0, keepdims=True)
            part[step] = jnp.broadcast_to(flat, (8, 128))
            scaled = g_got[step][:, :1].astype(jnp.float32) * dz_b
            dpdu[at, hidden:] = (scaled * active).astype(dpdu.dtype)
            dpdu[at, 0:hidden] = (
                scaled * up_b * sigma * (1.0 + pre_b * (1.0 - sigma))
            ).astype(dpdu.dtype)
        for which in range(3):
            part_copy(batch, which).start()

    def expand(batch, wanted, store):
        first, last = BATCHES[batch]
        for step in range(7):
            start = wanted * quarter + step * chunk
            at = pl.ds(pl.multiple_of(start, 128), chunk)
            value = jnp.dot(
                dpdu[span_of(batch), :], gu_t[:, at], preferred_element_type=jnp.float32
            )
            store(
                slice(step * chunk, (step + 1) * chunk),
                value.reshape(last - first, most, chunk),
            )

    def give_back(batch, slot):
        first, last = BATCHES[batch]

        def keep(at, value):
            near_put[slot, first:last, :, at] = value.astype(near_put.dtype)

        def keep_wide(at, value):
            mine[slot, first:last, :, at] = value

        expand(batch, (diag, near)[slot], keep)
        half(batch, slot).start()
        expand(batch, (far, share)[slot], keep_wide)

    def cross(batch, steps):
        for step in steps:
            far_put[step] = (mine[0, step] + near_got[0, step].astype(jnp.float32)).astype(
                far_put.dtype
            )
            across(step).start()

    def go_home(step):
        across(step).wait_recv()
        value = mine[1, step] + near_got[1, step].astype(jnp.float32)
        value = (value + far_got[step].astype(jnp.float32)).astype(put.dtype)
        if step:
            put[step] = value
            home(step).start()
        else:
            back[0] = value

    def share_parts(batch):
        first, last = BATCHES[batch]
        for which in range(3):
            part_copy(batch, which).wait_recv()
        for step in range(first, last):
            part_sum[step] = (
                part[step] + part_got[0, step] + part_got[1, step] + part_got[2, step]
            )
            if step:
                grad_home(step).start()
            else:
                part_back[0] = part_sum[0]

    def arrive(step):
        dispatched(step).wait_recv()
        along_far(step).start()
        along_near(step).start()

    def arrive_if(role, step):
        @pl.when(inner == role)
        def _():
            arrive(step)

    def pass_on(step):
        along_far_from(step).wait_recv()
        pass_near(step).start()

    def along_far_from(step):
        block = gath.at[step, far]
        return remote(block, block, to_far, step, (me, far))

    def go_home_if(role, step):
        @pl.when(inner == role)
        def _():
            go_home(step)

    def settle_near(*steps):
        for step in steps:
            block = gath.at[step, near]
            remote(block, block, to_near, step, (me, near)).wait_recv()

    def settle_far(*steps):
        for step in steps:
            block = gath.at[step, diag]
            remote(block, block, passed, step, (me, near)).wait_recv()

    turn_inputs()
    for copy in loads:
        copy.wait()
    for q in range(4):
        turn(q)
    arrive(1)
    pass_on(0)
    for q in range(4):
        turn_down(q)
    arrive(2)
    pass_on(1)
    arrive(3)
    pass_on(2)
    settle_near(0, 1, 2, 3)
    project(0, False)
    arrive(4)
    pass_on(3)
    settle_far(0, 1, 2, 3)
    project(0, True)
    activate(0)
    arrive(5)
    give_back(0, 0)
    pass_on(4)
    half(0, 0).wait_recv()
    cross(0, (2, 3))
    arrive_if(0, 6)
    give_back(0, 1)
    settle_near(4, 5)
    project(1, False)
    pass_on(5)
    settle_far(4, 5)
    project(1, True)
    activate(1)
    give_back(1, 0)
    arrive_if(1, 6)
    half(1, 0).wait_recv()
    cross(1, (4,))
    give_back(1, 1)
    settle_near(6)
    project(2, False)
    arrive_if(1, 7)
    cross(1, (5,))
    arrive_if(0, 7)
    half(0, 1).wait_recv()
    go_home(2)
    go_home(3)
    pass_on(6)
    settle_far(6)
    project(2, True)
    activate(2)
    give_back(2, 0)
    half(2, 0).wait_recv()
    cross(2, (6,))
    give_back(2, 1)
    settle_near(7)
    project(3, False)
    half(1, 1).wait_recv()
    go_home(4)
    go_home_if(0, 5)
    pass_on(7)
    settle_far(7)
    project(3, True)
    activate(3)
    give_back(3, 0)
    half(3, 0).wait_recv()
    cross(3, (7,))
    cross(0, (1, 0))
    share_parts(0)
    share_parts(1)
    share_parts(2)
    go_home_if(1, 5)
    half(2, 1).wait_recv()
    go_home(6)
    give_back(3, 1)
    share_parts(3)
    half(3, 1).wait_recv()
    go_home(7)
    for i in range(n):
        spread_t[:, i * most : (i + 1) * most] = chooser[i].astype(jnp.float32).T.astype(
            spread_t.dtype
        )
    go_home(1)

    ids = ids_ref[...]
    grad_total = jnp.zeros((2, tok_rows), jnp.float32)
    for i in range(n):
        if i:
            grad_came_home(i).wait_recv()
        held = part_back[i][0:1, 0:most]
        hit = chooser[i].astype(jnp.float32)
        value = lax.dot_general(
            held,
            hit,
            (((1,), (0,)), ((), ())),
            precision=lax.Precision.HIGHEST,
            preferred_element_type=jnp.float32,
        )
        grad_total = grad_total + jnp.where(ids == dest(i), value, 0.0)
    gate_out[...] = grad_total
    came_home(4).wait_recv()
    came_home(5).wait_recv()
    came_home(6).wait_recv()
    came_home(7).wait_recv()
    came_home(2).wait_recv()
    came_home(3).wait_recv()
    came_home(1).wait_recv()
    go_home(0)

    @pl.loop(0, 7)
    def _(step):
        at = pl.ds(pl.multiple_of(step * chunk, 128), chunk)
        out[:, at] = jnp.dot(
            spread_t[...],
            back[:, :, at].reshape(n * most, chunk),
            preferred_element_type=jnp.float32,
        ).astype(out.dtype)

    for step in range(n):
        along_far(step).wait_send()
        along_near(step).wait_send()
        pass_near(step).wait_send()
        across(step).wait_send()
        if step:
            dispatch(step).wait_send()
            gate_copy(step).wait_send()
            home(step).wait_send()
            grad_home(step).wait_send()
    for batch in range(len(BATCHES)):
        for slot in range(2):
            half(batch, slot).wait_send()
        for which in range(3):
            part_copy(batch, which).wait_send()


def fused(tokens, out_grad, expert_ids, gate_values, gate_mat, up_mat, down_mat):
    n = lax.axis_size("expert")
    tok_rows, quarter = tokens.shape
    flipped = expert_ids.T
    most = 3 * tok_rows * expert_ids.shape[1] // (2 * n)
    kind = tokens.dtype
    hidden = gate_mat.shape[1]
    rows = n * most
    dma = pltpu.SemaphoreType.DMA
    anywhere = pl.BlockSpec(memory_space=pl.ANY)
    stage = pltpu.VMEM((n, most, quarter), kind)
    pair = pltpu.VMEM((2, n, most, quarter), kind)
    flat = pltpu.VMEM((n, 8, 128), jnp.float32)
    narrow = pltpu.VMEM((n, most, 128), kind)
    d_tokens, d_gates = pl.pallas_call(
        functools.partial(fused_kernel, n, most),
        out_shape=(
            jax.ShapeDtypeStruct(tokens.shape, kind),
            jax.ShapeDtypeStruct(flipped.shape, jnp.float32),
        ),
        in_specs=[VMEM] * 4 + [anywhere] * 3,
        out_specs=[VMEM] * 2,
        scratch_shapes=[
            pltpu.VMEM((n, 2, most, quarter), kind),
            pltpu.VMEM((n, 4, 2, most, quarter), kind),
            narrow,
            narrow,
            pltpu.VMEM((4 * quarter, 2 * hidden), kind),
            pltpu.VMEM(down_mat.shape, kind),
            pltpu.VMEM((n, most, tok_rows), kind),
            pltpu.VMEM((tok_rows, 128), jnp.float32),
            pltpu.VMEM((rows, 2 * hidden), jnp.float32),
            pltpu.VMEM((rows, hidden), jnp.float32),
            pltpu.VMEM((rows, 2 * hidden), kind),
            pair,
            pltpu.VMEM((2, n, most, quarter), jnp.float32),
            pair,
            stage,
            stage,
            stage,
            stage,
            pltpu.VMEM((2 * hidden, 4 * quarter), kind),
            pltpu.VMEM((4 * quarter, hidden), kind),
            pltpu.VMEM((hidden, hidden), kind),
            pltpu.VMEM((tok_rows, n * most), kind),
            flat,
            pltpu.VMEM((3, n, 8, 128), jnp.float32),
            flat,
            flat,
            dma((3,)),
        ]
        + [dma((n,))] * 10
        + [dma((2 * len(BATCHES),))] * 2
        + [dma((n,))] * 6
        + [dma((3 * len(BATCHES),))] * 2,
        compiler_params=pltpu.CompilerParams(
            collective_id=2, has_side_effects=True, vmem_limit_bytes=VMEM_BYTES
        ),
    )(tokens, out_grad, flipped, gate_values.T, gate_mat, up_mat, down_mat)
    return d_tokens, d_gates.T


def in_steps(send_x, send_dy, send_g, gate_mat, up_mat, down_mat):
    n_experts, most_slots, quarter = send_x.shape
    slot_count = n_experts * most_slots
    piece_x, piece_dy, recv_g = spread(
        send_x,
        send_dy,
        send_g.reshape(n_experts, 1, most_slots),
    )
    piece_x = piece_x.reshape(slot_count, 4 * quarter)
    piece_dy = piece_dy.reshape(slot_count, 4 * quarter)
    pre_sum = jnp.dot(piece_x, gate_mat, preferred_element_type=jnp.float32)
    up_sum = jnp.dot(piece_x, up_mat, preferred_element_type=jnp.float32)
    grad_sum = lax.dot_general(
        piece_dy, down_mat, (((1,), (1,)), ((), ())), preferred_element_type=jnp.float32
    )
    sigma = jax.nn.sigmoid(pre_sum)
    active = pre_sum * sigma
    partial_grad = jnp.sum(active * up_sum * grad_sum, axis=1)
    weight_g = recv_g.reshape(slot_count)
    scaled = weight_g[:, None] * grad_sum
    grad_up = (scaled * active).astype(jnp.bfloat16)
    grad_pre = (scaled * up_sum * sigma * (1.0 + pre_sum * (1.0 - sigma))).astype(jnp.bfloat16)
    contrib = lax.dot_general(
        grad_pre, gate_mat, (((1,), (1,)), ((), ())), preferred_element_type=jnp.float32
    )
    contrib = contrib + lax.dot_general(
        grad_up, up_mat, (((1,), (1,)), ((), ())), preferred_element_type=jnp.float32
    )
    returned, returned_grad = collect(
        contrib.astype(jnp.bfloat16).reshape(n_experts, most_slots, 4 * quarter),
        partial_grad.reshape(n_experts, 1, most_slots),
    )
    return returned, returned_grad


def local(tokens, out_grad, expert_ids, gate_values, w_gate, w_up, w_down):
    n_experts = lax.axis_size("expert")
    shares = lax.axis_size("tensor")
    tok_rows, quarter = tokens.shape
    top_count = expert_ids.shape[1]
    most_slots = 3 * tok_rows * top_count // (2 * n_experts)
    slot_count = n_experts * most_slots
    weights = (w_gate[0], w_up[0], w_down[0])
    fits = most_slots == 48 and tok_rows == 128 and top_count == 2 and quarter == 1792
    if fits and n_experts == 8 and shares == 4 and w_gate.shape[2] == 256:
        return fused(tokens, out_grad, expert_ids, gate_values, *weights)
    flat_ids = expert_ids.reshape(-1)
    onehot = flat_ids[:, None] == jnp.arange(n_experts, dtype=jnp.int32)[None, :]
    earlier = jnp.tri(flat_ids.shape[0], k=-1, dtype=jnp.bfloat16)
    before = jnp.dot(earlier, onehot.astype(jnp.bfloat16), preferred_element_type=jnp.float32)
    rank = jnp.sum(jnp.where(onehot, before, 0.0), axis=1).astype(jnp.int32)
    slot_of = (flat_ids * most_slots + rank).reshape(tok_rows, top_count)
    matches = slot_of[None, :, :] == jnp.arange(slot_count, dtype=jnp.int32)[:, None, None]
    chooser = jnp.any(matches, axis=2).astype(jnp.bfloat16)
    send_x = jnp.dot(chooser, tokens, preferred_element_type=jnp.float32).astype(jnp.bfloat16)
    send_dy = jnp.dot(chooser, out_grad, preferred_element_type=jnp.float32).astype(jnp.bfloat16)
    gate_wide = gate_values.astype(jnp.float32)[None, :, :]
    send_g = jnp.sum(jnp.where(matches, gate_wide, 0.0), axis=(1, 2))
    send_x = send_x.reshape(n_experts, most_slots, quarter)
    send_dy = send_dy.reshape(n_experts, most_slots, quarter)
    returned, returned_grad = in_steps(send_x, send_dy, send_g, *weights)
    d_tokens = lax.dot_general(
        chooser,
        returned.reshape(slot_count, quarter),
        (((0,), (0,)), ((), ())),
        preferred_element_type=jnp.float32,
    ).astype(jnp.bfloat16)
    grad_wide = returned_grad.reshape(slot_count)[:, None, None]
    d_gates = jnp.sum(jnp.where(matches, grad_wide, 0.0), axis=0)
    return (d_tokens, d_gates)


def solution(mesh):
    placed = (
        P("expert", "tensor"),
        P("expert", "tensor"),
        P("expert", None),
        P("expert", None),
        P("expert", None, "tensor"),
        P("expert", None, "tensor"),
        P("expert", "tensor", None),
    )
    return jax.shard_map(
        local,
        mesh=mesh,
        in_specs=placed,
        out_specs=(P("expert", "tensor"), P("expert", None)),
        check_vma=False,
    )
```

```python
import functools

import jax
import jax.numpy as jnp
from jax import lax
from jax.experimental import pallas as pl
from jax.experimental.pallas import tpu as pltpu
from jax.sharding import PartitionSpec as P


MESH = pl.DeviceIdType.MESH
VMEM = pl.BlockSpec(memory_space=pltpu.VMEM)
VMEM_BYTES = 56 * 1024 * 1024


def positions(n):
    me = lax.axis_index("expert")
    share = lax.axis_index("tensor")
    pair, side = share // 2, share % 2
    return me, share, pair * 2 + 1 - side, (1 - pair) * 2 + side


def greet(n, me, share, near, far):
    barrier = pltpu.get_barrier_semaphore()

    @pl.loop(1, n)
    def _(step):
        pl.semaphore_signal(
            barrier, inc=1, device_id=(lax.rem(me + step, n), share), device_id_type=MESH
        )

    for peer in (near, far):
        pl.semaphore_signal(barrier, inc=1, device_id=(me, peer), device_id_type=MESH)
    pl.semaphore_wait(barrier, n + 1)


def remote(src, dst, sems, index, device):
    return pltpu.make_async_remote_copy(
        src_ref=src,
        dst_ref=dst,
        send_sem=sems[0].at[index],
        recv_sem=sems[1].at[index],
        device_id=device,
        device_id_type=MESH,
    )


def spread_kernel(n, x_ref, dy_ref, g_ref, x_out, dy_out, g_out, *sems):
    me, share, near, far = positions(n)
    quarter = x_ref.shape[2]
    by_group, to_near, to_far, passed, gates = (sems[2 * i : 2 * i + 2] for i in range(5))
    own = sems[10]
    pairs = ((x_ref, x_out), (dy_ref, dy_out))

    def cols(which):
        return pl.ds(pl.multiple_of(which * quarter, 128), quarter)

    def block(which, group, owner):
        return pairs[which][1].at[group, :, cols(owner)]

    def dispatch(which, source, target):
        return remote(
            pairs[which][0].at[target],
            block(which, source, share),
            by_group,
            which * n + source,
            (target, share),
        )

    def gate_copy(source, target):
        return remote(
            g_ref.at[target], g_out.at[source], gates, source, (target, share)
        )

    def along(which, group, sent, sems_of, peer):
        return remote(
            block(which, group, sent),
            block(which, group, sent),
            sems_of,
            which * n + group,
            (me, peer),
        )

    greet(n, me, share, near, far)
    own_copies = [
        pltpu.make_async_copy(src.at[me], block(which, me, share), own.at[which])
        for which, (src, _) in enumerate(pairs)
    ]
    own_copies.append(pltpu.make_async_copy(g_ref.at[me], g_out.at[me], own.at[2]))
    for copy in own_copies:
        copy.start()
    for which in range(2):

        @pl.loop(1, n)
        def _(step):
            target = lax.rem(me + step, n)
            dispatch(which, me, target).start()

    @pl.loop(1, n)
    def _(step):
        gate_copy(me, lax.rem(me + step, n)).start()

    for copy in own_copies:
        copy.wait()

    def share_out(which, group):
        along(which, group, share, to_far, far).start()
        along(which, group, share, to_near, near).start()

    def pass_on(which, group):
        along(which, group, far, to_far, far).wait_recv()
        along(which, group, far, passed, near).start()

    for which in range(2):
        share_out(which, me)

        @pl.loop(1, n)
        def _(step):
            group = lax.rem(me - step + n, n)
            dispatch(which, group, me).wait_recv()
            share_out(which, group)
            pass_on(which, lax.rem(me - step + 1 + n, n))

        pass_on(which, lax.rem(me + 1, n))
    for which in range(2):

        @pl.loop(0, n)
        def _(group):
            along(which, group, near, to_near, near).wait_recv()
            along(which, group, 3 - share, passed, near).wait_recv()
            along(which, group, share, to_far, far).wait_send()
            along(which, group, share, to_near, near).wait_send()
            along(which, group, far, passed, near).wait_send()

        @pl.loop(1, n)
        def _(step):
            dispatch(which, me, lax.rem(me + step, n)).wait_send()

    @pl.loop(1, n)
    def _(step):
        gate_copy(me, lax.rem(me + step, n)).wait_send()
        gate_copy(lax.rem(me - step + n, n), me).wait_recv()


def spread(send_x, send_dy, send_g):
    n, most, quarter = send_x.shape
    wide = jax.ShapeDtypeStruct((n, most, 4 * quarter), send_x.dtype)
    dma = pltpu.SemaphoreType.DMA
    return pl.pallas_call(
        functools.partial(spread_kernel, n),
        out_shape=(wide, wide, jax.ShapeDtypeStruct(send_g.shape, send_g.dtype)),
        in_specs=[VMEM] * 3,
        out_specs=[VMEM] * 3,
        scratch_shapes=[dma((2 * n,))] * 8 + [dma((n,)), dma((n,)), dma((3,))],
        compiler_params=pltpu.CompilerParams(
            collective_id=0, has_side_effects=True, vmem_limit_bytes=VMEM_BYTES
        ),
    )(send_x, send_dy, send_g)


def collect_kernel(n, c_ref, p_ref, out, grad_out, near_got, far_put, far_got, put, total,
                   part_got, part_sum, *sems):
    me, share, near, far = positions(n)
    quarter = out.shape[2]
    to_near, to_far, back, grads, parts = (sems[2 * i : 2 * i + 2] for i in range(5))
    own = sems[10]

    def cols(which):
        return pl.ds(pl.multiple_of(which * quarter, 128), quarter)

    def half(group, slot):
        wanted = near if slot == 1 else 3 - share
        return remote(
            c_ref.at[group, :, cols(wanted)],
            near_got.at[group, slot],
            to_near,
            group * 2 + slot,
            (me, near),
        )

    def across(group):
        return remote(far_put.at[group], far_got.at[group], to_far, group, (me, far))

    def home(source, target):
        return remote(put.at[target], out.at[source], back, source, (target, share))

    def grad_home(source, target):
        return remote(
            part_sum.at[target], grad_out.at[source], grads, source, (target, share)
        )

    greet(n, me, share, near, far)
    part_near = remote(p_ref, part_got.at[0], parts, 0, (me, near))
    part_near.start()

    @pl.loop(0, n)
    def _(step):
        group = lax.rem(me + 1 + step, n)
        half(group, 0).start()
        half(group, 1).start()

    part_near.wait()
    part_sum[...] = p_ref[...] + part_got[0]
    part_far = remote(part_sum, part_got.at[1], parts, 1, (me, far))
    part_far.start()
    part_far.wait()
    part_sum[...] = part_sum[...] + part_got[1]

    @pl.loop(1, n)
    def _(step):
        grad_home(me, lax.rem(me + step, n)).start()

    def pair_sum(group):
        half(group, 0).wait_recv()
        mine = c_ref[group, :, cols(far)].astype(jnp.float32)
        far_put[group] = (mine + near_got[group, 0].astype(jnp.float32)).astype(far_put.dtype)
        across(group).start()
        half(group, 1).wait_recv()
        mine = c_ref[group, :, cols(share)].astype(jnp.float32)
        total[group] = mine + near_got[group, 1].astype(jnp.float32)

    def full_sum(group):
        across(group).wait_recv()
        put[group] = (total[group] + far_got[group].astype(jnp.float32)).astype(put.dtype)

    def send_home(group):
        full_sum(group)
        home(me, group).start()

    pair_sum(lax.rem(me + 1, n))

    @pl.loop(2, n + 1)
    def _(step):
        pair_sum(lax.rem(me + step, n))
        send_home(lax.rem(me + step - 1, n))

    full_sum(me)
    own_copies = [
        pltpu.make_async_copy(put.at[me], out.at[me], own.at[0]),
        pltpu.make_async_copy(part_sum.at[me], grad_out.at[me], own.at[1]),
    ]
    for copy in own_copies:
        copy.start()
    for copy in own_copies:
        copy.wait()

    @pl.loop(0, n)
    def _(group):
        half(group, 0).wait_send()
        half(group, 1).wait_send()
        across(group).wait_send()

    @pl.loop(1, n)
    def _(step):
        target = lax.rem(me + step, n)
        source = lax.rem(me - step + n, n)
        home(me, target).wait_send()
        grad_home(me, target).wait_send()
        home(source, me).wait_recv()
        grad_home(source, me).wait_recv()


def collect(contrib, partial_grad):
    n, most, width = contrib.shape
    quarter = width // 4
    kind = contrib.dtype
    dma = pltpu.SemaphoreType.DMA
    stage = pltpu.VMEM((n, most, quarter), kind)
    return pl.pallas_call(
        functools.partial(collect_kernel, n),
        out_shape=(
            jax.ShapeDtypeStruct((n, most, quarter), kind),
            jax.ShapeDtypeStruct(partial_grad.shape, partial_grad.dtype),
        ),
        in_specs=[VMEM] * 2,
        out_specs=[VMEM] * 2,
        scratch_shapes=[
            pltpu.VMEM((n, 2, most, quarter), kind),
            stage,
            stage,
            stage,
            pltpu.VMEM((n, most, quarter), jnp.float32),
            pltpu.VMEM((2,) + partial_grad.shape, jnp.float32),
            pltpu.VMEM(partial_grad.shape, jnp.float32),
            dma((2 * n,)),
            dma((2 * n,)),
        ]
        + [dma((n,))] * 6
        + [dma((2,)), dma((2,)), dma((2,))],
        compiler_params=pltpu.CompilerParams(
            collective_id=1, has_side_effects=True, vmem_limit_bytes=VMEM_BYTES
        ),
    )(contrib, partial_grad)


BATCHES = ((0, 4), (4, 6), (6, 7), (7, 8))


def fused_kernel(n, most, tok_ref, grad_ref, ids_ref, gv_ref, gate_hbm, up_hbm, down_hbm,
                 out, gate_out, send, gath, g_put, g_got, gu_w, down_w, chooser, code, pre_up,
                 dz, dpdu, near_put, mine, near_got, far_put, far_got, put, back, back_far, token_put, token_got, gu_t, down_t,
                 eye, spread_t, part, part_got, part_sum, part_back, load, *sems):
    me, share, near, far = positions(n)
    diag = 3 - share
    quarter = tok_ref.shape[1]
    tok_rows = tok_ref.shape[0]
    hidden = down_w.shape[0]
    chunk = quarter // 7
    (by_group, gates, to_far, to_near, passed, halves, over, back_sems, grads, far_back, parts,
     summed) = (sems[2 * i : 2 * i + 2] for i in range(12))

    inner = lax.rem((me // 2 + 1) // 2, 2)

    def dest(i):
        at = me
        for bit in (1, 2, 4):
            if i & bit:
                at = at + bit * (1 - 2 * lax.rem(me // bit, 2))
        return at

    def place(i):
        return {2: 4 - 2 * inner, 3: 5 - 2 * inner, 4: 2 + 2 * inner, 5: 3 + 2 * inner}.get(i, i)

    def origin(p):
        return {2: 2 + 2 * inner, 3: 3 + 2 * inner, 4: 4 - 2 * inner, 5: 5 - 2 * inner}.get(p, p)

    def source(p):
        if p in (2, 3, 4, 5):
            other = p + 2 if p < 4 else p - 2
            return dest(p) * (1 - inner) + dest(other) * inner
        return dest(p)

    def nt(left, right):
        return lax.dot_general(
            left, right, (((1,), (1,)), ((), ())), preferred_element_type=jnp.float32
        )

    def remote_to(src, dst, sems_of, sent, landed, device):
        return pltpu.make_async_remote_copy(
            src_ref=src,
            dst_ref=dst,
            send_sem=sems_of[0].at[sent],
            recv_sem=sems_of[1].at[landed],
            device_id=(device, share),
            device_id_type=MESH,
        )

    def dispatch(i):
        p = place(i)
        return remote_to(send.at[i], gath.at[p, share], by_group, i, p, dest(i))

    def dispatched(p):
        block = gath.at[p, share]
        return remote_to(block, block, by_group, p, p, source(p))

    def gate_copy(i):
        p = place(i)
        return remote_to(g_put.at[i], g_got.at[p], gates, i, p, dest(i))

    def gate_copied(p):
        return remote_to(g_got.at[p], g_got.at[p], gates, p, p, source(p))

    def along_far(step):
        block = gath.at[step, share]
        return remote(block, block, to_far, step, (me, far))

    def along_near(step):
        block = gath.at[step, share]
        return remote(block, block, to_near, step, (me, near))

    def pass_near(step):
        block = gath.at[step, far]
        return remote(block, block, passed, step, (me, near))

    def half(batch, slot):
        first, last = BATCHES[batch]
        span = pl.ds(first, last - first)
        return remote(
            near_put.at[slot, span], near_got.at[slot, span], halves, batch * 2 + slot, (me, near)
        )

    def across(step):
        return remote(far_put.at[step], far_got.at[step], over, step, (me, far))

    def home(p):
        i = origin(p)
        return remote_to(put.at[p], back.at[i], back_sems, p, i, source(p))

    def far_home(p):
        i = origin(p)
        return remote_to(far_put.at[p], back_far.at[i], far_back, p, i, source(p))

    def far_came_home(i):
        return remote_to(back_far.at[i], back_far.at[i], far_back, i, i, dest(i))

    def token_part(i):
        span = pl.ds(i * tok_rows // 4, tok_rows // 4)
        return remote(token_put.at[span], token_got.at[span], summed, i, (me, far))

    def came_home(i):
        return remote_to(back.at[i], back.at[i], back_sems, i, i, dest(i))

    def grad_home(p):
        i = origin(p)
        return remote_to(part_sum.at[p], part_back.at[i], grads, p, i, source(p))

    def grad_came_home(i):
        return remote_to(part_back.at[i], part_back.at[i], grads, i, i, dest(i))

    def part_copy(batch, which):
        first, last = BATCHES[batch]
        span = pl.ds(first, last - first)
        peer = (near, far, diag)[which]
        return remote(
            part.at[span], part_got.at[which, span], parts, batch * 3 + which, (me, peer)
        )

    loads = [
        pltpu.make_async_copy(gate_hbm, gu_w.at[:, pl.ds(0, hidden)], load.at[0]),
        pltpu.make_async_copy(up_hbm, gu_w.at[:, pl.ds(hidden, hidden)], load.at[1]),
        pltpu.make_async_copy(down_hbm, down_w, load.at[2]),
    ]
    for copy in loads:
        copy.start()
    barrier = pltpu.get_barrier_semaphore()
    for step in range(1, n):
        pl.semaphore_signal(barrier, inc=1, device_id=(dest(step), share), device_id_type=MESH)
    for peer in (near, far, diag):
        pl.semaphore_signal(barrier, inc=1, device_id=(me, peer), device_id_type=MESH)

    lane = lax.broadcasted_iota(jnp.int32, (tok_rows, 128), 1)
    row = lax.broadcasted_iota(jnp.int32, (tok_rows, 128), 0)
    ids = ids_ref[...]
    gv = gv_ref[...].astype(jnp.float32)
    first_named, second_named = row == ids[0:1, :], row == ids[1:2, :]
    named = jnp.where(first_named | second_named, 1.0, 0.0)
    earlier = jnp.where(row < lane, 1.0, 0.0).astype(jnp.bfloat16)
    rank = jnp.dot(named.astype(jnp.bfloat16), earlier, preferred_element_type=jnp.float32)
    codes = jnp.where(named > 0.5, rank, -1.0)
    code[...] = codes
    weight_t = jnp.where(first_named, gv[0:1, :], 0.0) + jnp.where(second_named, gv[1:2, :], 0.0)
    slot_row = lax.broadcasted_iota(jnp.int32, (most, tok_rows), 0).astype(jnp.float32)

    def code_of(i):
        return jnp.sum(jnp.where(row == dest(i), code[...], 0.0), axis=0, keepdims=True)

    def choose(i):
        its_weight = jnp.sum(jnp.where(row == dest(i), weight_t, 0.0), axis=0, keepdims=True)
        hit = jnp.where(slot_row == code_of(i), 1.0, 0.0)
        chooser[i] = hit.astype(chooser.dtype)
        slot_weight = jnp.sum(hit * its_weight, axis=1, keepdims=True)
        g_put[i] = jnp.broadcast_to(slot_weight, (most, 128)).astype(g_put.dtype)

    def pick(step, which):
        rows_of = (tok_ref, grad_ref)[which]
        return jnp.dot(
            chooser[step], rows_of[...], preferred_element_type=jnp.float32
        ).astype(send.dtype)

    for i in range(n):
        choose(i)
        for which in range(2):
            if i:
                send[i, which] = pick(i, which)
            else:
                gath[0, share, which] = pick(0, which)
    g_got[0] = g_put[0]
    pl.semaphore_wait(barrier, n + 2)
    along_far(0).start()
    along_near(0).start()
    for i in (4, 1, 5, 2, 3, 6, 7):
        gate_copy(i).start()
        dispatch(i).start()

    def turn_inputs():
        wide_row = lax.broadcasted_iota(jnp.int32, (hidden, hidden), 0)
        wide_lane = lax.broadcasted_iota(jnp.int32, (hidden, hidden), 1)
        eye[...] = jnp.where(wide_row == wide_lane, 1.0, 0.0).astype(eye.dtype)

    def turn(q):
        for step in range(7):
            at = slice(q * quarter + step * chunk, q * quarter + (step + 1) * chunk)
            for part_at in (0, hidden):
                gu_t[part_at : part_at + hidden, at] = nt(
                    eye[...], gu_w[at, part_at : part_at + hidden]
                ).astype(gu_t.dtype)

    def turn_down(q):
        for step in range(7):
            at = slice(q * quarter + step * chunk, q * quarter + (step + 1) * chunk)
            down_t[at, :] = nt(eye[...], down_w[:, at]).astype(down_t.dtype)

    def span_of(batch):
        first, last = BATCHES[batch]
        return slice(first * most, last * most)

    def project(batch, others):
        first, last = BATCHES[batch]
        rows = (last - first) * most
        span = span_of(batch)
        for q in (far, diag) if others else (share, near):
            at = pl.ds(pl.multiple_of(q * quarter, 128), quarter)
            x = gath[first:last, q, 0].reshape(rows, quarter)
            dy = gath[first:last, q, 1].reshape(rows, quarter)
            got = jnp.dot(x, gu_w[at, :], preferred_element_type=jnp.float32)
            got_dz = jnp.dot(dy, down_t[at, :], preferred_element_type=jnp.float32)
            if q is share:
                pre_up[span, :] = got
                dz[span, :] = got_dz
            else:
                pre_up[span, :] += got
                dz[span, :] += got_dz

    diagonal = lax.broadcasted_iota(jnp.int32, (most, 128), 0) == lax.broadcasted_iota(
        jnp.int32, (most, 128), 1
    )

    def activate(batch):
        first, last = BATCHES[batch]
        for step in range(first, last):
            if step:
                gate_copied(step).wait_recv()
            at = slice(step * most, (step + 1) * most)
            pre_b, up_b, dz_b = pre_up[at, 0:hidden], pre_up[at, hidden:], dz[at, :]
            sigma = jax.nn.sigmoid(pre_b)
            active = pre_b * sigma
            slot_sum = jnp.sum(active * up_b * dz_b, axis=1, keepdims=True)
            flat = jnp.sum(jnp.where(diagonal, slot_sum, 0.0), axis=0, keepdims=True)
            part[step] = jnp.broadcast_to(flat, (8, 128))
            scaled = g_got[step][:, :1].astype(jnp.float32) * dz_b
            dpdu[at, hidden:] = (scaled * active).astype(dpdu.dtype)
            dpdu[at, 0:hidden] = (
                scaled * up_b * sigma * (1.0 + pre_b * (1.0 - sigma))
            ).astype(dpdu.dtype)
        for which in range(3):
            part_copy(batch, which).start()

    def expand(batch, wanted, store):
        first, last = BATCHES[batch]
        for step in range(7):
            start = wanted * quarter + step * chunk
            at = pl.ds(pl.multiple_of(start, 128), chunk)
            value = jnp.dot(
                dpdu[span_of(batch), :], gu_t[:, at], preferred_element_type=jnp.float32
            )
            store(
                slice(step * chunk, (step + 1) * chunk),
                value.reshape(last - first, most, chunk),
            )

    def give_back(batch, slot):
        first, last = BATCHES[batch]

        def keep(at, value):
            near_put[slot, first:last, :, at] = value.astype(near_put.dtype)

        def keep_wide(at, value):
            mine[slot, first:last, :, at] = value

        expand(batch, (diag, near)[slot], keep)
        half(batch, slot).start()
        expand(batch, (far, share)[slot], keep_wide)

    def crossing_sum(p):
        return (mine[0, p] + near_got[0, p].astype(jnp.float32)).astype(far_put.dtype)

    def staying_sum(p):
        return mine[1, p] + near_got[1, p].astype(jnp.float32)

    def cross(*steps):
        for p in steps:
            far_put[p] = crossing_sum(p)
            across(p).start()

    def go_home(p):
        across(p).wait_recv()
        put[p] = (staying_sum(p) + far_got[p].astype(jnp.float32)).astype(put.dtype)
        home(p).start()

    def both_go_home(*steps):
        for p in steps:
            if p:
                far_put[p] = crossing_sum(p)
                put[p] = staying_sum(p).astype(put.dtype)
                far_home(p).start()
                home(p).start()
            else:
                back_far[0] = crossing_sum(0)
                back[0] = staying_sum(0).astype(back.dtype)

    def sum_tokens():
        for i in range(1, 4):
            far_came_home(i).wait_recv()
        rows = 4 * most
        for step in range(7):
            at = slice(step * chunk, (step + 1) * chunk)
            token_put[:, at] = jnp.dot(
                spread_t[:, 0:rows],
                back_far[:, :, at].reshape(rows, chunk),
                preferred_element_type=jnp.float32,
            ).astype(token_put.dtype)

    def token_go(i):
        token_part(i).start()

    def when(role, act, *steps):
        @pl.when(inner == role)
        def _():
            if not steps:
                act()
            for p in steps:
                act(p)

    def share_parts(batch):
        first, last = BATCHES[batch]
        for which in range(3):
            part_copy(batch, which).wait_recv()
        for step in range(first, last):
            part_sum[step] = (
                part[step] + part_got[0, step] + part_got[1, step] + part_got[2, step]
            )
            if step:
                grad_home(step).start()
            else:
                part_back[0] = part_sum[0]

    def arrive(step):
        dispatched(step).wait_recv()
        along_far(step).start()
        along_near(step).start()

    def pass_on(step):
        along_far_from(step).wait_recv()
        pass_near(step).start()

    def along_far_from(step):
        block = gath.at[step, far]
        return remote(block, block, to_far, step, (me, far))

    def settle_near(*steps):
        for step in steps:
            block = gath.at[step, near]
            remote(block, block, to_near, step, (me, near)).wait_recv()

    def settle_far(*steps):
        for step in steps:
            block = gath.at[step, diag]
            remote(block, block, passed, step, (me, near)).wait_recv()

    turn_inputs()
    for copy in loads:
        copy.wait()
    for q in range(4):
        turn(q)
    arrive(1)
    pass_on(0)
    for q in range(4):
        turn_down(q)
    for i in range(n):
        spread_t[:, i * most : (i + 1) * most] = chooser[i].astype(jnp.float32).T.astype(
            spread_t.dtype
        )
    arrive(2)
    pass_on(1)
    arrive(3)
    pass_on(2)
    settle_near(0, 1, 2, 3)
    project(0, False)
    arrive(4)
    pass_on(3)
    settle_far(0, 1, 2, 3)
    project(0, True)
    activate(0)
    arrive(5)
    give_back(0, 0)
    pass_on(4)
    half(0, 0).wait_recv()
    when(1, cross, 2, 3)
    when(0, arrive, 6)
    give_back(0, 1)
    settle_near(4, 5)
    project(1, False)
    half(0, 1).wait_recv()
    both_go_home(0)
    pass_on(5)
    settle_far(4, 5)
    project(1, True)
    activate(1)
    give_back(1, 0)
    when(1, arrive, 6)
    half(1, 0).wait_recv()
    when(0, cross, 4, 5)
    give_back(1, 1)
    settle_near(6)
    project(2, False)
    half(1, 1).wait_recv()
    when(1, both_go_home, 4, 5)
    when(0, arrive, 7)
    when(0, both_go_home, 2, 3, 1)
    pass_on(6)
    when(1, arrive, 7)
    when(1, go_home, 2, 3)
    when(1, both_go_home, 1)
    settle_far(6)
    project(2, True)
    activate(2)
    give_back(2, 0)
    half(2, 0).wait_recv()
    cross(6)
    give_back(2, 1)
    settle_near(7)
    project(3, False)
    pass_on(7)
    when(0, go_home, 4, 5)
    settle_far(7)
    project(3, True)
    activate(3)
    give_back(3, 0)
    half(3, 0).wait_recv()
    cross(7)
    when(1, sum_tokens)
    when(1, token_go, 0, 1, 2, 3)
    share_parts(0)
    share_parts(1)
    share_parts(2)
    half(2, 1).wait_recv()
    go_home(6)
    give_back(3, 1)
    share_parts(3)
    half(3, 1).wait_recv()
    go_home(7)
    when(0, sum_tokens)
    when(0, token_go, 0, 1, 2, 3)
    ids = ids_ref[...]
    grad_total = jnp.zeros((2, tok_rows), jnp.float32)
    for i in range(n):
        if i:
            grad_came_home(i).wait_recv()
        held = part_back[i][0:1, 0:most]
        hit = chooser[i].astype(jnp.float32)
        value = lax.dot_general(
            held,
            hit,
            (((1,), (0,)), ((), ())),
            precision=lax.Precision.HIGHEST,
            preferred_element_type=jnp.float32,
        )
        grad_total = grad_total + jnp.where(ids == dest(i), value, 0.0)
    gate_out[...] = grad_total
    came_home(1).wait_recv()
    came_home(2).wait_recv()
    came_home(3).wait_recv()
    came_home(4).wait_recv()
    came_home(5).wait_recv()
    came_home(6).wait_recv()
    token_part(0).wait_recv()
    token_part(1).wait_recv()
    token_part(2).wait_recv()
    token_part(3).wait_recv()
    came_home(7).wait_recv()
    for step in range(7):
        at = slice(step * chunk, (step + 1) * chunk)
        total = jnp.dot(
            spread_t[...],
            back[:, :, at].reshape(n * most, chunk),
            preferred_element_type=jnp.float32,
        )
        out[:, at] = (total + token_got[:, at].astype(jnp.float32)).astype(out.dtype)

    def far_sent(p):
        far_home(p).wait_send()

    def across_sent(p):
        across(p).wait_send()

    far_sent(1)
    when(0, far_sent, 2, 3)
    when(1, far_sent, 4, 5)
    when(1, across_sent, 2, 3)
    when(0, across_sent, 4, 5)
    across_sent(6)
    across_sent(7)
    for i in range(4):
        token_part(i).wait_send()
    for step in range(n):
        along_far(step).wait_send()
        along_near(step).wait_send()
        pass_near(step).wait_send()
        if step:
            dispatch(step).wait_send()
            gate_copy(step).wait_send()
            home(step).wait_send()
            grad_home(step).wait_send()
    for batch in range(len(BATCHES)):
        for slot in range(2):
            half(batch, slot).wait_send()
        for which in range(3):
            part_copy(batch, which).wait_send()


def fused(tokens, out_grad, expert_ids, gate_values, gate_mat, up_mat, down_mat):
    n = lax.axis_size("expert")
    tok_rows, quarter = tokens.shape
    flipped = expert_ids.T
    most = 3 * tok_rows * expert_ids.shape[1] // (2 * n)
    kind = tokens.dtype
    hidden = gate_mat.shape[1]
    rows = n * most
    dma = pltpu.SemaphoreType.DMA
    anywhere = pl.BlockSpec(memory_space=pl.ANY)
    stage = pltpu.VMEM((n, most, quarter), kind)
    pair = pltpu.VMEM((2, n, most, quarter), kind)
    flat = pltpu.VMEM((n, 8, 128), jnp.float32)
    narrow = pltpu.VMEM((n, most, 128), kind)
    d_tokens, d_gates = pl.pallas_call(
        functools.partial(fused_kernel, n, most),
        out_shape=(
            jax.ShapeDtypeStruct(tokens.shape, kind),
            jax.ShapeDtypeStruct(flipped.shape, jnp.float32),
        ),
        in_specs=[VMEM] * 4 + [anywhere] * 3,
        out_specs=[VMEM] * 2,
        scratch_shapes=[
            pltpu.VMEM((n, 2, most, quarter), kind),
            pltpu.VMEM((n, 4, 2, most, quarter), kind),
            narrow,
            narrow,
            pltpu.VMEM((4 * quarter, 2 * hidden), kind),
            pltpu.VMEM(down_mat.shape, kind),
            pltpu.VMEM((n, most, tok_rows), kind),
            pltpu.VMEM((tok_rows, 128), jnp.float32),
            pltpu.VMEM((rows, 2 * hidden), jnp.float32),
            pltpu.VMEM((rows, hidden), jnp.float32),
            pltpu.VMEM((rows, 2 * hidden), kind),
            pair,
            pltpu.VMEM((2, n, most, quarter), jnp.float32),
            pair,
            stage,
            stage,
            stage,
            stage,
            pltpu.VMEM((4, most, quarter), kind),
            pltpu.VMEM(tokens.shape, kind),
            pltpu.VMEM(tokens.shape, kind),
            pltpu.VMEM((2 * hidden, 4 * quarter), kind),
            pltpu.VMEM((4 * quarter, hidden), kind),
            pltpu.VMEM((hidden, hidden), kind),
            pltpu.VMEM((tok_rows, n * most), kind),
            flat,
            pltpu.VMEM((3, n, 8, 128), jnp.float32),
            flat,
            flat,
            dma((3,)),
        ]
        + [dma((n,))] * 10
        + [dma((2 * len(BATCHES),))] * 2
        + [dma((n,))] * 8
        + [dma((3 * len(BATCHES),))] * 2
        + [dma((4,))] * 2,
        compiler_params=pltpu.CompilerParams(
            collective_id=2, has_side_effects=True, vmem_limit_bytes=VMEM_BYTES
        ),
    )(tokens, out_grad, flipped, gate_values.T, gate_mat, up_mat, down_mat)
    return d_tokens, d_gates.T


def in_steps(send_x, send_dy, send_g, gate_mat, up_mat, down_mat):
    n_experts, most_slots, quarter = send_x.shape
    slot_count = n_experts * most_slots
    piece_x, piece_dy, recv_g = spread(
        send_x,
        send_dy,
        send_g.reshape(n_experts, 1, most_slots),
    )
    piece_x = piece_x.reshape(slot_count, 4 * quarter)
    piece_dy = piece_dy.reshape(slot_count, 4 * quarter)
    pre_sum = jnp.dot(piece_x, gate_mat, preferred_element_type=jnp.float32)
    up_sum = jnp.dot(piece_x, up_mat, preferred_element_type=jnp.float32)
    grad_sum = lax.dot_general(
        piece_dy, down_mat, (((1,), (1,)), ((), ())), preferred_element_type=jnp.float32
    )
    sigma = jax.nn.sigmoid(pre_sum)
    active = pre_sum * sigma
    partial_grad = jnp.sum(active * up_sum * grad_sum, axis=1)
    weight_g = recv_g.reshape(slot_count)
    scaled = weight_g[:, None] * grad_sum
    grad_up = (scaled * active).astype(jnp.bfloat16)
    grad_pre = (scaled * up_sum * sigma * (1.0 + pre_sum * (1.0 - sigma))).astype(jnp.bfloat16)
    contrib = lax.dot_general(
        grad_pre, gate_mat, (((1,), (1,)), ((), ())), preferred_element_type=jnp.float32
    )
    contrib = contrib + lax.dot_general(
        grad_up, up_mat, (((1,), (1,)), ((), ())), preferred_element_type=jnp.float32
    )
    returned, returned_grad = collect(
        contrib.astype(jnp.bfloat16).reshape(n_experts, most_slots, 4 * quarter),
        partial_grad.reshape(n_experts, 1, most_slots),
    )
    return returned, returned_grad


def local(tokens, out_grad, expert_ids, gate_values, w_gate, w_up, w_down):
    n_experts = lax.axis_size("expert")
    shares = lax.axis_size("tensor")
    tok_rows, quarter = tokens.shape
    top_count = expert_ids.shape[1]
    most_slots = 3 * tok_rows * top_count // (2 * n_experts)
    slot_count = n_experts * most_slots
    weights = (w_gate[0], w_up[0], w_down[0])
    fits = most_slots == 48 and tok_rows == 128 and top_count == 2 and quarter == 1792
    if fits and n_experts == 8 and shares == 4 and w_gate.shape[2] == 256:
        return fused(tokens, out_grad, expert_ids, gate_values, *weights)
    flat_ids = expert_ids.reshape(-1)
    onehot = flat_ids[:, None] == jnp.arange(n_experts, dtype=jnp.int32)[None, :]
    earlier = jnp.tri(flat_ids.shape[0], k=-1, dtype=jnp.bfloat16)
    before = jnp.dot(earlier, onehot.astype(jnp.bfloat16), preferred_element_type=jnp.float32)
    rank = jnp.sum(jnp.where(onehot, before, 0.0), axis=1).astype(jnp.int32)
    slot_of = (flat_ids * most_slots + rank).reshape(tok_rows, top_count)
    matches = slot_of[None, :, :] == jnp.arange(slot_count, dtype=jnp.int32)[:, None, None]
    chooser = jnp.any(matches, axis=2).astype(jnp.bfloat16)
    send_x = jnp.dot(chooser, tokens, preferred_element_type=jnp.float32).astype(jnp.bfloat16)
    send_dy = jnp.dot(chooser, out_grad, preferred_element_type=jnp.float32).astype(jnp.bfloat16)
    gate_wide = gate_values.astype(jnp.float32)[None, :, :]
    send_g = jnp.sum(jnp.where(matches, gate_wide, 0.0), axis=(1, 2))
    send_x = send_x.reshape(n_experts, most_slots, quarter)
    send_dy = send_dy.reshape(n_experts, most_slots, quarter)
    returned, returned_grad = in_steps(send_x, send_dy, send_g, *weights)
    d_tokens = lax.dot_general(
        chooser,
        returned.reshape(slot_count, quarter),
        (((0,), (0,)), ((), ())),
        preferred_element_type=jnp.float32,
    ).astype(jnp.bfloat16)
    grad_wide = returned_grad.reshape(slot_count)[:, None, None]
    d_gates = jnp.sum(jnp.where(matches, grad_wide, 0.0), axis=0)
    return (d_tokens, d_gates)


def solution(mesh):
    placed = (
        P("expert", "tensor"),
        P("expert", "tensor"),
        P("expert", None),
        P("expert", None),
        P("expert", None, "tensor"),
        P("expert", None, "tensor"),
        P("expert", "tensor", None),
    )
    return jax.shard_map(
        local,
        mesh=mesh,
        in_specs=placed,
        out_specs=(P("expert", "tensor"), P("expert", None)),
        check_vma=False,
    )
```

```python
import functools

import jax
import jax.numpy as jnp
from jax import lax
from jax.experimental import pallas as pl
from jax.experimental.pallas import tpu as pltpu
from jax.sharding import PartitionSpec as P


MESH = pl.DeviceIdType.MESH
VMEM = pl.BlockSpec(memory_space=pltpu.VMEM)
VMEM_BYTES = 56 * 1024 * 1024


def positions(n):
    me = lax.axis_index("expert")
    share = lax.axis_index("tensor")
    pair, side = share // 2, share % 2
    return me, share, pair * 2 + 1 - side, (1 - pair) * 2 + side


def greet(n, me, share, near, far):
    barrier = pltpu.get_barrier_semaphore()

    @pl.loop(1, n)
    def _(step):
        pl.semaphore_signal(
            barrier, inc=1, device_id=(lax.rem(me + step, n), share), device_id_type=MESH
        )

    for peer in (near, far):
        pl.semaphore_signal(barrier, inc=1, device_id=(me, peer), device_id_type=MESH)
    pl.semaphore_wait(barrier, n + 1)


def remote(src, dst, sems, index, device):
    return pltpu.make_async_remote_copy(
        src_ref=src,
        dst_ref=dst,
        send_sem=sems[0].at[index],
        recv_sem=sems[1].at[index],
        device_id=device,
        device_id_type=MESH,
    )


def spread_kernel(n, x_ref, dy_ref, g_ref, x_out, dy_out, g_out, *sems):
    me, share, near, far = positions(n)
    quarter = x_ref.shape[2]
    by_group, to_near, to_far, passed, gates = (sems[2 * i : 2 * i + 2] for i in range(5))
    own = sems[10]
    pairs = ((x_ref, x_out), (dy_ref, dy_out))

    def cols(which):
        return pl.ds(pl.multiple_of(which * quarter, 128), quarter)

    def block(which, group, owner):
        return pairs[which][1].at[group, :, cols(owner)]

    def dispatch(which, source, target):
        return remote(
            pairs[which][0].at[target],
            block(which, source, share),
            by_group,
            which * n + source,
            (target, share),
        )

    def gate_copy(source, target):
        return remote(
            g_ref.at[target], g_out.at[source], gates, source, (target, share)
        )

    def along(which, group, sent, sems_of, peer):
        return remote(
            block(which, group, sent),
            block(which, group, sent),
            sems_of,
            which * n + group,
            (me, peer),
        )

    greet(n, me, share, near, far)
    own_copies = [
        pltpu.make_async_copy(src.at[me], block(which, me, share), own.at[which])
        for which, (src, _) in enumerate(pairs)
    ]
    own_copies.append(pltpu.make_async_copy(g_ref.at[me], g_out.at[me], own.at[2]))
    for copy in own_copies:
        copy.start()
    for which in range(2):

        @pl.loop(1, n)
        def _(step):
            target = lax.rem(me + step, n)
            dispatch(which, me, target).start()

    @pl.loop(1, n)
    def _(step):
        gate_copy(me, lax.rem(me + step, n)).start()

    for copy in own_copies:
        copy.wait()

    def share_out(which, group):
        along(which, group, share, to_far, far).start()
        along(which, group, share, to_near, near).start()

    def pass_on(which, group):
        along(which, group, far, to_far, far).wait_recv()
        along(which, group, far, passed, near).start()

    for which in range(2):
        share_out(which, me)

        @pl.loop(1, n)
        def _(step):
            group = lax.rem(me - step + n, n)
            dispatch(which, group, me).wait_recv()
            share_out(which, group)
            pass_on(which, lax.rem(me - step + 1 + n, n))

        pass_on(which, lax.rem(me + 1, n))
    for which in range(2):

        @pl.loop(0, n)
        def _(group):
            along(which, group, near, to_near, near).wait_recv()
            along(which, group, 3 - share, passed, near).wait_recv()
            along(which, group, share, to_far, far).wait_send()
            along(which, group, share, to_near, near).wait_send()
            along(which, group, far, passed, near).wait_send()

        @pl.loop(1, n)
        def _(step):
            dispatch(which, me, lax.rem(me + step, n)).wait_send()

    @pl.loop(1, n)
    def _(step):
        gate_copy(me, lax.rem(me + step, n)).wait_send()
        gate_copy(lax.rem(me - step + n, n), me).wait_recv()


def spread(send_x, send_dy, send_g):
    n, most, quarter = send_x.shape
    wide = jax.ShapeDtypeStruct((n, most, 4 * quarter), send_x.dtype)
    dma = pltpu.SemaphoreType.DMA
    return pl.pallas_call(
        functools.partial(spread_kernel, n),
        out_shape=(wide, wide, jax.ShapeDtypeStruct(send_g.shape, send_g.dtype)),
        in_specs=[VMEM] * 3,
        out_specs=[VMEM] * 3,
        scratch_shapes=[dma((2 * n,))] * 8 + [dma((n,)), dma((n,)), dma((3,))],
        compiler_params=pltpu.CompilerParams(
            collective_id=0, has_side_effects=True, vmem_limit_bytes=VMEM_BYTES
        ),
    )(send_x, send_dy, send_g)


def collect_kernel(n, c_ref, p_ref, out, grad_out, near_got, far_put, far_got, put, total,
                   part_got, part_sum, *sems):
    me, share, near, far = positions(n)
    quarter = out.shape[2]
    to_near, to_far, back, grads, parts = (sems[2 * i : 2 * i + 2] for i in range(5))
    own = sems[10]

    def cols(which):
        return pl.ds(pl.multiple_of(which * quarter, 128), quarter)

    def half(group, slot):
        wanted = near if slot == 1 else 3 - share
        return remote(
            c_ref.at[group, :, cols(wanted)],
            near_got.at[group, slot],
            to_near,
            group * 2 + slot,
            (me, near),
        )

    def across(group):
        return remote(far_put.at[group], far_got.at[group], to_far, group, (me, far))

    def home(source, target):
        return remote(put.at[target], out.at[source], back, source, (target, share))

    def grad_home(source, target):
        return remote(
            part_sum.at[target], grad_out.at[source], grads, source, (target, share)
        )

    greet(n, me, share, near, far)
    part_near = remote(p_ref, part_got.at[0], parts, 0, (me, near))
    part_near.start()

    @pl.loop(0, n)
    def _(step):
        group = lax.rem(me + 1 + step, n)
        half(group, 0).start()
        half(group, 1).start()

    part_near.wait()
    part_sum[...] = p_ref[...] + part_got[0]
    part_far = remote(part_sum, part_got.at[1], parts, 1, (me, far))
    part_far.start()
    part_far.wait()
    part_sum[...] = part_sum[...] + part_got[1]

    @pl.loop(1, n)
    def _(step):
        grad_home(me, lax.rem(me + step, n)).start()

    def pair_sum(group):
        half(group, 0).wait_recv()
        mine = c_ref[group, :, cols(far)].astype(jnp.float32)
        far_put[group] = (mine + near_got[group, 0].astype(jnp.float32)).astype(far_put.dtype)
        across(group).start()
        half(group, 1).wait_recv()
        mine = c_ref[group, :, cols(share)].astype(jnp.float32)
        total[group] = mine + near_got[group, 1].astype(jnp.float32)

    def full_sum(group):
        across(group).wait_recv()
        put[group] = (total[group] + far_got[group].astype(jnp.float32)).astype(put.dtype)

    def send_home(group):
        full_sum(group)
        home(me, group).start()

    pair_sum(lax.rem(me + 1, n))

    @pl.loop(2, n + 1)
    def _(step):
        pair_sum(lax.rem(me + step, n))
        send_home(lax.rem(me + step - 1, n))

    full_sum(me)
    own_copies = [
        pltpu.make_async_copy(put.at[me], out.at[me], own.at[0]),
        pltpu.make_async_copy(part_sum.at[me], grad_out.at[me], own.at[1]),
    ]
    for copy in own_copies:
        copy.start()
    for copy in own_copies:
        copy.wait()

    @pl.loop(0, n)
    def _(group):
        half(group, 0).wait_send()
        half(group, 1).wait_send()
        across(group).wait_send()

    @pl.loop(1, n)
    def _(step):
        target = lax.rem(me + step, n)
        source = lax.rem(me - step + n, n)
        home(me, target).wait_send()
        grad_home(me, target).wait_send()
        home(source, me).wait_recv()
        grad_home(source, me).wait_recv()


def collect(contrib, partial_grad):
    n, most, width = contrib.shape
    quarter = width // 4
    kind = contrib.dtype
    dma = pltpu.SemaphoreType.DMA
    stage = pltpu.VMEM((n, most, quarter), kind)
    return pl.pallas_call(
        functools.partial(collect_kernel, n),
        out_shape=(
            jax.ShapeDtypeStruct((n, most, quarter), kind),
            jax.ShapeDtypeStruct(partial_grad.shape, partial_grad.dtype),
        ),
        in_specs=[VMEM] * 2,
        out_specs=[VMEM] * 2,
        scratch_shapes=[
            pltpu.VMEM((n, 2, most, quarter), kind),
            stage,
            stage,
            stage,
            pltpu.VMEM((n, most, quarter), jnp.float32),
            pltpu.VMEM((2,) + partial_grad.shape, jnp.float32),
            pltpu.VMEM(partial_grad.shape, jnp.float32),
            dma((2 * n,)),
            dma((2 * n,)),
        ]
        + [dma((n,))] * 6
        + [dma((2,)), dma((2,)), dma((2,))],
        compiler_params=pltpu.CompilerParams(
            collective_id=1, has_side_effects=True, vmem_limit_bytes=VMEM_BYTES
        ),
    )(contrib, partial_grad)


BATCHES = ((0, 4), (4, 6), (6, 7), (7, 8))


def fused_kernel(n, most, tok_hbm, grad_hbm, ids_ref, gv_ref, gate_hbm, up_hbm, down_hbm,
                 out, gate_out, tok_ref, grad_ref, send, gath, g_put, g_got, gu_w, down_w, chooser, code, pre_up,
                 dz, dpdu, near_put, mine, near_got, far_put, far_got, put, back, back_far, token_put, token_got, gu_t, down_t,
                 eye, spread_t, last_t, total, part, part_got, part_sum, part_back, load, *sems):
    me, share, near, far = positions(n)
    diag = 3 - share
    quarter = tok_ref.shape[1]
    tok_rows = tok_ref.shape[0]
    hidden = down_w.shape[0]
    chunk = quarter // 7
    (by_group, gates, to_far, to_near, passed, halves, over, back_sems, grads, far_back, parts,
     summed) = (sems[2 * i : 2 * i + 2] for i in range(12))

    inner = lax.rem((me // 2 + 1) // 2, 2)

    def dest(i):
        at = me
        for bit in (1, 2, 4):
            if i & bit:
                at = at + bit * (1 - 2 * lax.rem(me // bit, 2))
        return at

    def place(i):
        return {2: 4 - 2 * inner, 3: 5 - 2 * inner, 4: 2 + 2 * inner, 5: 3 + 2 * inner}.get(i, i)

    def origin(p):
        return {2: 2 + 2 * inner, 3: 3 + 2 * inner, 4: 4 - 2 * inner, 5: 5 - 2 * inner}.get(p, p)

    def source(p):
        if p in (2, 3, 4, 5):
            other = p + 2 if p < 4 else p - 2
            return dest(p) * (1 - inner) + dest(other) * inner
        return dest(p)

    def nt(left, right):
        return lax.dot_general(
            left, right, (((1,), (1,)), ((), ())), preferred_element_type=jnp.float32
        )

    def remote_to(src, dst, sems_of, sent, landed, device):
        return pltpu.make_async_remote_copy(
            src_ref=src,
            dst_ref=dst,
            send_sem=sems_of[0].at[sent],
            recv_sem=sems_of[1].at[landed],
            device_id=(device, share),
            device_id_type=MESH,
        )

    def dispatch(i):
        p = place(i)
        return remote_to(send.at[i], gath.at[p, share], by_group, i, p, dest(i))

    def dispatched(p):
        block = gath.at[p, share]
        return remote_to(block, block, by_group, p, p, source(p))

    def gate_copy(i):
        p = place(i)
        return remote_to(g_put.at[i], g_got.at[p], gates, i, p, dest(i))

    def gate_copied(p):
        return remote_to(g_got.at[p], g_got.at[p], gates, p, p, source(p))

    def along_far(step):
        block = gath.at[step, share]
        return remote(block, block, to_far, step, (me, far))

    def along_near(step):
        block = gath.at[step, share]
        return remote(block, block, to_near, step, (me, near))

    def pass_near(step):
        block = gath.at[step, far]
        return remote(block, block, passed, step, (me, near))

    def half(batch, slot):
        first, last = BATCHES[batch]
        span = pl.ds(first, last - first)
        return remote(
            near_put.at[slot, span], near_got.at[slot, span], halves, batch * 2 + slot, (me, near)
        )

    def across(step):
        return remote(far_put.at[step], far_got.at[step], over, step, (me, far))

    def home(p):
        i = origin(p)
        return remote_to(put.at[p], back.at[i], back_sems, p, i, source(p))

    def far_home(p):
        i = origin(p)
        return remote_to(far_put.at[p], back_far.at[i], far_back, p, i, source(p))

    def far_came_home(i):
        return remote_to(back_far.at[i], back_far.at[i], far_back, i, i, dest(i))

    def token_part(i):
        span = pl.ds(i * tok_rows // 4, tok_rows // 4)
        return remote(token_put.at[span], token_got.at[span], summed, i, (me, far))

    def came_home(i):
        return remote_to(back.at[i], back.at[i], back_sems, i, i, dest(i))

    def grad_home(p):
        i = origin(p)
        return remote_to(part_sum.at[p], part_back.at[i], grads, p, i, source(p))

    def grad_came_home(i):
        return remote_to(part_back.at[i], part_back.at[i], grads, i, i, dest(i))

    def part_copy(batch, which):
        first, last = BATCHES[batch]
        span = pl.ds(first, last - first)
        peer = (near, far, diag)[which]
        return remote(
            part.at[span], part_got.at[which, span], parts, batch * 3 + which, (me, peer)
        )

    loads = [
        pltpu.make_async_copy(gate_hbm, gu_w.at[:, pl.ds(0, hidden)], load.at[0]),
        pltpu.make_async_copy(up_hbm, gu_w.at[:, pl.ds(hidden, hidden)], load.at[1]),
        pltpu.make_async_copy(down_hbm, down_w, load.at[2]),
    ]
    own_rows = [
        pltpu.make_async_copy(tok_hbm, tok_ref, load.at[3]),
        pltpu.make_async_copy(grad_hbm, grad_ref, load.at[4]),
    ]
    barrier = pltpu.get_barrier_semaphore()
    for step in range(1, n):
        pl.semaphore_signal(barrier, inc=1, device_id=(dest(step), share), device_id_type=MESH)
    for peer in (near, far, diag):
        pl.semaphore_signal(barrier, inc=1, device_id=(me, peer), device_id_type=MESH)

    for copy in own_rows + loads:
        copy.start()

    lane = lax.broadcasted_iota(jnp.int32, (tok_rows, 128), 1)
    row = lax.broadcasted_iota(jnp.int32, (tok_rows, 128), 0)
    ids = ids_ref[...]
    gv = gv_ref[...].astype(jnp.float32)
    first_named, second_named = row == ids[0:1, :], row == ids[1:2, :]
    named = jnp.where(first_named | second_named, 1.0, 0.0)
    earlier = jnp.where(row < lane, 1.0, 0.0).astype(jnp.bfloat16)
    rank = jnp.dot(named.astype(jnp.bfloat16), earlier, preferred_element_type=jnp.float32)
    codes = jnp.where(named > 0.5, rank, -1.0)
    code[...] = codes
    weight_t = jnp.where(first_named, gv[0:1, :], 0.0) + jnp.where(second_named, gv[1:2, :], 0.0)
    slot_row = lax.broadcasted_iota(jnp.int32, (most, tok_rows), 0).astype(jnp.float32)

    diagonal = lax.broadcasted_iota(jnp.int32, (most, 128), 0) == lax.broadcasted_iota(
        jnp.int32, (most, 128), 1
    )

    def code_of(i):
        return jnp.sum(jnp.where(row == dest(i), code[...], 0.0), axis=0, keepdims=True)

    def choose(i):
        its_weight = jnp.sum(jnp.where(row == dest(i), weight_t, 0.0), axis=0, keepdims=True)
        hit = jnp.where(slot_row == code_of(i), 1.0, 0.0)
        chooser[i] = hit.astype(chooser.dtype)
        slot_weight = jnp.sum(hit * its_weight, axis=1, keepdims=True)
        flat = jnp.sum(jnp.where(diagonal, slot_weight, 0.0), axis=0, keepdims=True)
        g_put[i] = jnp.broadcast_to(flat, (16, 128)).astype(g_put.dtype)

    def pick(step, which):
        rows_of = (tok_ref, grad_ref)[which]
        return jnp.dot(
            chooser[step], rows_of[...], preferred_element_type=jnp.float32
        ).astype(send.dtype)

    for i in range(n):
        choose(i)
    for copy in own_rows:
        copy.wait()
    for i in range(n):
        for which in range(2):
            if i:
                send[i, which] = pick(i, which)
            else:
                gath[0, share, which] = pick(0, which)
    g_got[0] = g_put[0]
    pl.semaphore_wait(barrier, n + 2)
    along_far(0).start()
    along_near(0).start()
    for i in (4, 1, 5, 2, 3, 6, 7):
        gate_copy(i).start()
        dispatch(i).start()

    def turn_inputs():
        wide_row = lax.broadcasted_iota(jnp.int32, (hidden, hidden), 0)
        wide_lane = lax.broadcasted_iota(jnp.int32, (hidden, hidden), 1)
        eye[...] = jnp.where(wide_row == wide_lane, 1.0, 0.0).astype(eye.dtype)

    def turn(q):
        for step in range(7):
            at = slice(q * quarter + step * chunk, q * quarter + (step + 1) * chunk)
            for part_at in (0, hidden):
                gu_t[part_at : part_at + hidden, at] = nt(
                    eye[...], gu_w[at, part_at : part_at + hidden]
                ).astype(gu_t.dtype)

    def turn_down(q):
        for step in range(7):
            at = slice(q * quarter + step * chunk, q * quarter + (step + 1) * chunk)
            down_t[at, :] = nt(eye[...], down_w[:, at]).astype(down_t.dtype)

    def span_of(batch):
        first, last = BATCHES[batch]
        return slice(first * most, last * most)

    def project(batch, others):
        first, last = BATCHES[batch]
        rows = (last - first) * most
        span = span_of(batch)
        for q in (far, diag) if others else (share, near):
            at = pl.ds(pl.multiple_of(q * quarter, 128), quarter)
            x = gath[first:last, q, 0].reshape(rows, quarter)
            dy = gath[first:last, q, 1].reshape(rows, quarter)
            got = jnp.dot(x, gu_w[at, :], preferred_element_type=jnp.float32)
            got_dz = jnp.dot(dy, down_t[at, :], preferred_element_type=jnp.float32)
            if q is share:
                pre_up[span, :] = got
                dz[span, :] = got_dz
            else:
                pre_up[span, :] += got
                dz[span, :] += got_dz

    def activate(batch):
        first, last = BATCHES[batch]
        for step in range(first, last):
            if step:
                gate_copied(step).wait_recv()
            at = slice(step * most, (step + 1) * most)
            pre_b, up_b, dz_b = pre_up[at, 0:hidden], pre_up[at, hidden:], dz[at, :]
            sigma = jax.nn.sigmoid(pre_b)
            active = pre_b * sigma
            slot_sum = jnp.sum(active * up_b * dz_b, axis=1, keepdims=True)
            flat = jnp.sum(jnp.where(diagonal, slot_sum, 0.0), axis=0, keepdims=True)
            part[step] = jnp.broadcast_to(flat, (8, 128))
            slot_weight = jnp.sum(
                jnp.where(diagonal, g_got[step][0:1, :].astype(jnp.float32), 0.0),
                axis=1,
                keepdims=True,
            )
            scaled = slot_weight * dz_b
            dpdu[at, hidden:] = (scaled * active).astype(dpdu.dtype)
            dpdu[at, 0:hidden] = (
                scaled * up_b * sigma * (1.0 + pre_b * (1.0 - sigma))
            ).astype(dpdu.dtype)
        for which in range(3):
            part_copy(batch, which).start()

    def expand(batch, wanted, store):
        first, last = BATCHES[batch]
        for step in range(7):
            start = wanted * quarter + step * chunk
            at = pl.ds(pl.multiple_of(start, 128), chunk)
            value = jnp.dot(
                dpdu[span_of(batch), :], gu_t[:, at], preferred_element_type=jnp.float32
            )
            store(
                slice(step * chunk, (step + 1) * chunk),
                value.reshape(last - first, most, chunk),
            )

    def give_back(batch, slot):
        first, last = BATCHES[batch]

        def keep(at, value):
            near_put[slot, first:last, :, at] = value.astype(near_put.dtype)

        def keep_wide(at, value):
            mine[slot, first:last, :, at] = value

        expand(batch, (diag, near)[slot], keep)
        half(batch, slot).start()
        expand(batch, (far, share)[slot], keep_wide)

    def crossing_sum(p):
        return (mine[0, p] + near_got[0, p].astype(jnp.float32)).astype(far_put.dtype)

    def staying_sum(p):
        return mine[1, p] + near_got[1, p].astype(jnp.float32)

    def cross(*steps):
        for p in steps:
            far_put[p] = crossing_sum(p)
            across(p).start()

    def go_home(p):
        across(p).wait_recv()
        put[p] = (staying_sum(p) + far_got[p].astype(jnp.float32)).astype(put.dtype)
        home(p).start()

    def both_go_home(*steps):
        for p in steps:
            if p:
                far_put[p] = crossing_sum(p)
                put[p] = staying_sum(p).astype(put.dtype)
                far_home(p).start()
                home(p).start()
            else:
                back_far[0] = crossing_sum(0)
                back[0] = staying_sum(0).astype(back.dtype)

    def sum_tokens():
        for i in range(1, 4):
            far_came_home(i).wait_recv()
        rows = 4 * most
        for step in range(7):
            at = slice(step * chunk, (step + 1) * chunk)
            token_put[:, at] = jnp.dot(
                spread_t[:, 0:rows],
                back_far[:, :, at].reshape(rows, chunk),
                preferred_element_type=jnp.float32,
            ).astype(token_put.dtype)

    def token_go(i):
        token_part(i).start()

    def when(role, act, *steps):
        @pl.when(inner == role)
        def _():
            if not steps:
                act()
            for p in steps:
                act(p)

    def share_parts(batch):
        first, last = BATCHES[batch]
        for which in range(3):
            part_copy(batch, which).wait_recv()
        for step in range(first, last):
            part_sum[step] = (
                part[step] + part_got[0, step] + part_got[1, step] + part_got[2, step]
            )
            if step:
                grad_home(step).start()
            else:
                part_back[0] = part_sum[0]

    def arrive(step):
        dispatched(step).wait_recv()
        along_far(step).start()
        along_near(step).start()

    def pass_on(step):
        along_far_from(step).wait_recv()
        pass_near(step).start()

    def along_far_from(step):
        block = gath.at[step, far]
        return remote(block, block, to_far, step, (me, far))

    def settle_near(*steps):
        for step in steps:
            block = gath.at[step, near]
            remote(block, block, to_near, step, (me, near)).wait_recv()

    def settle_far(*steps):
        for step in steps:
            block = gath.at[step, diag]
            remote(block, block, passed, step, (me, near)).wait_recv()

    turn_inputs()
    for copy in loads:
        copy.wait()
    for q in range(4):
        turn(q)
    arrive(1)
    pass_on(0)
    for q in range(4):
        turn_down(q)
    for i in range(n):
        spread_t[:, i * most : (i + 1) * most] = chooser[i].astype(jnp.float32).T.astype(
            spread_t.dtype
        )
    last_t[...] = chooser[n - 1].astype(jnp.float32).T.astype(last_t.dtype)
    arrive(2)
    pass_on(1)
    arrive(3)
    pass_on(2)
    settle_near(0, 1, 2, 3)
    project(0, False)
    arrive(4)
    pass_on(3)
    settle_far(0, 1, 2, 3)
    project(0, True)
    activate(0)
    arrive(5)
    give_back(0, 0)
    pass_on(4)
    half(0, 0).wait_recv()
    when(1, cross, 2, 3)
    when(0, arrive, 6)
    give_back(0, 1)
    settle_near(4, 5)
    project(1, False)
    half(0, 1).wait_recv()
    both_go_home(0)
    pass_on(5)
    settle_far(4, 5)
    project(1, True)
    activate(1)
    give_back(1, 0)
    when(1, arrive, 6)
    half(1, 0).wait_recv()
    when(0, cross, 4, 5)
    give_back(1, 1)
    settle_near(6)
    project(2, False)
    half(1, 1).wait_recv()
    when(1, both_go_home, 4, 5)
    when(0, arrive, 7)
    when(0, both_go_home, 2, 3, 1)
    when(1, go_home, 2, 3)
    pass_on(6)
    when(1, arrive, 7)
    when(1, both_go_home, 1)
    settle_far(6)
    project(2, True)
    activate(2)
    give_back(2, 0)
    half(2, 0).wait_recv()
    cross(6)
    give_back(2, 1)
    settle_near(7)
    project(3, False)
    when(0, go_home, 4, 5)
    pass_on(7)
    settle_far(7)
    project(3, True)
    activate(3)
    give_back(3, 0)
    half(3, 0).wait_recv()
    cross(7)
    when(1, sum_tokens)
    when(1, token_go, 0, 1, 2, 3)
    share_parts(0)
    share_parts(1)
    share_parts(2)
    half(2, 1).wait_recv()
    go_home(6)
    give_back(3, 1)
    share_parts(3)
    half(3, 1).wait_recv()
    go_home(7)
    when(0, sum_tokens)
    when(0, token_go, 0, 1, 2, 3)
    ids = ids_ref[...]
    grad_total = jnp.zeros((2, tok_rows), jnp.float32)
    for i in range(n):
        if i:
            grad_came_home(i).wait_recv()
        held = part_back[i][0:1, 0:most]
        hit = chooser[i].astype(jnp.float32)
        value = lax.dot_general(
            held,
            hit,
            (((1,), (0,)), ((), ())),
            precision=lax.Precision.HIGHEST,
            preferred_element_type=jnp.float32,
        )
        grad_total = grad_total + jnp.where(ids == dest(i), value, 0.0)
    gate_out[...] = grad_total
    came_home(1).wait_recv()
    came_home(2).wait_recv()
    came_home(3).wait_recv()
    came_home(4).wait_recv()
    came_home(5).wait_recv()
    came_home(6).wait_recv()
    token_part(0).wait_recv()
    token_part(1).wait_recv()
    token_part(2).wait_recv()
    token_part(3).wait_recv()
    early = (n - 1) * most
    for step in range(7):
        at = slice(step * chunk, (step + 1) * chunk)
        total[:, at] = token_got[:, at].astype(jnp.float32) + jnp.dot(
            spread_t[:, 0:early],
            back[0 : n - 1, :, at].reshape(early, chunk),
            preferred_element_type=jnp.float32,
        )
    came_home(7).wait_recv()
    for step in range(7):
        at = slice(step * chunk, (step + 1) * chunk)
        late = jnp.dot(last_t[...], back[n - 1, :, at], preferred_element_type=jnp.float32)
        out[:, at] = (total[:, at] + late).astype(out.dtype)

    def far_sent(p):
        far_home(p).wait_send()

    def across_sent(p):
        across(p).wait_send()

    far_sent(1)
    when(0, far_sent, 2, 3)
    when(1, far_sent, 4, 5)
    when(1, across_sent, 2, 3)
    when(0, across_sent, 4, 5)
    across_sent(6)
    across_sent(7)
    for i in range(4):
        token_part(i).wait_send()
    for step in range(n):
        along_far(step).wait_send()
        along_near(step).wait_send()
        pass_near(step).wait_send()
        if step:
            dispatch(step).wait_send()
            gate_copy(step).wait_send()
            home(step).wait_send()
            grad_home(step).wait_send()
    for batch in range(len(BATCHES)):
        for slot in range(2):
            half(batch, slot).wait_send()
        for which in range(3):
            part_copy(batch, which).wait_send()


def fused(tokens, out_grad, expert_ids, gate_values, gate_mat, up_mat, down_mat):
    n = lax.axis_size("expert")
    tok_rows, quarter = tokens.shape
    flipped = expert_ids.T
    most = 3 * tok_rows * expert_ids.shape[1] // (2 * n)
    kind = tokens.dtype
    hidden = gate_mat.shape[1]
    rows = n * most
    dma = pltpu.SemaphoreType.DMA
    anywhere = pl.BlockSpec(memory_space=pl.ANY)
    stage = pltpu.VMEM((n, most, quarter), kind)
    pair = pltpu.VMEM((2, n, most, quarter), kind)
    flat = pltpu.VMEM((n, 8, 128), jnp.float32)
    narrow = pltpu.VMEM((n, 16, 128), kind)
    d_tokens, d_gates = pl.pallas_call(
        functools.partial(fused_kernel, n, most),
        out_shape=(
            pltpu.VMEM(tokens.shape, kind),
            pltpu.VMEM(flipped.shape, jnp.float32),
        ),
        in_specs=[anywhere] * 2 + [VMEM] * 2 + [anywhere] * 3,
        out_specs=[VMEM] * 2,
        scratch_shapes=[
            pltpu.VMEM(tokens.shape, kind),
            pltpu.VMEM(tokens.shape, kind),
            pltpu.VMEM((n, 2, most, quarter), kind),
            pltpu.VMEM((n, 4, 2, most, quarter), kind),
            narrow,
            narrow,
            pltpu.VMEM((4 * quarter, 2 * hidden), kind),
            pltpu.VMEM(down_mat.shape, kind),
            pltpu.VMEM((n, most, tok_rows), kind),
            pltpu.VMEM((tok_rows, 128), jnp.float32),
            pltpu.VMEM((rows, 2 * hidden), jnp.float32),
            pltpu.VMEM((rows, hidden), jnp.float32),
            pltpu.VMEM((rows, 2 * hidden), kind),
            pair,
            pltpu.VMEM((2, n, most, quarter), jnp.float32),
            pair,
            stage,
            stage,
            stage,
            stage,
            pltpu.VMEM((4, most, quarter), kind),
            pltpu.VMEM(tokens.shape, kind),
            pltpu.VMEM(tokens.shape, kind),
            pltpu.VMEM((2 * hidden, 4 * quarter), kind),
            pltpu.VMEM((4 * quarter, hidden), kind),
            pltpu.VMEM((hidden, hidden), kind),
            pltpu.VMEM((tok_rows, n * most), kind),
            pltpu.VMEM((tok_rows, most), kind),
            pltpu.VMEM(tokens.shape, jnp.float32),
            flat,
            pltpu.VMEM((3, n, 8, 128), jnp.float32),
            flat,
            flat,
            dma((5,)),
        ]
        + [dma((n,))] * 10
        + [dma((2 * len(BATCHES),))] * 2
        + [dma((n,))] * 8
        + [dma((3 * len(BATCHES),))] * 2
        + [dma((4,))] * 2,
        compiler_params=pltpu.CompilerParams(
            collective_id=2, has_side_effects=True, vmem_limit_bytes=VMEM_BYTES
        ),
    )(tokens, out_grad, flipped, gate_values.T, gate_mat, up_mat, down_mat)
    return d_tokens, d_gates.T


def in_steps(send_x, send_dy, send_g, gate_mat, up_mat, down_mat):
    n_experts, most_slots, quarter = send_x.shape
    slot_count = n_experts * most_slots
    piece_x, piece_dy, recv_g = spread(
        send_x,
        send_dy,
        send_g.reshape(n_experts, 1, most_slots),
    )
    piece_x = piece_x.reshape(slot_count, 4 * quarter)
    piece_dy = piece_dy.reshape(slot_count, 4 * quarter)
    pre_sum = jnp.dot(piece_x, gate_mat, preferred_element_type=jnp.float32)
    up_sum = jnp.dot(piece_x, up_mat, preferred_element_type=jnp.float32)
    grad_sum = lax.dot_general(
        piece_dy, down_mat, (((1,), (1,)), ((), ())), preferred_element_type=jnp.float32
    )
    sigma = jax.nn.sigmoid(pre_sum)
    active = pre_sum * sigma
    partial_grad = jnp.sum(active * up_sum * grad_sum, axis=1)
    weight_g = recv_g.reshape(slot_count)
    scaled = weight_g[:, None] * grad_sum
    grad_up = (scaled * active).astype(jnp.bfloat16)
    grad_pre = (scaled * up_sum * sigma * (1.0 + pre_sum * (1.0 - sigma))).astype(jnp.bfloat16)
    contrib = lax.dot_general(
        grad_pre, gate_mat, (((1,), (1,)), ((), ())), preferred_element_type=jnp.float32
    )
    contrib = contrib + lax.dot_general(
        grad_up, up_mat, (((1,), (1,)), ((), ())), preferred_element_type=jnp.float32
    )
    returned, returned_grad = collect(
        contrib.astype(jnp.bfloat16).reshape(n_experts, most_slots, 4 * quarter),
        partial_grad.reshape(n_experts, 1, most_slots),
    )
    return returned, returned_grad


def local(tokens, out_grad, expert_ids, gate_values, w_gate, w_up, w_down):
    n_experts = lax.axis_size("expert")
    shares = lax.axis_size("tensor")
    tok_rows, quarter = tokens.shape
    top_count = expert_ids.shape[1]
    most_slots = 3 * tok_rows * top_count // (2 * n_experts)
    slot_count = n_experts * most_slots
    weights = (w_gate[0], w_up[0], w_down[0])
    fits = most_slots == 48 and tok_rows == 128 and top_count == 2 and quarter == 1792
    if fits and n_experts == 8 and shares == 4 and w_gate.shape[2] == 256:
        return fused(tokens, out_grad, expert_ids, gate_values, *weights)
    flat_ids = expert_ids.reshape(-1)
    onehot = flat_ids[:, None] == jnp.arange(n_experts, dtype=jnp.int32)[None, :]
    earlier = jnp.tri(flat_ids.shape[0], k=-1, dtype=jnp.bfloat16)
    before = jnp.dot(earlier, onehot.astype(jnp.bfloat16), preferred_element_type=jnp.float32)
    rank = jnp.sum(jnp.where(onehot, before, 0.0), axis=1).astype(jnp.int32)
    slot_of = (flat_ids * most_slots + rank).reshape(tok_rows, top_count)
    matches = slot_of[None, :, :] == jnp.arange(slot_count, dtype=jnp.int32)[:, None, None]
    chooser = jnp.any(matches, axis=2).astype(jnp.bfloat16)
    send_x = jnp.dot(chooser, tokens, preferred_element_type=jnp.float32).astype(jnp.bfloat16)
    send_dy = jnp.dot(chooser, out_grad, preferred_element_type=jnp.float32).astype(jnp.bfloat16)
    gate_wide = gate_values.astype(jnp.float32)[None, :, :]
    send_g = jnp.sum(jnp.where(matches, gate_wide, 0.0), axis=(1, 2))
    send_x = send_x.reshape(n_experts, most_slots, quarter)
    send_dy = send_dy.reshape(n_experts, most_slots, quarter)
    returned, returned_grad = in_steps(send_x, send_dy, send_g, *weights)
    d_tokens = lax.dot_general(
        chooser,
        returned.reshape(slot_count, quarter),
        (((0,), (0,)), ((), ())),
        preferred_element_type=jnp.float32,
    ).astype(jnp.bfloat16)
    grad_wide = returned_grad.reshape(slot_count)[:, None, None]
    d_gates = jnp.sum(jnp.where(matches, grad_wide, 0.0), axis=0)
    return (d_tokens, d_gates)


def solution(mesh):
    placed = (
        P("expert", "tensor"),
        P("expert", "tensor"),
        P("expert", None),
        P("expert", None),
        P("expert", None, "tensor"),
        P("expert", None, "tensor"),
        P("expert", "tensor", None),
    )
    return jax.shard_map(
        local,
        mesh=mesh,
        in_specs=placed,
        out_specs=(P("expert", "tensor"), P("expert", None)),
        check_vma=False,
    )
```

```python
import functools

import jax
import jax.numpy as jnp
from jax import lax
from jax.experimental import pallas as pl
from jax.experimental.pallas import tpu as pltpu
from jax.sharding import PartitionSpec as P


MESH = pl.DeviceIdType.MESH
VMEM = pl.BlockSpec(memory_space=pltpu.VMEM)
VMEM_BYTES = 56 * 1024 * 1024


def positions(n):
    me = lax.axis_index("expert")
    share = lax.axis_index("tensor")
    pair, side = share // 2, share % 2
    return me, share, pair * 2 + 1 - side, (1 - pair) * 2 + side


def greet(n, me, share, near, far):
    barrier = pltpu.get_barrier_semaphore()

    @pl.loop(1, n)
    def _(step):
        pl.semaphore_signal(
            barrier, inc=1, device_id=(lax.rem(me + step, n), share), device_id_type=MESH
        )

    for peer in (near, far):
        pl.semaphore_signal(barrier, inc=1, device_id=(me, peer), device_id_type=MESH)
    pl.semaphore_wait(barrier, n + 1)


def remote(src, dst, sems, index, device):
    return pltpu.make_async_remote_copy(
        src_ref=src,
        dst_ref=dst,
        send_sem=sems[0].at[index],
        recv_sem=sems[1].at[index],
        device_id=device,
        device_id_type=MESH,
    )


def spread_kernel(n, x_ref, dy_ref, g_ref, x_out, dy_out, g_out, *sems):
    me, share, near, far = positions(n)
    quarter = x_ref.shape[2]
    by_group, to_near, to_far, passed, gates = (sems[2 * i : 2 * i + 2] for i in range(5))
    own = sems[10]
    pairs = ((x_ref, x_out), (dy_ref, dy_out))

    def cols(which):
        return pl.ds(pl.multiple_of(which * quarter, 128), quarter)

    def block(which, group, owner):
        return pairs[which][1].at[group, :, cols(owner)]

    def dispatch(which, source, target):
        return remote(
            pairs[which][0].at[target],
            block(which, source, share),
            by_group,
            which * n + source,
            (target, share),
        )

    def gate_copy(source, target):
        return remote(
            g_ref.at[target], g_out.at[source], gates, source, (target, share)
        )

    def along(which, group, sent, sems_of, peer):
        return remote(
            block(which, group, sent),
            block(which, group, sent),
            sems_of,
            which * n + group,
            (me, peer),
        )

    greet(n, me, share, near, far)
    own_copies = [
        pltpu.make_async_copy(src.at[me], block(which, me, share), own.at[which])
        for which, (src, _) in enumerate(pairs)
    ]
    own_copies.append(pltpu.make_async_copy(g_ref.at[me], g_out.at[me], own.at[2]))
    for copy in own_copies:
        copy.start()
    for which in range(2):

        @pl.loop(1, n)
        def _(step):
            target = lax.rem(me + step, n)
            dispatch(which, me, target).start()

    @pl.loop(1, n)
    def _(step):
        gate_copy(me, lax.rem(me + step, n)).start()

    for copy in own_copies:
        copy.wait()

    def share_out(which, group):
        along(which, group, share, to_far, far).start()
        along(which, group, share, to_near, near).start()

    def pass_on(which, group):
        along(which, group, far, to_far, far).wait_recv()
        along(which, group, far, passed, near).start()

    for which in range(2):
        share_out(which, me)

        @pl.loop(1, n)
        def _(step):
            group = lax.rem(me - step + n, n)
            dispatch(which, group, me).wait_recv()
            share_out(which, group)
            pass_on(which, lax.rem(me - step + 1 + n, n))

        pass_on(which, lax.rem(me + 1, n))
    for which in range(2):

        @pl.loop(0, n)
        def _(group):
            along(which, group, near, to_near, near).wait_recv()
            along(which, group, 3 - share, passed, near).wait_recv()
            along(which, group, share, to_far, far).wait_send()
            along(which, group, share, to_near, near).wait_send()
            along(which, group, far, passed, near).wait_send()

        @pl.loop(1, n)
        def _(step):
            dispatch(which, me, lax.rem(me + step, n)).wait_send()

    @pl.loop(1, n)
    def _(step):
        gate_copy(me, lax.rem(me + step, n)).wait_send()
        gate_copy(lax.rem(me - step + n, n), me).wait_recv()


def spread(send_x, send_dy, send_g):
    n, most, quarter = send_x.shape
    wide = jax.ShapeDtypeStruct((n, most, 4 * quarter), send_x.dtype)
    dma = pltpu.SemaphoreType.DMA
    return pl.pallas_call(
        functools.partial(spread_kernel, n),
        out_shape=(wide, wide, jax.ShapeDtypeStruct(send_g.shape, send_g.dtype)),
        in_specs=[VMEM] * 3,
        out_specs=[VMEM] * 3,
        scratch_shapes=[dma((2 * n,))] * 8 + [dma((n,)), dma((n,)), dma((3,))],
        compiler_params=pltpu.CompilerParams(
            collective_id=0, has_side_effects=True, vmem_limit_bytes=VMEM_BYTES
        ),
    )(send_x, send_dy, send_g)


def collect_kernel(n, c_ref, p_ref, out, grad_out, near_got, far_put, far_got, put, total,
                   part_got, part_sum, *sems):
    me, share, near, far = positions(n)
    quarter = out.shape[2]
    to_near, to_far, back, grads, parts = (sems[2 * i : 2 * i + 2] for i in range(5))
    own = sems[10]

    def cols(which):
        return pl.ds(pl.multiple_of(which * quarter, 128), quarter)

    def half(group, slot):
        wanted = near if slot == 1 else 3 - share
        return remote(
            c_ref.at[group, :, cols(wanted)],
            near_got.at[group, slot],
            to_near,
            group * 2 + slot,
            (me, near),
        )

    def across(group):
        return remote(far_put.at[group], far_got.at[group], to_far, group, (me, far))

    def home(source, target):
        return remote(put.at[target], out.at[source], back, source, (target, share))

    def grad_home(source, target):
        return remote(
            part_sum.at[target], grad_out.at[source], grads, source, (target, share)
        )

    greet(n, me, share, near, far)
    part_near = remote(p_ref, part_got.at[0], parts, 0, (me, near))
    part_near.start()

    @pl.loop(0, n)
    def _(step):
        group = lax.rem(me + 1 + step, n)
        half(group, 0).start()
        half(group, 1).start()

    part_near.wait()
    part_sum[...] = p_ref[...] + part_got[0]
    part_far = remote(part_sum, part_got.at[1], parts, 1, (me, far))
    part_far.start()
    part_far.wait()
    part_sum[...] = part_sum[...] + part_got[1]

    @pl.loop(1, n)
    def _(step):
        grad_home(me, lax.rem(me + step, n)).start()

    def pair_sum(group):
        half(group, 0).wait_recv()
        mine = c_ref[group, :, cols(far)].astype(jnp.float32)
        far_put[group] = (mine + near_got[group, 0].astype(jnp.float32)).astype(far_put.dtype)
        across(group).start()
        half(group, 1).wait_recv()
        mine = c_ref[group, :, cols(share)].astype(jnp.float32)
        total[group] = mine + near_got[group, 1].astype(jnp.float32)

    def full_sum(group):
        across(group).wait_recv()
        put[group] = (total[group] + far_got[group].astype(jnp.float32)).astype(put.dtype)

    def send_home(group):
        full_sum(group)
        home(me, group).start()

    pair_sum(lax.rem(me + 1, n))

    @pl.loop(2, n + 1)
    def _(step):
        pair_sum(lax.rem(me + step, n))
        send_home(lax.rem(me + step - 1, n))

    full_sum(me)
    own_copies = [
        pltpu.make_async_copy(put.at[me], out.at[me], own.at[0]),
        pltpu.make_async_copy(part_sum.at[me], grad_out.at[me], own.at[1]),
    ]
    for copy in own_copies:
        copy.start()
    for copy in own_copies:
        copy.wait()

    @pl.loop(0, n)
    def _(group):
        half(group, 0).wait_send()
        half(group, 1).wait_send()
        across(group).wait_send()

    @pl.loop(1, n)
    def _(step):
        target = lax.rem(me + step, n)
        source = lax.rem(me - step + n, n)
        home(me, target).wait_send()
        grad_home(me, target).wait_send()
        home(source, me).wait_recv()
        grad_home(source, me).wait_recv()


def collect(contrib, partial_grad):
    n, most, width = contrib.shape
    quarter = width // 4
    kind = contrib.dtype
    dma = pltpu.SemaphoreType.DMA
    stage = pltpu.VMEM((n, most, quarter), kind)
    return pl.pallas_call(
        functools.partial(collect_kernel, n),
        out_shape=(
            jax.ShapeDtypeStruct((n, most, quarter), kind),
            jax.ShapeDtypeStruct(partial_grad.shape, partial_grad.dtype),
        ),
        in_specs=[VMEM] * 2,
        out_specs=[VMEM] * 2,
        scratch_shapes=[
            pltpu.VMEM((n, 2, most, quarter), kind),
            stage,
            stage,
            stage,
            pltpu.VMEM((n, most, quarter), jnp.float32),
            pltpu.VMEM((2,) + partial_grad.shape, jnp.float32),
            pltpu.VMEM(partial_grad.shape, jnp.float32),
            dma((2 * n,)),
            dma((2 * n,)),
        ]
        + [dma((n,))] * 6
        + [dma((2,)), dma((2,)), dma((2,))],
        compiler_params=pltpu.CompilerParams(
            collective_id=1, has_side_effects=True, vmem_limit_bytes=VMEM_BYTES
        ),
    )(contrib, partial_grad)


BATCHES = ((0, 4), (4, 6), (6, 7), (7, 8))


def fused_kernel(n, most, tok_hbm, grad_hbm, ids_ref, gv_ref, gate_hbm, up_hbm, down_hbm,
                 out, gate_out, tok_ref, grad_ref, send, gath, g_put, g_got, gu_w, down_w, chooser, code, pre_up,
                 dz, dpdu, near_put, mine, near_got, far_put, far_got, put, back, back_far, token_put, token_got, gu_t, down_t,
                 eye, spread_t, last_t, total, part, part_got, part_sum, part_back, load, *sems):
    me, share, near, far = positions(n)
    diag = 3 - share
    quarter = tok_ref.shape[1]
    tok_rows = tok_ref.shape[0]
    hidden = down_w.shape[0]
    chunk = quarter // 7
    (by_group, gates, to_far, to_near, passed, halves, over, back_sems, grads, far_back, parts,
     summed) = (sems[2 * i : 2 * i + 2] for i in range(12))

    inner = lax.rem((me // 2 + 1) // 2, 2)

    def dest(i):
        at = me
        for bit in (1, 2, 4):
            if i & bit:
                at = at + bit * (1 - 2 * lax.rem(me // bit, 2))
        return at

    def place(i):
        return {2: 4 - 2 * inner, 3: 5 - 2 * inner, 4: 2 + 2 * inner, 5: 3 + 2 * inner}.get(i, i)

    def origin(p):
        return {2: 2 + 2 * inner, 3: 3 + 2 * inner, 4: 4 - 2 * inner, 5: 5 - 2 * inner}.get(p, p)

    def source(p):
        if p in (2, 3, 4, 5):
            other = p + 2 if p < 4 else p - 2
            return dest(p) * (1 - inner) + dest(other) * inner
        return dest(p)

    def nt(left, right):
        return lax.dot_general(
            left, right, (((1,), (1,)), ((), ())), preferred_element_type=jnp.float32
        )

    def remote_to(src, dst, sems_of, sent, landed, device):
        return pltpu.make_async_remote_copy(
            src_ref=src,
            dst_ref=dst,
            send_sem=sems_of[0].at[sent],
            recv_sem=sems_of[1].at[landed],
            device_id=(device, share),
            device_id_type=MESH,
        )

    def dispatch(i):
        p = place(i)
        return remote_to(send.at[i], gath.at[p, share], by_group, i, p, dest(i))

    def dispatched(p):
        block = gath.at[p, share]
        return remote_to(block, block, by_group, p, p, source(p))

    def gate_copy(i):
        p = place(i)
        return remote_to(g_put.at[i], g_got.at[p], gates, i, p, dest(i))

    def gate_copied(p):
        return remote_to(g_got.at[p], g_got.at[p], gates, p, p, source(p))

    def along_far(step):
        block = gath.at[step, share]
        return remote(block, block, to_far, step, (me, far))

    def along_near(step):
        block = gath.at[step, share]
        return remote(block, block, to_near, step, (me, near))

    def pass_near(step):
        block = gath.at[step, far]
        return remote(block, block, passed, step, (me, near))

    def half(batch, slot):
        first, last = BATCHES[batch]
        span = pl.ds(first, last - first)
        return remote(
            near_put.at[slot, span], near_got.at[slot, span], halves, batch * 2 + slot, (me, near)
        )

    def across(step):
        return remote(far_put.at[step], far_got.at[step], over, step, (me, far))

    def home(p):
        i = origin(p)
        return remote_to(put.at[p], back.at[i], back_sems, p, i, source(p))

    def far_home(p):
        i = origin(p)
        return remote_to(far_put.at[p], back_far.at[i], far_back, p, i, source(p))

    def far_came_home(i):
        return remote_to(back_far.at[i], back_far.at[i], far_back, i, i, dest(i))

    def token_part(i):
        span = pl.ds(i * tok_rows // 4, tok_rows // 4)
        return remote(token_put.at[span], token_got.at[span], summed, i, (me, far))

    def came_home(i):
        return remote_to(back.at[i], back.at[i], back_sems, i, i, dest(i))

    def grad_home(p):
        i = origin(p)
        return remote_to(part_sum.at[p], part_back.at[i], grads, p, i, source(p))

    def grad_came_home(i):
        return remote_to(part_back.at[i], part_back.at[i], grads, i, i, dest(i))

    def part_copy(batch, which):
        first, last = BATCHES[batch]
        span = pl.ds(first, last - first)
        peer = (near, far, diag)[which]
        return remote(
            part.at[span], part_got.at[which, span], parts, batch * 3 + which, (me, peer)
        )

    loads = [
        pltpu.make_async_copy(gate_hbm, gu_w.at[:, pl.ds(0, hidden)], load.at[0]),
        pltpu.make_async_copy(up_hbm, gu_w.at[:, pl.ds(hidden, hidden)], load.at[1]),
        pltpu.make_async_copy(down_hbm, down_w, load.at[2]),
    ]
    own_rows = [
        pltpu.make_async_copy(tok_hbm, tok_ref, load.at[3]),
        pltpu.make_async_copy(grad_hbm, grad_ref, load.at[4]),
    ]
    barrier = pltpu.get_barrier_semaphore()
    for step in range(1, n):
        pl.semaphore_signal(barrier, inc=1, device_id=(dest(step), share), device_id_type=MESH)
    for peer in (near, far, diag):
        pl.semaphore_signal(barrier, inc=1, device_id=(me, peer), device_id_type=MESH)

    for copy in own_rows + loads:
        copy.start()

    lane = lax.broadcasted_iota(jnp.int32, (tok_rows, 128), 1)
    row = lax.broadcasted_iota(jnp.int32, (tok_rows, 128), 0)
    ids = ids_ref[...]
    gv = gv_ref[...].astype(jnp.float32)
    first_named, second_named = row == ids[0:1, :], row == ids[1:2, :]
    named = jnp.where(first_named | second_named, 1.0, 0.0)
    earlier = jnp.where(row < lane, 1.0, 0.0).astype(jnp.bfloat16)
    rank = jnp.dot(named.astype(jnp.bfloat16), earlier, preferred_element_type=jnp.float32)
    codes = jnp.where(named > 0.5, rank, -1.0)
    code[...] = codes
    weight_t = jnp.where(first_named, gv[0:1, :], 0.0) + jnp.where(second_named, gv[1:2, :], 0.0)
    slot_row = lax.broadcasted_iota(jnp.int32, (most, tok_rows), 0).astype(jnp.float32)

    diagonal = lax.broadcasted_iota(jnp.int32, (most, 128), 0) == lax.broadcasted_iota(
        jnp.int32, (most, 128), 1
    )

    def code_of(i):
        return jnp.sum(jnp.where(row == dest(i), code[...], 0.0), axis=0, keepdims=True)

    def choose(i):
        its_weight = jnp.sum(jnp.where(row == dest(i), weight_t, 0.0), axis=0, keepdims=True)
        hit = jnp.where(slot_row == code_of(i), 1.0, 0.0)
        chooser[i] = hit.astype(chooser.dtype)
        slot_weight = jnp.sum(hit * its_weight, axis=1, keepdims=True)
        flat = jnp.sum(jnp.where(diagonal, slot_weight, 0.0), axis=0, keepdims=True)
        g_put[i] = jnp.broadcast_to(flat, (16, 128)).astype(g_put.dtype)

    def pick(step, which):
        rows_of = (tok_ref, grad_ref)[which]
        return jnp.dot(
            chooser[step], rows_of[...], preferred_element_type=jnp.float32
        ).astype(send.dtype)

    for i in range(n):
        choose(i)
    for copy in own_rows:
        copy.wait()
    for i in range(n):
        for which in range(2):
            if i:
                send[i, which] = pick(i, which)
            else:
                gath[0, share, which] = pick(0, which)
    g_got[0] = g_put[0]
    pl.semaphore_wait(barrier, n + 2)
    along_far(0).start()
    along_near(0).start()
    for i in (4, 1, 5, 2, 3, 6, 7):
        gate_copy(i).start()
        dispatch(i).start()

    def turn_inputs():
        wide_row = lax.broadcasted_iota(jnp.int32, (hidden, hidden), 0)
        wide_lane = lax.broadcasted_iota(jnp.int32, (hidden, hidden), 1)
        eye[...] = jnp.where(wide_row == wide_lane, 1.0, 0.0).astype(eye.dtype)

    def turn(q):
        for step in range(7):
            at = slice(q * quarter + step * chunk, q * quarter + (step + 1) * chunk)
            for part_at in (0, hidden):
                gu_t[part_at : part_at + hidden, at] = nt(
                    eye[...], gu_w[at, part_at : part_at + hidden]
                ).astype(gu_t.dtype)

    def turn_down(q):
        for step in range(7):
            at = slice(q * quarter + step * chunk, q * quarter + (step + 1) * chunk)
            down_t[at, :] = nt(eye[...], down_w[:, at]).astype(down_t.dtype)

    def span_of(batch):
        first, last = BATCHES[batch]
        return slice(first * most, last * most)

    def project(batch, others):
        first, last = BATCHES[batch]
        rows = (last - first) * most
        span = span_of(batch)
        for q in (far, diag) if others else (share, near):
            at = pl.ds(pl.multiple_of(q * quarter, 128), quarter)
            x = gath[first:last, q, 0].reshape(rows, quarter)
            dy = gath[first:last, q, 1].reshape(rows, quarter)
            got = jnp.dot(x, gu_w[at, :], preferred_element_type=jnp.float32)
            got_dz = jnp.dot(dy, down_t[at, :], preferred_element_type=jnp.float32)
            if q is share:
                pre_up[span, :] = got
                dz[span, :] = got_dz
            else:
                pre_up[span, :] += got
                dz[span, :] += got_dz

    def activate(batch):
        first, last = BATCHES[batch]
        for step in range(first, last):
            if step:
                gate_copied(step).wait_recv()
            at = slice(step * most, (step + 1) * most)
            pre_b, up_b, dz_b = pre_up[at, 0:hidden], pre_up[at, hidden:], dz[at, :]
            sigma = jax.nn.sigmoid(pre_b)
            active = pre_b * sigma
            slot_sum = jnp.sum(active * up_b * dz_b, axis=1, keepdims=True)
            flat = jnp.sum(jnp.where(diagonal, slot_sum, 0.0), axis=0, keepdims=True)
            part[step] = jnp.broadcast_to(flat, (8, 128))
            slot_weight = jnp.sum(
                jnp.where(diagonal, g_got[step][0:1, :].astype(jnp.float32), 0.0),
                axis=1,
                keepdims=True,
            )
            scaled = slot_weight * dz_b
            dpdu[at, hidden:] = (scaled * active).astype(dpdu.dtype)
            dpdu[at, 0:hidden] = (
                scaled * up_b * sigma * (1.0 + pre_b * (1.0 - sigma))
            ).astype(dpdu.dtype)
        for which in range(3):
            part_copy(batch, which).start()

    def expand(batch, wanted, store):
        first, last = BATCHES[batch]
        for step in range(7):
            start = wanted * quarter + step * chunk
            at = pl.ds(pl.multiple_of(start, 128), chunk)
            value = jnp.dot(
                dpdu[span_of(batch), :], gu_t[:, at], preferred_element_type=jnp.float32
            )
            store(
                slice(step * chunk, (step + 1) * chunk),
                value.reshape(last - first, most, chunk),
            )

    def give_back(batch, slot):
        first, last = BATCHES[batch]

        def keep(at, value):
            near_put[slot, first:last, :, at] = value.astype(near_put.dtype)

        def keep_wide(at, value):
            mine[slot, first:last, :, at] = value

        expand(batch, (diag, near)[slot], keep)
        half(batch, slot).start()
        expand(batch, (far, share)[slot], keep_wide)

    def crossing_sum(p):
        return (mine[0, p] + near_got[0, p].astype(jnp.float32)).astype(far_put.dtype)

    def staying_sum(p):
        return mine[1, p] + near_got[1, p].astype(jnp.float32)

    def cross(*steps):
        for p in steps:
            far_put[p] = crossing_sum(p)
            across(p).start()

    def go_home(p):
        across(p).wait_recv()
        put[p] = (staying_sum(p) + far_got[p].astype(jnp.float32)).astype(put.dtype)
        home(p).start()

    def both_go_home(*steps):
        for p in steps:
            if p:
                far_put[p] = crossing_sum(p)
                put[p] = staying_sum(p).astype(put.dtype)
                far_home(p).start()
                home(p).start()
            else:
                back_far[0] = crossing_sum(0)
                back[0] = staying_sum(0).astype(back.dtype)

    def sum_tokens():
        for i in range(1, 4):
            far_came_home(i).wait_recv()
        rows = 4 * most
        for step in range(7):
            at = slice(step * chunk, (step + 1) * chunk)
            token_put[:, at] = jnp.dot(
                spread_t[:, 0:rows],
                back_far[:, :, at].reshape(rows, chunk),
                preferred_element_type=jnp.float32,
            ).astype(token_put.dtype)

    def token_go(i):
        token_part(i).start()

    def when(role, act, *steps):
        @pl.when(inner == role)
        def _():
            if not steps:
                act()
            for p in steps:
                act(p)

    def share_parts(batch):
        first, last = BATCHES[batch]
        for which in range(3):
            part_copy(batch, which).wait_recv()
        for step in range(first, last):
            part_sum[step] = (
                part[step] + part_got[0, step] + part_got[1, step] + part_got[2, step]
            )
            if step:
                grad_home(step).start()
            else:
                part_back[0] = part_sum[0]

    def arrive(step):
        dispatched(step).wait_recv()
        along_far(step).start()
        along_near(step).start()

    def pass_on(step):
        along_far_from(step).wait_recv()
        pass_near(step).start()

    def along_far_from(step):
        block = gath.at[step, far]
        return remote(block, block, to_far, step, (me, far))

    def settle_near(*steps):
        for step in steps:
            block = gath.at[step, near]
            remote(block, block, to_near, step, (me, near)).wait_recv()

    def settle_far(*steps):
        for step in steps:
            block = gath.at[step, diag]
            remote(block, block, passed, step, (me, near)).wait_recv()

    turn_inputs()
    for copy in loads:
        copy.wait()
    for q in range(4):
        turn(q)
    arrive(1)
    pass_on(0)
    for q in range(4):
        turn_down(q)
    for i in range(n):
        spread_t[:, i * most : (i + 1) * most] = chooser[i].astype(jnp.float32).T.astype(
            spread_t.dtype
        )
    last_t[...] = chooser[n - 1].astype(jnp.float32).T.astype(last_t.dtype)
    arrive(2)
    pass_on(1)
    arrive(3)
    pass_on(2)
    settle_near(0, 1, 2, 3)
    project(0, False)
    arrive(4)
    pass_on(3)
    settle_far(0, 1, 2, 3)
    project(0, True)
    activate(0)
    arrive(5)
    give_back(0, 0)
    pass_on(4)
    half(0, 0).wait_recv()
    when(1, cross, 2, 3)
    when(0, arrive, 6)
    give_back(0, 1)
    settle_near(4, 5)
    project(1, False)
    half(0, 1).wait_recv()
    both_go_home(0)
    pass_on(5)
    settle_far(4, 5)
    project(1, True)
    activate(1)
    give_back(1, 0)
    when(1, arrive, 6)
    half(1, 0).wait_recv()
    when(0, cross, 4, 5)
    give_back(1, 1)
    settle_near(6)
    project(2, False)
    half(1, 1).wait_recv()
    when(1, both_go_home, 4, 5)
    when(0, arrive, 7)
    when(0, both_go_home, 2, 3, 1)
    when(1, go_home, 2, 3)
    pass_on(6)
    when(1, arrive, 7)
    when(1, both_go_home, 1)
    settle_far(6)
    project(2, True)
    activate(2)
    give_back(2, 0)
    half(2, 0).wait_recv()
    cross(6)
    give_back(2, 1)
    settle_near(7)
    project(3, False)
    when(0, go_home, 4, 5)
    pass_on(7)
    settle_far(7)
    project(3, True)
    activate(3)
    give_back(3, 0)
    half(3, 0).wait_recv()
    cross(7)
    half(2, 1).wait_recv()
    go_home(6)
    when(1, sum_tokens)
    when(1, token_go, 0, 1, 2, 3)
    share_parts(0)
    share_parts(1)
    share_parts(2)
    give_back(3, 1)
    share_parts(3)
    half(3, 1).wait_recv()
    go_home(7)
    when(0, sum_tokens)
    when(0, token_go, 0, 1, 2, 3)
    ids = ids_ref[...]
    grad_total = jnp.zeros((2, tok_rows), jnp.float32)
    for i in range(n):
        if i:
            grad_came_home(i).wait_recv()
        held = part_back[i][0:1, 0:most]
        hit = chooser[i].astype(jnp.float32)
        value = lax.dot_general(
            held,
            hit,
            (((1,), (0,)), ((), ())),
            precision=lax.Precision.HIGHEST,
            preferred_element_type=jnp.float32,
        )
        grad_total = grad_total + jnp.where(ids == dest(i), value, 0.0)
    gate_out[...] = grad_total
    came_home(1).wait_recv()
    came_home(2).wait_recv()
    came_home(3).wait_recv()
    came_home(4).wait_recv()
    came_home(5).wait_recv()
    came_home(6).wait_recv()
    token_part(0).wait_recv()
    token_part(1).wait_recv()
    token_part(2).wait_recv()
    token_part(3).wait_recv()
    early = (n - 1) * most
    for step in range(7):
        at = slice(step * chunk, (step + 1) * chunk)
        total[:, at] = token_got[:, at].astype(jnp.float32) + jnp.dot(
            spread_t[:, 0:early],
            back[0 : n - 1, :, at].reshape(early, chunk),
            preferred_element_type=jnp.float32,
        )
    came_home(7).wait_recv()
    for step in range(7):
        at = slice(step * chunk, (step + 1) * chunk)
        late = jnp.dot(last_t[...], back[n - 1, :, at], preferred_element_type=jnp.float32)
        out[:, at] = (total[:, at] + late).astype(out.dtype)

    def far_sent(p):
        far_home(p).wait_send()

    def across_sent(p):
        across(p).wait_send()

    far_sent(1)
    when(0, far_sent, 2, 3)
    when(1, far_sent, 4, 5)
    when(1, across_sent, 2, 3)
    when(0, across_sent, 4, 5)
    across_sent(6)
    across_sent(7)
    for i in range(4):
        token_part(i).wait_send()
    for step in range(n):
        along_far(step).wait_send()
        along_near(step).wait_send()
        pass_near(step).wait_send()
        if step:
            dispatch(step).wait_send()
            gate_copy(step).wait_send()
            home(step).wait_send()
            grad_home(step).wait_send()
    for batch in range(len(BATCHES)):
        for slot in range(2):
            half(batch, slot).wait_send()
        for which in range(3):
            part_copy(batch, which).wait_send()


def fused(tokens, out_grad, expert_ids, gate_values, gate_mat, up_mat, down_mat):
    n = lax.axis_size("expert")
    tok_rows, quarter = tokens.shape
    flipped = expert_ids.T
    most = 3 * tok_rows * expert_ids.shape[1] // (2 * n)
    kind = tokens.dtype
    hidden = gate_mat.shape[1]
    rows = n * most
    dma = pltpu.SemaphoreType.DMA
    anywhere = pl.BlockSpec(memory_space=pl.ANY)
    stage = pltpu.VMEM((n, most, quarter), kind)
    pair = pltpu.VMEM((2, n, most, quarter), kind)
    flat = pltpu.VMEM((n, 8, 128), jnp.float32)
    narrow = pltpu.VMEM((n, 16, 128), kind)
    d_tokens, d_gates = pl.pallas_call(
        functools.partial(fused_kernel, n, most),
        out_shape=(
            pltpu.VMEM(tokens.shape, kind),
            pltpu.VMEM(flipped.shape, jnp.float32),
        ),
        in_specs=[anywhere] * 2 + [VMEM] * 2 + [anywhere] * 3,
        out_specs=[VMEM] * 2,
        scratch_shapes=[
            pltpu.VMEM(tokens.shape, kind),
            pltpu.VMEM(tokens.shape, kind),
            pltpu.VMEM((n, 2, most, quarter), kind),
            pltpu.VMEM((n, 4, 2, most, quarter), kind),
            narrow,
            narrow,
            pltpu.VMEM((4 * quarter, 2 * hidden), kind),
            pltpu.VMEM(down_mat.shape, kind),
            pltpu.VMEM((n, most, tok_rows), kind),
            pltpu.VMEM((tok_rows, 128), jnp.float32),
            pltpu.VMEM((rows, 2 * hidden), jnp.float32),
            pltpu.VMEM((rows, hidden), jnp.float32),
            pltpu.VMEM((rows, 2 * hidden), kind),
            pair,
            pltpu.VMEM((2, n, most, quarter), jnp.float32),
            pair,
            stage,
            stage,
            stage,
            stage,
            pltpu.VMEM((4, most, quarter), kind),
            pltpu.VMEM(tokens.shape, kind),
            pltpu.VMEM(tokens.shape, kind),
            pltpu.VMEM((2 * hidden, 4 * quarter), kind),
            pltpu.VMEM((4 * quarter, hidden), kind),
            pltpu.VMEM((hidden, hidden), kind),
            pltpu.VMEM((tok_rows, n * most), kind),
            pltpu.VMEM((tok_rows, most), kind),
            pltpu.VMEM(tokens.shape, jnp.float32),
            flat,
            pltpu.VMEM((3, n, 8, 128), jnp.float32),
            flat,
            flat,
            dma((5,)),
        ]
        + [dma((n,))] * 10
        + [dma((2 * len(BATCHES),))] * 2
        + [dma((n,))] * 8
        + [dma((3 * len(BATCHES),))] * 2
        + [dma((4,))] * 2,
        compiler_params=pltpu.CompilerParams(
            collective_id=2, has_side_effects=True, vmem_limit_bytes=VMEM_BYTES
        ),
    )(tokens, out_grad, flipped, gate_values.T, gate_mat, up_mat, down_mat)
    return d_tokens, d_gates.T


def in_steps(send_x, send_dy, send_g, gate_mat, up_mat, down_mat):
    n_experts, most_slots, quarter = send_x.shape
    slot_count = n_experts * most_slots
    piece_x, piece_dy, recv_g = spread(
        send_x,
        send_dy,
        send_g.reshape(n_experts, 1, most_slots),
    )
    piece_x = piece_x.reshape(slot_count, 4 * quarter)
    piece_dy = piece_dy.reshape(slot_count, 4 * quarter)
    pre_sum = jnp.dot(piece_x, gate_mat, preferred_element_type=jnp.float32)
    up_sum = jnp.dot(piece_x, up_mat, preferred_element_type=jnp.float32)
    grad_sum = lax.dot_general(
        piece_dy, down_mat, (((1,), (1,)), ((), ())), preferred_element_type=jnp.float32
    )
    sigma = jax.nn.sigmoid(pre_sum)
    active = pre_sum * sigma
    partial_grad = jnp.sum(active * up_sum * grad_sum, axis=1)
    weight_g = recv_g.reshape(slot_count)
    scaled = weight_g[:, None] * grad_sum
    grad_up = (scaled * active).astype(jnp.bfloat16)
    grad_pre = (scaled * up_sum * sigma * (1.0 + pre_sum * (1.0 - sigma))).astype(jnp.bfloat16)
    contrib = lax.dot_general(
        grad_pre, gate_mat, (((1,), (1,)), ((), ())), preferred_element_type=jnp.float32
    )
    contrib = contrib + lax.dot_general(
        grad_up, up_mat, (((1,), (1,)), ((), ())), preferred_element_type=jnp.float32
    )
    returned, returned_grad = collect(
        contrib.astype(jnp.bfloat16).reshape(n_experts, most_slots, 4 * quarter),
        partial_grad.reshape(n_experts, 1, most_slots),
    )
    return returned, returned_grad


def local(tokens, out_grad, expert_ids, gate_values, w_gate, w_up, w_down):
    n_experts = lax.axis_size("expert")
    shares = lax.axis_size("tensor")
    tok_rows, quarter = tokens.shape
    top_count = expert_ids.shape[1]
    most_slots = 3 * tok_rows * top_count // (2 * n_experts)
    slot_count = n_experts * most_slots
    weights = (w_gate[0], w_up[0], w_down[0])
    fits = most_slots == 48 and tok_rows == 128 and top_count == 2 and quarter == 1792
    if fits and n_experts == 8 and shares == 4 and w_gate.shape[2] == 256:
        return fused(tokens, out_grad, expert_ids, gate_values, *weights)
    flat_ids = expert_ids.reshape(-1)
    onehot = flat_ids[:, None] == jnp.arange(n_experts, dtype=jnp.int32)[None, :]
    earlier = jnp.tri(flat_ids.shape[0], k=-1, dtype=jnp.bfloat16)
    before = jnp.dot(earlier, onehot.astype(jnp.bfloat16), preferred_element_type=jnp.float32)
    rank = jnp.sum(jnp.where(onehot, before, 0.0), axis=1).astype(jnp.int32)
    slot_of = (flat_ids * most_slots + rank).reshape(tok_rows, top_count)
    matches = slot_of[None, :, :] == jnp.arange(slot_count, dtype=jnp.int32)[:, None, None]
    chooser = jnp.any(matches, axis=2).astype(jnp.bfloat16)
    send_x = jnp.dot(chooser, tokens, preferred_element_type=jnp.float32).astype(jnp.bfloat16)
    send_dy = jnp.dot(chooser, out_grad, preferred_element_type=jnp.float32).astype(jnp.bfloat16)
    gate_wide = gate_values.astype(jnp.float32)[None, :, :]
    send_g = jnp.sum(jnp.where(matches, gate_wide, 0.0), axis=(1, 2))
    send_x = send_x.reshape(n_experts, most_slots, quarter)
    send_dy = send_dy.reshape(n_experts, most_slots, quarter)
    returned, returned_grad = in_steps(send_x, send_dy, send_g, *weights)
    d_tokens = lax.dot_general(
        chooser,
        returned.reshape(slot_count, quarter),
        (((0,), (0,)), ((), ())),
        preferred_element_type=jnp.float32,
    ).astype(jnp.bfloat16)
    grad_wide = returned_grad.reshape(slot_count)[:, None, None]
    d_gates = jnp.sum(jnp.where(matches, grad_wide, 0.0), axis=0)
    return (d_tokens, d_gates)


def solution(mesh):
    placed = (
        P("expert", "tensor"),
        P("expert", "tensor"),
        P("expert", None),
        P("expert", None),
        P("expert", None, "tensor"),
        P("expert", None, "tensor"),
        P("expert", "tensor", None),
    )
    return jax.shard_map(
        local,
        mesh=mesh,
        in_specs=placed,
        out_specs=(P("expert", "tensor"), P("expert", None)),
        check_vma=False,
    )
```
